256 devices in a mesh: gx: 8 (over z), gy: 4 (over x_hi, core), gz: 8 (over x_lo, y).
Axes of the slice: x: 4 (x_hi: 2, x_lo: 2; x = x_hi * 2 + x_lo), y: 4, z: 8, core: 2. Of those that a mesh axis runs over, the one named last changes fastest.
Arguments:
- velocity: float32 [3, 128, 32, 1024], P(None, 'gx', 'gy', 'gz'), may hold values from -6 to 6
- acoustic: float32 [8192, 4, 512], P(('gx', 'gy', 'gz')), may hold values from -6 to 6
- projection: float32 [64, 512], replicated, may hold values from -0.75 to 0.75
- owner_index: int32 [8192, 1], P(('gx', 'gy', 'gz')), may hold values from 0 to 31; in each aligned block of 32 rows (0 to 31, 32 to 63, ...) at most 2 rows name the same one
- slot_element: int32 [256, 64], P(('gx', 'gy', 'gz')), may hold values from 0 to 31
- element_cell: int32 [256, 32], P(('gx', 'gy', 'gz')), may hold values from 0 to 31, each once within a row
Outputs:
- velocity_out: float32 [3, 128, 32, 1024], P(None, 'gx', 'gy', 'gz')
- acoustic_out: float32 [8192, 4, 512], P(('gx', 'gy', 'gz'))
The draws below stay inside these ranges and needn't reach their ends.
Inputs may be any that keep to these rules, and one draw needn't show every extreme that they name: `owner_index`: owners are numbered gy index times 8 plus gz index within the sender's gx plane; among one device's 32 rows no owner appears more than 2 times. Slot q of a device feeds its stored element slot_element[q]. `element_cell`: each row is a permutation of the brick cells of one device.
All inputs are finite; a program needn't handle non-finite values.
Results may differ from the reference program's by a relative error of at most 0.0019.
Values may be sent and summed in bfloat16 or wider, within the bound.
No kernel may reach another device: no remote copies, remote signals or barrier semaphores. Data moves between devices by JAX's collectives and lax.ppermute only.
A program may use at most 128 MiB of HBM per device.

```python
import math
import jax
import jax.numpy as jnp
import numpy as np
from jax import lax

CX = 16
CY = 8
CZ = 128
VS = 4
ORDER = 7
EBX = 1
EBY = 2
EBZ = 16
NODES = 512
VOL = 64
NV = 32
ELEM = 32
PEERS = 32
CAP = 2
SLOTS = 64
NX = 128
NY = 32
NZ = 1024
ELEMENTS = 8192
N_GX = 8
N_GY = 4
N_GZ = 8
DEVICES = 256


def with_ends(result, rng, least, largest):
    longest = result.shape.index(max(result.shape))
    spots = []
    for shift in (0, 1):
        where = [jax.random.randint(jax.random.fold_in(rng, axis), (), 0, length) for axis, length in enumerate(result.shape)]
        where[longest] = (where[longest] + shift) % result.shape[longest]
        spots.append(tuple(where))
    return result.at[spots[0]].set(least).at[spots[1]].set(largest)


def block_scale(rng, shape, cuts, least, high):
    def one(axis_at, blocks):
        draws = jax.random.uniform(jax.random.fold_in(jax.random.fold_in(rng, 6), axis_at), (blocks,), jnp.float32, least / len(cuts), high / len(cuts))
        return jnp.repeat(jnp.exp(draws), shape[axis_at] // blocks).reshape((-1,) + (1,) * (len(shape) - axis_at - 1))

    gain = one(*cuts[0])
    for cut in cuts[1:]:
        gain = gain * one(*cut)
    return gain


def assign_block(rng, own, number, rows, amount, top, most, skew):
    sequence = jax.random.permutation(rng, amount)
    packed, ordinary = portions_of(amount, rows * top, most, skew, True), portions_of(amount, rows * top, most, skew, False)
    places = jnp.arange(amount)

    def named(sizes, rotation):
        used = int((sizes > 0).sum())
        fixed = max(1, used // 4)
        moved = fixed + (places - fixed + rotation * (used - fixed)) % max(1, amount - fixed)
        return jnp.zeros((amount,), jnp.int32).at[sequence[jnp.where(places < fixed, places, moved)]].set(jnp.asarray(sizes, jnp.int32))

    sizes = jnp.where(number % 4 == 0, named(packed, number // 4), named(ordinary, number - number // 4 - 1))
    mixed = jax.random.permutation(jax.random.fold_in(own, 3), amount)
    giver, sink = mixed[0:amount // 2 * 2:2], mixed[1:amount // 2 * 2:2]
    slack = jnp.minimum(sizes[giver] - 1, most - sizes[sink]) // 2
    slack = jnp.where((giver == sequence[0]) | (sink == sequence[0]) | (sizes[sink] == 0), 0, jnp.maximum(slack, 0))
    moved = jax.random.randint(jax.random.fold_in(own, 4), (amount // 2,), 0, 1 << 20) % (slack + 1)
    sizes = sizes.at[giver].add(-moved).at[sink].add(moved)
    members = jnp.searchsorted(jnp.cumsum(sizes), jnp.arange(rows * top), side="right").astype(jnp.int32)
    listing = members.reshape(top, rows).T
    listing = listing[jax.random.permutation(jax.random.fold_in(own, 1), rows)]
    rotation = jax.random.randint(jax.random.fold_in(own, 2), (rows, 1), 0, top)
    return jnp.take_along_axis(listing, (jnp.arange(top)[None, :] + rotation) % top, axis=1)


def portions_of(count, total, limit, slope, full):
    portions = [(1 << 20) // math.isqrt(rank ** slope) + 1 for rank in range(1, count + 1)]
    largest = limit if full else min(limit, max(-(-total // count), total * portions[0] // sum(portions)))
    least = 1 if total - largest >= count - 1 else 0
    given, surplus = [largest] + [least] * (count - 1), total - largest - least * (count - 1)
    while surplus > 0:
        movable = [i for i in range(1, count) if given[i] < largest] or [i for i in range(1, count) if given[i] < limit]
        pool, budget = sum([portions[i] for i in movable]), surplus
        for i in movable:
            more = min(limit - given[i], max(1, budget * portions[i] // pool), surplus)
            given[i] = given[i] + more
            surplus = surplus - more
    return np.array(given)


def noise(rng, dims, scale, most, cuts=(), held_as=jnp.bfloat16):
    level = block_scale(rng, dims, cuts, -0.22, 0.18) if cuts else 1.0
    array = jax.random.normal(rng, dims, jnp.float32) * scale * level
    return jnp.minimum(jnp.maximum(array, -most), most).astype(held_as)


def setup_inputs(seed: int = 0) -> dict:
    seeds = jax.random.split(jax.random.key(seed), 7)
    velocity = noise(seeds[0], (3, NX, NY, NZ), 1.0, 6.0, ((1, 8), (2, 4), (3, 8)), jnp.float32)
    acoustic = noise(seeds[1], (ELEMENTS, 4, NODES), 1.0, 6.0, ((0, 256),), jnp.float32)
    projection = noise(seeds[2], (VOL, NODES), VOL ** -0.5, 0.75, (), jnp.float32)
    owner_index_keys = jax.random.split(jax.random.fold_in(seeds[3], 1), (DEVICES * NV) // NV)
    owner_index_turns = jax.random.permutation(jax.random.fold_in(seeds[3], 3), (DEVICES * NV) // NV)
    owner_index = jax.vmap(lambda own, number: assign_block(jax.random.fold_in(seeds[3], 2), own, number, NV, N_GY * N_GZ, 1, CAP, 2))(owner_index_keys, owner_index_turns).reshape((DEVICES * NV, 1))
    slot_element = with_ends(jax.random.randint(seeds[4], (DEVICES, N_GY * N_GZ * CAP), 0, ELEM), jax.random.fold_in(seeds[4], 1), 0, ELEM - 1).astype(jnp.int32)
    element_cell = jax.vmap(lambda own: jax.random.permutation(own, ELEM))(jax.random.split(seeds[5], DEVICES)).reshape((DEVICES, ELEM)).astype(jnp.int32)
    return {"velocity": velocity, "acoustic": acoustic, "projection": projection, "owner_index": owner_index, "slot_element": slot_element, "element_cell": element_cell}


HIGHEST = lax.Precision.HIGHEST
FLOW_STEP = 0.1
VISCOSITY = 0.05
WAVE_STEP = 0.02
SOURCE_GAIN = 25.0


def legendre_table(points, order):
    columns = [points * 0.0 + 1.0, points]
    for degree in range(2, order + 1):
        columns.append(((2 * degree - 1) * points * columns[degree - 1] - (degree - 1) * columns[degree - 2]) / degree)
    return np.stack(columns, axis=1)


def lobatto_tables(order):
    point_count = order + 1
    points = -np.cos(np.pi * np.arange(point_count) / order)
    for newton_step in range(60):
        legendre = legendre_table(points, order)
        points = points - (points * legendre[:, order] - legendre[:, order - 1]) / (point_count * legendre[:, order])
    legendre = legendre_table(points, order)
    highest = legendre[:, order]
    spacing = points[:, None] - points[None, :] + np.eye(point_count)
    derivative = highest[:, None] / (highest[None, :] * spacing)
    derivative = derivative * (1.0 - np.eye(point_count))
    derivative[0, 0] = -order * point_count / 4.0
    derivative[order, order] = order * point_count / 4.0
    return derivative


def wave_tables(order):
    width = order + 1
    derivative = lobatto_tables(order)
    unit = np.eye(width)
    along_x = np.kron(np.kron(derivative, unit), unit)
    along_y = np.kron(np.kron(unit, derivative), unit)
    along_z = np.kron(np.kron(unit, unit), derivative)
    gradient_table = np.concatenate([along_x.T, along_y.T, along_z.T], axis=1)
    divergence_table = np.concatenate([along_x.T, along_y.T, along_z.T], axis=0)
    selector = np.zeros((width ** 3, 6 * width * width))
    for face_id in range(6):
        along = face_id // 2
        level = (width - 1) * (face_id % 2)
        for first in range(width):
            for second in range(width):
                index_list = [first, second]
                index_list.insert(along, level)
                node_id = (index_list[0] * width + index_list[1]) * width + index_list[2]
                selector[node_id, face_id * width * width + first * width + second] = 1.0
    lift_scale = order * (order + 1) / 2.0
    return (jnp.asarray(gradient_table, jnp.float32), jnp.asarray(divergence_table, jnp.float32), jnp.asarray(selector, jnp.float32), lift_scale)


def shifted(padded, along):
    lower_index = [slice(None), slice(1, -1), slice(1, -1), slice(1, -1)]
    upper_index = list(lower_index)
    lower_index[along + 1] = slice(0, -2)
    upper_index[along + 1] = slice(2, None)
    return padded[tuple(lower_index)], padded[tuple(upper_index)]


def advance(padded):
    centre = padded[:, 1:-1, 1:-1, 1:-1]
    rates = jnp.zeros_like(centre)
    slopes = []
    for along in range(3):
        lower_cells, upper_cells = shifted(padded, along)
        gradient_part = 0.5 * (upper_cells - lower_cells)
        slopes.append(gradient_part)
        rates = rates - centre[along] * gradient_part + VISCOSITY * (upper_cells + lower_cells - 2.0 * centre)
    updated = centre + FLOW_STEP * rates
    swirl = jnp.stack([slopes[1][2] - slopes[2][1], slopes[2][0] - slopes[0][2], slopes[0][1] - slopes[1][0]])
    lamb_vector = jnp.stack([swirl[1] * centre[2] - swirl[2] * centre[1], swirl[2] * centre[0] - swirl[0] * centre[2], swirl[0] * centre[1] - swirl[1] * centre[0]])
    return updated, lamb_vector


def face_terms(jumps, lift_scale):
    pieces = []
    for face_id in range(6):
        along = face_id // 2
        normal = 1.0 if face_id % 2 else -1.0
        face_jump = jumps[..., face_id, :]
        pressure_jump = face_jump[..., 0, :]
        normal_jump = face_jump[..., 1 + along, :]
        flux_rows = []
        for variable in range(4):
            if variable == 0:
                flux_rows.append(normal * normal_jump)
            elif variable == 1 + along:
                flux_rows.append(normal * pressure_jump)
            else:
                flux_rows.append(jnp.zeros_like(pressure_jump))
        face_flux = jnp.stack(flux_rows, axis=-2)
        pieces.append(0.5 * lift_scale * (face_flux - face_jump))
    return jnp.stack(pieces, axis=-2)


def outer_traces(padded):
    extent = [padded.shape[0] - 2, padded.shape[1] - 2, padded.shape[2] - 2]
    pieces = []
    for face_id in range(6):
        along = face_id // 2
        offset = [1, 1, 1]
        offset[along] = 2 if face_id % 2 else 0
        neighbour_block = padded[offset[0]:offset[0] + extent[0], offset[1]:offset[1] + extent[1], offset[2]:offset[2] + extent[2]]
        pieces.append(neighbour_block[..., face_id ^ 1, :])
    return jnp.stack(pieces, axis=-2)


def face_values(wave_state, selector):
    elements, variables, points = wave_state.shape
    return jnp.dot(wave_state.reshape(elements * variables, points), selector, precision=HIGHEST).reshape(elements, variables, 6, -1)


def wave_update(wave_state, inner_trace, outer_trace, source, tables):
    gradient_table, divergence_table, selector, lift_scale = tables
    elements, variables, points = wave_state.shape
    gradient = jnp.dot(wave_state[:, 0], gradient_table, precision=HIGHEST).reshape(elements, 3, points)
    divergence = jnp.dot(wave_state[:, 1:].reshape(elements, 3 * points), divergence_table, precision=HIGHEST)
    corrections = face_terms(inner_trace - outer_trace, lift_scale).reshape(elements * variables, -1)
    lifted = jnp.dot(corrections, selector.T, precision=HIGHEST).reshape(elements, variables, points)
    rates = jnp.concatenate([-divergence[:, None], -gradient - SOURCE_GAIN * source], axis=1) + lifted
    return wave_state + WAVE_STEP * rates


def to_global_brick(stored, element_cell):
    device_rows = jnp.arange(DEVICES, dtype=jnp.int32)[:, None]
    local_brick = jnp.zeros_like(stored).at[device_rows, element_cell].set(stored)
    trailing = stored.shape[2:]
    shaped = local_brick.reshape((N_GX, N_GY, N_GZ, EBX, EBY, EBZ) + trailing)
    extra = tuple(range(6, 6 + len(trailing)))
    return shaped.transpose((0, 3, 1, 4, 2, 5) + extra).reshape((N_GX * EBX, N_GY * EBY, N_GZ * EBZ) + trailing)


def from_global_brick(brick, element_cell):
    trailing = brick.shape[3:]
    shaped = brick.reshape((N_GX, EBX, N_GY, EBY, N_GZ, EBZ) + trailing)
    extra = tuple(range(6, 6 + len(trailing)))
    local_brick = shaped.transpose((0, 2, 4, 1, 3, 5) + extra).reshape((DEVICES, ELEM) + trailing)
    device_rows = jnp.arange(DEVICES, dtype=jnp.int32)[:, None]
    return local_brick[device_rows, element_cell]


def global_sources(lamb_vector, projection, owner_index, slot_element, element_cell):
    coarse = lamb_vector.reshape(3, NX // 2, 2, NY // 2, 2, NZ // 2, 2).mean(axis=(2, 4, 6))
    blocks = coarse.reshape(3, N_GX, CX // (2 * VS), VS, N_GY, CY // (2 * VS), VS, N_GZ, CZ // (2 * VS), VS)
    volumes = blocks.transpose(1, 4, 7, 2, 5, 8, 0, 3, 6, 9).reshape(DEVICES, NV, 3 * VOL).astype(jnp.bfloat16)
    owners = owner_index.reshape(DEVICES, NV).astype(jnp.int32)
    order_index = jnp.arange(NV, dtype=jnp.int32)
    matches = (owners[:, :, None] == owners[:, None, :]) & (order_index[None, None, :] < order_index[None, :, None])
    ranking = jnp.sum(matches.astype(jnp.int32), axis=-1).astype(jnp.int32)
    slots = owners * CAP + ranking
    placement = (slots[:, None, :] == jnp.arange(SLOTS, dtype=jnp.int32)[None, :, None]).astype(jnp.float32)
    sent = jnp.einsum("dsv,dvc->dsc", placement, volumes.astype(jnp.float32), precision=HIGHEST).astype(jnp.bfloat16)
    received = sent.reshape(N_GX, PEERS, PEERS, CAP, 3 * VOL).transpose(0, 2, 1, 3, 4).reshape(DEVICES, SLOTS, 3, VOL)
    projected = jnp.dot(received.astype(jnp.float32).reshape(-1, VOL), projection, precision=HIGHEST).reshape(DEVICES, SLOTS, 3 * NODES)
    target = (slot_element[:, None, :] == jnp.arange(ELEM, dtype=jnp.int32)[None, :, None]).astype(jnp.float32)
    source = jnp.einsum("dep,dpc->dec", target, projected, precision=HIGHEST).reshape(DEVICES, ELEM, 3, NODES)
    return to_global_brick(source, element_cell)


def reference(velocity, acoustic, projection, owner_index, slot_element, element_cell):
    tables = wave_tables(ORDER)
    selector = tables[2]
    wave_state = to_global_brick(acoustic.reshape(DEVICES, ELEM, 4, NODES), element_cell)
    brick_shape = wave_state.shape
    flow = velocity
    for time_step in range(2):
        padded = jnp.pad(flow, ((0, 0), (1, 1), (1, 1), (1, 1)), mode="wrap")
        flow, lamb_vector = advance(padded)
        source = global_sources(lamb_vector, projection, owner_index, slot_element, element_cell)
        flat_state = wave_state.reshape(-1, 4, NODES)
        inner_trace = face_values(flat_state, selector)
        inner_brick = inner_trace.reshape(brick_shape[:3] + (4, 6, -1))
        padded_trace = jnp.pad(inner_brick, ((1, 1), (1, 1), (1, 1), (0, 0), (0, 0), (0, 0)), mode="wrap")
        outer_trace = outer_traces(padded_trace).reshape(inner_trace.shape)
        flat_state = wave_update(flat_state, inner_trace, outer_trace, source.reshape(-1, 3, NODES), tables)
        wave_state = flat_state.reshape(brick_shape)
    acoustic_out = from_global_brick(wave_state, element_cell).reshape(ELEMENTS, 4, NODES)
    return flow, acoustic_out
```

```python
import jax
import jax.numpy as jnp
import numpy as np
from jax import lax
from jax.experimental import pallas as pl
from jax.experimental.pallas import tpu as pltpu
from jax.sharding import PartitionSpec as P

F32 = jnp.float32
BF = jnp.bfloat16
ORDER = 7
K = ORDER + 1
LANES = 128
ROWS = K**3
FACE = K * K
FLOW_STEP = 0.1
VISCOSITY = 0.05
WAVE_STEP = 0.02
SOURCE_GAIN = 25.0
LIFT = WAVE_STEP * 0.5 * ORDER * (ORDER + 1) / 2.0
XV = 48
YV = 144
ZV = 32


def legendre_table(points, order):
    columns = [points * 0.0 + 1.0, points]
    for degree in range(2, order + 1):
        columns.append(
            ((2 * degree - 1) * points * columns[degree - 1] - (degree - 1) * columns[degree - 2])
            / degree
        )
    return np.stack(columns, axis=1)


def lobatto_tables(order):
    point_count = order + 1
    points = -np.cos(np.pi * np.arange(point_count) / order)
    for _ in range(60):
        legendre = legendre_table(points, order)
        points = points - (points * legendre[:, order] - legendre[:, order - 1]) / (
            point_count * legendre[:, order]
        )
    legendre = legendre_table(points, order)
    highest = legendre[:, order]
    spacing = points[:, None] - points[None, :] + np.eye(point_count)
    derivative = highest[:, None] / (highest[None, :] * spacing)
    derivative = derivative * (1.0 - np.eye(point_count))
    derivative[0, 0] = -order * point_count / 4.0
    derivative[order, order] = order * point_count / 4.0
    return derivative


DERIV = lobatto_tables(ORDER) * (-WAVE_STEP)


def split2(value):
    high = value.astype(BF)
    return high, (value - high.astype(F32)).astype(BF)


def nn(a, b):
    return lax.dot_general(a, b, (((1,), (0,)), ((), ())), preferred_element_type=F32)


def nt(a, b):
    return lax.dot_general(a, b, (((1,), (1,)), ((), ())), preferred_element_type=F32)


def tn(a, b):
    return lax.dot_general(a, b, (((0,), (0,)), ((), ())), preferred_element_type=F32)


def iota(shape, axis):
    return lax.broadcasted_iota(jnp.int32, shape, axis)


def roll(value, shift, axis):
    size = value.shape[axis]
    return pltpu.roll(value, shift % size, axis)


def call(kernel, out_shape, *args, scratch=(), flops=10**6, moved=10**6):
    return pl.pallas_call(
        kernel,
        out_shape=out_shape,
        in_specs=[pl.BlockSpec(memory_space=pltpu.VMEM)] * len(args),
        out_specs=jax.tree.map(lambda _: pl.BlockSpec(memory_space=pltpu.VMEM), out_shape),
        scratch_shapes=list(scratch),
        compiler_params=pltpu.CompilerParams(vmem_limit_bytes=16 * 2**20),
        cost_estimate=pl.CostEstimate(flops=flops, bytes_accessed=moved, transcendentals=0),
    )(*args)


def shape(*dims, dtype=F32):
    return jax.ShapeDtypeStruct(dims, dtype)


def stored_rows(acoustic_ref, first, last):
    return jnp.concatenate([acoustic_ref[:, v, first:last] for v in range(4)], axis=0)


def cell_matrix(cell_ref):
    cell = jnp.concatenate([cell_ref[...]] * 4, axis=1)
    cell = jnp.broadcast_to(cell, (LANES, LANES))
    row, column = iota((LANES, LANES), 0), iota((LANES, LANES), 1)
    return (cell == row % 32) & (row // 32 == column // 32)


def start_kernel(velocity_ref, acoustic_ref, cell_ref, low_ref, high_ref):
    place = jnp.where(cell_matrix(cell_ref), 1.0, 0.0).astype(BF)
    faces = jnp.concatenate(
        [stored_rows(acoustic_ref, 0, FACE), stored_rows(acoustic_ref, ROWS - FACE, ROWS)], axis=1
    )
    brick = nn(place, faces.astype(BF))
    turned = jnp.transpose(brick).astype(BF)
    low_ref[XV:, :] = turned[:FACE]
    high_ref[XV:, :] = turned[FACE:]
    for c in range(3):
        low_ref[c * 16 : c * 16 + 16, :] = velocity_ref[c, 0:16, :].astype(BF)
        high_ref[c * 16 : c * 16 + 16, :] = velocity_ref[c, 112:128, :].astype(BF)


def prepare_kernel(
    acoustic_ref,
    cell_ref,
    projection_ref,
    state_ref,
    ylow_ref,
    yhigh_ref,
    zlow_ref,
    zhigh_ref,
    back_ref,
    table_ref,
):
    chosen = jnp.where(cell_matrix(cell_ref), 1.0, 0.0)
    place = chosen.astype(BF)
    back_ref[...] = jnp.transpose(chosen).astype(BF)
    high, low = split2(stored_rows(acoustic_ref, 0, ROWS))
    brick = nn(place, high) + nn(place, low)
    state_ref[...] = jnp.transpose(brick)
    for a in range(K):
        ylow_ref[a * K : a * K + K, :] = state_ref[a * FACE : a * FACE + K, :]
        yhigh_ref[a * K : a * K + K, :] = state_ref[a * FACE + FACE - K : a * FACE + FACE, :]
    zlow_ref[...] = state_ref[pl.ds(0, FACE, stride=K), :]
    zhigh_ref[...] = state_ref[pl.ds(K - 1, FACE, stride=K), :]
    high, low = split2(projection_ref[...])
    row, column = iota((64, 64), 0), iota((64, 64), 1)
    order = jnp.where(column == (row % 16) * 4 + row // 16, 1.0, 0.0).astype(BF)
    high, low = nn(order, high), nn(order, low)
    table_ref[...] = jnp.transpose(jnp.concatenate([high, low, high], axis=0)).astype(BF)


def y_kernel(velocity_ref, xlow_ref, xhigh_ref, ylow_ref, yhigh_ref, low_ref, high_ref, wide):
    for c in range(3):
        wide[c, 0:16, :] = xlow_ref[c * 16 : c * 16 + 16, :].astype(F32)
        wide[c, 16:144, :] = velocity_ref[c]
        wide[c, 144:160, :] = xhigh_ref[c * 16 : c * 16 + 16, :].astype(F32)
    for out, first, trace in ((low_ref, 0, ylow_ref), (high_ref, 6, yhigh_ref)):
        pieces = []
        for y in range(2):
            for c in range(3):
                pieces.append(wide[c, pl.ds(first + y, 20, stride=8), :])
                pieces.append(jnp.zeros((4, LANES), F32))
        out[0:YV, :] = jnp.concatenate(pieces, axis=0).astype(BF)
        out[YV:, :] = trace[...].astype(BF)


def z_kernel(
    velocity_ref,
    xlow_ref,
    xhigh_ref,
    ylow_ref,
    yhigh_ref,
    zlow_ref,
    zhigh_ref,
    wide_ref,
    own_ref,
    low_ref,
    high_ref,
    held,
):
    held[0] = ylow_ref[0:YV, :].astype(F32)
    held[1] = yhigh_ref[0:YV, :].astype(F32)
    for c in range(3):
        low = xlow_ref[c * 16 : c * 16 + 16, :].astype(F32)
        high = xhigh_ref[c * 16 : c * 16 + 16, :].astype(F32)
        for x in range(2):
            wide_ref[c, x, 2:10, :] = low[x * 8 : x * 8 + 8]
            wide_ref[c, 18 + x, 2:10, :] = high[x * 8 : x * 8 + 8]
        for x in range(16):
            wide_ref[c, 2 + x, 2:10, :] = velocity_ref[c, x * 8 : x * 8 + 8, :]
        for y in range(2):
            for side in range(2):
                rows = held[side, y * 72 + c * 24 : y * 72 + c * 24 + 20, :]
                wide_ref[c, :, y + 10 * side, :] = rows
        wide_ref[c, :, 12:16, :] = jnp.zeros((20, 4, LANES), F32)
    row, column = iota((16, LANES), 0), iota((16, LANES), 1)
    picks = ((row < 2) & (column == row)) | ((row >= 2) & (row < 4) & (column == row + 124))
    picks = jnp.where(picks, 1.0, 0.0).astype(BF)
    for c in range(3):
        rows = wide_ref[c].reshape(320, LANES).astype(BF)
        own = nt(picks, rows)
        own_ref[c, :, 0:320] = own[0:8]
        own_ref[c, :, 320:384] = jnp.zeros((8, 64), F32)
    for out, first, trace in ((low_ref, 0, zlow_ref), (high_ref, 2, zhigh_ref)):
        pieces = []
        for c in range(3):
            for j in range(3):
                pieces.append(own_ref[c, first : first + 2, j * 128 : j * 128 + 128])
        pieces.append(jnp.zeros((ZV - 18, LANES), F32))
        out[0:ZV, :] = jnp.concatenate(pieces, axis=0).astype(BF)
        out[ZV:, :] = trace[...].astype(BF)


def differences(low, high):
    return [[high[a][c] - low[a][c] for c in range(3)] for a in range(3)]


def moved_on(centre, low, high, diff):
    scaled = [(-0.5 * FLOW_STEP) * centre[a] for a in range(3)]
    out = []
    for c in range(3):
        spread = (low[0][c] + high[0][c]) + (low[1][c] + high[1][c]) + (low[2][c] + high[2][c])
        carried = scaled[0] * diff[0][c] + scaled[1] * diff[1][c] + scaled[2] * diff[2][c]
        out.append(
            (1.0 - 6.0 * FLOW_STEP * VISCOSITY) * centre[c]
            + (FLOW_STEP * VISCOSITY) * spread
            + carried
        )
    return out


def lamb(centre, diff):
    w = [diff[1][2] - diff[2][1], diff[2][0] - diff[0][2], diff[0][1] - diff[1][0]]
    return [
        w[1] * centre[2] - w[2] * centre[1],
        w[2] * centre[0] - w[0] * centre[2],
        w[0] * centre[1] - w[1] * centre[0],
    ]


def flow_kernel(
    wide_ref,
    own_ref,
    zlow_ref,
    zhigh_ref,
    place_ref,
    out_ref,
    volume_ref,
    ends,
    halo,
    middle,
    sums,
):
    low = zlow_ref[0:ZV, :].astype(F32)
    high = zhigh_ref[0:ZV, :].astype(F32)
    for c in range(3):
        for j in range(3):
            lane = slice(j * 128, j * 128 + 128)
            at = 2 * (3 * c + j)
            ends[c, 0:2, lane] = low[at : at + 2]
            ends[c, 2:6, lane] = own_ref[c, 0:4, lane]
            ends[c, 6:8, lane] = high[at : at + 2]
    row, column = iota((16, LANES), 0), iota((16, LANES), 1)
    spots = ((row == 1) & (column == 0)) | ((row == 6) & (column == 127))
    spots = jnp.where(spots, 1.0, 0.0).astype(BF)
    zeros = jnp.zeros((8, 384), F32)

    def spread_out(values, level):
        for c in range(3):
            both = jnp.concatenate([values[c], zeros], axis=0).astype(BF)
            halo[level, c] = tn(both, spots)[0:320].reshape(20, 16, LANES)

    edge = [ends[c] for c in range(3)]
    spread_out(edge, 0)
    edge_low = [
        [roll(e, 16, 1) for e in edge],
        [roll(e, 1, 1) for e in edge],
        [roll(e, 1, 0) for e in edge],
    ]
    edge_high = [
        [roll(e, -16, 1) for e in edge],
        [roll(e, -1, 1) for e in edge],
        [roll(e, -1, 0) for e in edge],
    ]
    spread_out(
        moved_on(edge, edge_low, edge_high, differences(edge_low, edge_high)), 1
    )

    def along_z(values, edges):
        lane = iota(values[0].shape, values[0].ndim - 1)
        axis = values[0].ndim - 1
        low = [jnp.where(lane == 0, h, roll(v, 1, axis)) for v, h in zip(values, edges)]
        high = [jnp.where(lane == 127, h, roll(v, -1, axis)) for v, h in zip(values, edges)]
        return low, high

    def plane(source, x, level, y):
        centre = [source[c, x, y, :] for c in range(3)]
        zlow, zhigh = along_z(centre, [halo[level, c, x, y, :] for c in range(3)])
        up = slice(y.start + 1, y.stop + 1)
        down = slice(y.start - 1, y.stop - 1)
        low = [
            [source[c, x - 1, y, :] for c in range(3)],
            [source[c, x, down, :] for c in range(3)],
            zlow,
        ]
        high = [
            [source[c, x + 1, y, :] for c in range(3)],
            [source[c, x, up, :] for c in range(3)],
            zhigh,
        ]
        return centre, low, high

    inner = slice(2, 10)
    for y in (1, 10):
        def line(source, first, at):
            return [source[c, first : first + 16, at, :] for c in range(3)]

        centre = line(wide_ref, 2, y)
        zlow, zhigh = along_z(
            centre, [halo[0, c, 2:18, y, :] for c in range(3)]
        )
        low = [line(wide_ref, 1, y), line(wide_ref, 2, y - 1), zlow]
        high = [line(wide_ref, 3, y), line(wide_ref, 2, y + 1), zhigh]
        new = moved_on(centre, low, high, differences(low, high))
        for c in range(3):
            middle[c, 2:18, y, :] = new[c]

    def add_lamb(parts, x, step):
        i, a = (x // 2) // 4, (x // 2) % 4
        for c in range(3):
            at = ((step * 3 + c) * 4 + a) * 8
            sums[i, at : at + 8, :] = parts[c]

    held = None
    for x in range(1, 19):
        centre, low, high = plane(wide_ref, x, 0, inner)
        diff = differences(low, high)
        new = moved_on(centre, low, high, diff)
        for c in range(3):
            middle[c, x, inner, :] = new[c]
        if 2 <= x < 18:
            parts = lamb(centre, diff)
            if x % 2 == 0:
                held = parts
            else:
                add_lamb([p + h for p, h in zip(parts, held)], x - 2, 0)
    for x in range(2, 18):
        centre, low, high = plane(middle, x, 1, inner)
        diff = differences(low, high)
        new = moved_on(centre, low, high, diff)
        for c in range(3):
            out_ref[c, (x - 2) * 8 : (x - 2) * 8 + 8, :] = new[c]
        parts = lamb(centre, diff)
        if x % 2 == 0:
            held = parts
        else:
            add_lamb([p + h for p, h in zip(parts, held)], x - 2, 1)
    both = []
    for i in range(2):
        both.append(sums[i, pl.ds(0, 96, stride=2), :] + sums[i, pl.ds(1, 96, stride=2), :])
    pairs = jnp.concatenate(both, axis=1)
    pairs = jnp.concatenate([pairs, jnp.zeros((32, 256), F32)], axis=0)
    high, low = split2(pairs)
    place = place_ref[...]
    volume_ref[...] = ((nt(place, high) + nt(place, low)) * (1.0 / 16.0)).astype(BF)


def swapped(value, axis):
    kind = iota(value.shape, value.ndim - 1) // 32
    shift = 32 * (1 + axis)
    last = value.ndim - 1
    return jnp.where(
        kind == 0,
        roll(value, -shift, last),
        jnp.where(kind == 1 + axis, roll(value, shift, last), 0.0),
    )


def outer(axis, own_low, own_high, from_low, from_high):
    if axis == 0:
        return from_low, from_high
    lane = iota(own_low.shape, 1)
    if axis == 1:
        part = (lane // 16) % 2
        low = jnp.where(part == 1, from_low, own_high)
        high = jnp.where(part == 0, from_high, own_low)

        def turn(v):
            return jnp.where(part == 0, roll(v, -16, 1), roll(v, 16, 1))

        return turn(low), turn(high)
    part = lane % 16
    low = jnp.where(part == 15, from_low, own_high)
    high = jnp.where(part == 0, from_high, own_low)
    return (
        jnp.where(part == 0, roll(low, -15, 1), roll(low, 1, 1)),
        jnp.where(part == 15, roll(high, 15, 1), roll(high, -1, 1)),
    )


def lifts(axis, own_low, own_high, from_low, from_high):
    low, high = outer(axis, own_low, own_high, from_low, from_high)
    low, high = own_low - low, own_high - high
    return -LIFT * (swapped(low, axis) + low), LIFT * (swapped(high, axis) - high)


def face_pair(ref, axis):
    if axis == 0:
        return ref[0:FACE, :], ref[ROWS - FACE : ROWS, :]
    if axis == 1:
        low = [ref[a * FACE : a * FACE + K, :] for a in range(K)]
        high = [ref[a * FACE + FACE - K : a * FACE + FACE, :] for a in range(K)]
        return jnp.concatenate(low, axis=0), jnp.concatenate(high, axis=0)
    return ref[pl.ds(0, FACE, stride=K), :], ref[pl.ds(K - 1, FACE, stride=K), :]


def add_pair(ref, axis, low, high):
    if axis == 0:
        ref[0:FACE, :] += low
        ref[ROWS - FACE : ROWS, :] += high
    elif axis == 1:
        for a in range(K):
            ref[a * FACE : a * FACE + K, :] += low[a * K : a * K + K]
            ref[a * FACE + FACE - K : a * FACE + FACE, :] += high[a * K : a * K + K]
    else:
        ref[pl.ds(0, FACE, stride=K), :] += low
        ref[pl.ds(K - 1, FACE, stride=K), :] += high


def volume_part(state_ref, out_ref, column_ref, extra_ref=None):
    for a in range(K):
        rows = [state_ref[a * FACE + b * K : a * FACE + b * K + K, :] for b in range(K)]
        along_y = [swapped(r, 1) for r in rows]
        along_z = [swapped(r, 2) for r in rows]
        for b in range(K):
            total = rows[b]
            at = a * FACE + b * K
            if extra_ref is not None:
                total = total - extra_ref[at : at + K, :]
            for m in range(K):
                total = total + float(DERIV[b, m]) * along_y[m]
            for m in range(K):
                total = total + column_ref[m * K : m * K + K, :] * jnp.broadcast_to(
                    along_z[b][m : m + 1, :], (K, LANES)
                )
            out_ref[at : at + K, :] = total
    for b in range(K):
        rows = [
            swapped(state_ref[a * FACE + b * K : a * FACE + b * K + K, :], 0) for a in range(K)
        ]
        for a in range(K):
            at = a * FACE + b * K
            total = out_ref[at : at + K, :]
            for m in range(K):
                total = total + float(DERIV[a, m]) * rows[m]
            out_ref[at : at + K, :] = total


def first_kernel(
    state_ref, column_ref, xlow_ref, xhigh_ref, ylow_ref, yhigh_ref, out_ref
):
    volume_part(state_ref, out_ref, column_ref)
    for axis, low, high, skip in ((0, xlow_ref, xhigh_ref, XV), (1, ylow_ref, yhigh_ref, YV)):
        pair = face_pair(state_ref, axis)
        pair = lifts(axis, *pair, low[skip:, :].astype(F32), high[skip:, :].astype(F32))
        add_pair(out_ref, axis, *pair)


def source_kernel(
    arrived_ref,
    gather_ref,
    table_ref,
    base_ref,
    zown_low_ref,
    zown_high_ref,
    zlow_ref,
    zhigh_ref,
    state_ref,
    extra_ref,
    xl_ref,
    xh_ref,
    yl_ref,
    yh_ref,
    zl_ref,
    zh_ref,
):
    summed = tn(arrived_ref[...], gather_ref[...])
    kind = iota((16, LANES), 1) // 32
    steps = []
    for t in range(2):
        rows = []
        for z in range(4):
            total = jnp.zeros((16, LANES), F32)
            for c in range(3):
                at = t * 48 + c * 16
                total = jnp.where(
                    kind == 1 + c, summed[at : at + 16, z * 128 : z * 128 + 128], total
                )
            rows.append(total)
        steps.append(jnp.concatenate(rows, axis=0))
    high, low = split2(jnp.concatenate(steps, axis=1))
    source = nn(table_ref[...], jnp.concatenate([high, high, low], axis=0))
    source = (WAVE_STEP * SOURCE_GAIN) * source
    state_ref[...] = base_ref[...] - source[:, 0:LANES]
    extra_ref[...] = source[:, LANES:]
    pair = lifts(
        2,
        zown_low_ref[...],
        zown_high_ref[...],
        zlow_ref[ZV:, :].astype(F32),
        zhigh_ref[ZV:, :].astype(F32),
    )
    add_pair(state_ref, 2, *pair)
    for axis, outs in enumerate(((xl_ref, xh_ref), (yl_ref, yh_ref), (zl_ref, zh_ref))):
        low, high = face_pair(state_ref, axis)
        outs[0][...] = low.astype(BF)
        outs[1][...] = high.astype(BF)


def second_kernel(state_ref, extra_ref, column_ref, out_ref):
    volume_part(state_ref, out_ref, column_ref, extra_ref)


def last_kernel(
    base_ref, state_ref, back_ref, xl_ref, xh_ref, yl_ref, yh_ref, zl_ref, zh_ref, out_ref, total
):
    total[...] = base_ref[...]
    for axis, (low, high) in enumerate(((xl_ref, xh_ref), (yl_ref, yh_ref), (zl_ref, zh_ref))):
        pair = face_pair(state_ref, axis)
        pair = lifts(axis, *pair, low[...].astype(F32), high[...].astype(F32))
        add_pair(total, axis, *pair)
    high, low = split2(jnp.transpose(total[...]))
    back = back_ref[...]
    rows = nn(back, high) + nn(back, low)
    for v in range(4):
        out_ref[:, v, :] = rows[v * 32 : v * 32 + 32, :]


def both_ways(low, high, axis):
    count = lax.axis_size(axis)
    up = [(i, (i + 1) % count) for i in range(count)]
    down = [(b, a) for a, b in up]
    return lax.ppermute(high, axis, up), lax.ppermute(low, axis, down)


def placement(owner_index):
    owners = owner_index[:, 0]
    order = jnp.arange(32, dtype=jnp.int32)
    same = (owners[:, None] == owners[None, :]) & (order[None, :] < order[:, None])
    slots = owners * 2 + jnp.sum(same.astype(jnp.int32), axis=1)
    row, column = iota((256, 256), 0), iota((256, 256), 1)
    wanted = (row // 8) * 2 + row % 2
    fits = (jnp.repeat(slots, 8)[None, :] == wanted) & ((column % 8) // 2 == (row % 8) // 2)
    return fits.astype(BF)


def gathering(slot_element, element_cell):
    element = jnp.arange(32, dtype=jnp.int32)
    named = slot_element[0][:, None] == element[None, :]
    targets = jnp.sum(jnp.where(named, element_cell, 0), axis=1)
    targets = jnp.broadcast_to(targets.reshape(32, 1, 2), (32, 4, 2)).reshape(256)
    row, column = iota((256, 512), 0), iota((256, 512), 1)
    fits = (targets[:, None] == column % 32) & (column // 128 == (row % 8) // 2)
    return fits.astype(BF)


def on_device(velocity, acoustic, projection, owner_index, slot_element, element_cell):
    velocity = velocity.reshape(3, 128, LANES)
    face = shape(FACE, LANES, dtype=BF)
    state = shape(ROWS, LANES)
    column = jnp.asarray(
        np.broadcast_to(DERIV.T.reshape(FACE, 1), (FACE, LANES)), F32
    )
    send = shape(XV + FACE, LANES, dtype=BF)
    xlow, xhigh = call(start_kernel, (send, send), velocity, acoustic, element_cell)
    xlow, xhigh = both_ways(xlow, xhigh, "gx")
    trace = shape(FACE, LANES)
    first, yown_low, yown_high, zown_low, zown_high, back, table = call(
        prepare_kernel,
        (state, trace, trace, trace, trace, shape(LANES, LANES, dtype=BF), shape(ROWS, 192, dtype=BF)),
        acoustic,
        element_cell,
        projection,
    )
    place = placement(owner_index)
    gather = gathering(slot_element, element_cell)
    send = shape(YV + FACE, LANES, dtype=BF)
    ylow, yhigh = call(
        y_kernel,
        (send, send),
        velocity,
        xlow,
        xhigh,
        yown_low,
        yown_high,
        scratch=[pltpu.VMEM((3, 160, LANES), F32)],
    )
    ylow, yhigh = both_ways(ylow, yhigh, "gy")
    send = shape(ZV + FACE, LANES, dtype=BF)
    wide, own, zlow, zhigh = call(
        z_kernel,
        (shape(3, 20, 16, LANES), shape(3, 8, 384), send, send),
        velocity,
        xlow,
        xhigh,
        ylow,
        yhigh,
        zown_low,
        zown_high,
        scratch=[pltpu.VMEM((2, YV, LANES), F32)],
    )
    zlow, zhigh = both_ways(zlow, zhigh, "gz")
    base = call(first_kernel, state, first, column, xlow, xhigh, ylow, yhigh)
    flow, volumes = call(
        flow_kernel,
        (shape(3, 128, LANES), shape(256, LANES, dtype=BF)),
        wide,
        own,
        zlow,
        zhigh,
        place,
        scratch=[
            pltpu.VMEM((3, 8, 384), F32),
            pltpu.VMEM((2, 3, 20, 16, LANES), F32),
            pltpu.VMEM((3, 20, 16, LANES), F32),
            pltpu.VMEM((2, 192, LANES), F32),
        ],
    )
    arrived = lax.all_to_all(
        volumes.reshape(32, 8, LANES), ("gy", "gz"), split_axis=0, concat_axis=0, tiled=True
    ).reshape(256, LANES)
    state1, extra, *faces = call(
        source_kernel,
        (state, state) + (face,) * 6,
        arrived,
        gather,
        table,
        base,
        zown_low,
        zown_high,
        zlow,
        zhigh,
    )
    got = []
    for at, axis in ((4, "gz"), (2, "gy"), (0, "gx")):
        got = list(both_ways(faces[at], faces[at + 1], axis)) + got
    base = call(second_kernel, state, state1, extra, column)
    out = call(
        last_kernel,
        shape(*acoustic.shape),
        base,
        state1,
        back,
        *got,
        scratch=[pltpu.VMEM((ROWS, LANES), F32)],
    )
    return flow.reshape(3, 16, 8, LANES), out


def solution(mesh):
    whole = P(("gx", "gy", "gz"), None, None)
    rows = P(("gx", "gy", "gz"), None)
    flow = P(None, "gx", "gy", "gz")
    return jax.shard_map(
        on_device,
        mesh=mesh,
        in_specs=(flow, whole, P(), rows, rows, rows),
        out_specs=(flow, whole),
        check_vma=False,
    )
```

```python
import jax
import jax.numpy as jnp
import numpy as np
from jax import lax
from jax.experimental import pallas as pl
from jax.experimental.pallas import tpu as pltpu
from jax.sharding import PartitionSpec as P

F32 = jnp.float32
BF = jnp.bfloat16
ORDER = 7
K = ORDER + 1
LANES = 128
ROWS = K**3
FACE = K * K
FLOW_STEP = 0.1
VISCOSITY = 0.05
WAVE_STEP = 0.02
SOURCE_GAIN = 25.0
GAIN = WAVE_STEP * SOURCE_GAIN
LIFT = WAVE_STEP * 0.5 * ORDER * (ORDER + 1) / 2.0
XV = 48
YV = 144
ZV = 32


def legendre_table(points, order):
    columns = [points * 0.0 + 1.0, points]
    for degree in range(2, order + 1):
        columns.append(
            ((2 * degree - 1) * points * columns[degree - 1] - (degree - 1) * columns[degree - 2])
            / degree
        )
    return np.stack(columns, axis=1)


def lobatto_tables(order):
    point_count = order + 1
    points = -np.cos(np.pi * np.arange(point_count) / order)
    for _ in range(60):
        legendre = legendre_table(points, order)
        points = points - (points * legendre[:, order] - legendre[:, order - 1]) / (
            point_count * legendre[:, order]
        )
    legendre = legendre_table(points, order)
    highest = legendre[:, order]
    spacing = points[:, None] - points[None, :] + np.eye(point_count)
    derivative = highest[:, None] / (highest[None, :] * spacing)
    derivative = derivative * (1.0 - np.eye(point_count))
    derivative[0, 0] = -order * point_count / 4.0
    derivative[order, order] = order * point_count / 4.0
    return derivative


DERIV = lobatto_tables(ORDER) * (-WAVE_STEP)


def split2(value):
    high = value.astype(BF)
    return high, (value - high.astype(F32)).astype(BF)


def nn(a, b):
    return lax.dot_general(a, b, (((1,), (0,)), ((), ())), preferred_element_type=F32)


def nt(a, b):
    return lax.dot_general(a, b, (((1,), (1,)), ((), ())), preferred_element_type=F32)


def tn(a, b):
    return lax.dot_general(a, b, (((0,), (0,)), ((), ())), preferred_element_type=F32)


def iota(shape, axis):
    return lax.broadcasted_iota(jnp.int32, shape, axis)


def roll(value, shift, axis):
    size = value.shape[axis]
    return pltpu.roll(value, shift % size, axis)


def call(
    kernel, out_shape, *args, scratch=(), far_in=(), far_out=(), alias={}, flops=10**6, moved=10**6
):
    near, far = pl.BlockSpec(memory_space=pltpu.VMEM), pl.BlockSpec(memory_space=pl.ANY)
    outs = [far if i in far_out else near for i in range(len(jax.tree.leaves(out_shape)))]
    return pl.pallas_call(
        kernel,
        out_shape=out_shape,
        in_specs=[far if i in far_in else near for i in range(len(args))],
        out_specs=tuple(outs) if isinstance(out_shape, tuple) else outs[0],
        scratch_shapes=list(scratch),
        input_output_aliases=alias,
        compiler_params=pltpu.CompilerParams(vmem_limit_bytes=16 * 2**20),
        cost_estimate=pl.CostEstimate(flops=flops, bytes_accessed=moved, transcendentals=0),
    )(*args)


def shape(*dims, dtype=F32):
    return jax.ShapeDtypeStruct(dims, dtype)


def stored_rows(acoustic_ref):
    return jnp.concatenate([acoustic_ref[:, v, :] for v in range(4)], axis=0)


def cell_matrix(cell_ref):
    cell = jnp.concatenate([cell_ref[...]] * 4, axis=1)
    cell = jnp.broadcast_to(cell, (LANES, LANES))
    row, column = iota((LANES, LANES), 0), iota((LANES, LANES), 1)
    return (cell == row % 32) & (row // 32 == column // 32)


def swapped(value, axis):
    kind = iota(value.shape, value.ndim - 1) // 32
    shift = 32 * (1 + axis)
    last = value.ndim - 1
    return jnp.where(
        kind == 0,
        roll(value, -shift, last),
        jnp.where(kind == 1 + axis, roll(value, shift, last), 0.0),
    )


def low_lift(axis, jump):
    return -LIFT * (swapped(jump, axis) + jump)


def high_lift(axis, jump):
    return LIFT * (swapped(jump, axis) - jump)


def cut_of(axis, dims):
    lane = iota(dims, 1)
    if axis == 1:
        part = (lane // 16) % 2
        return part == 0, part == 1
    part = lane % 16
    return part == 0, part == 15


def outer(axis, own_low, own_high, near):
    at_low, at_high = cut_of(axis, own_low.shape)
    low = jnp.where(at_high, near, own_high)
    high = jnp.where(at_low, near, own_low)
    wrap = 16 if axis == 1 else 15
    step = 16 if axis == 1 else 1
    return (
        jnp.where(at_low, roll(low, -wrap, 1), roll(low, step, 1)),
        jnp.where(at_high, roll(high, wrap, 1), roll(high, -step, 1)),
    )


def facing(axis, own_low, own_high):
    at_low, at_high = cut_of(axis, own_low.shape)
    wrap = 16 if axis == 1 else 15
    return jnp.where(at_high, roll(own_low, wrap, 1), roll(own_high, -wrap, 1))


def near_lift(axis, near, own_low, own_high):
    _, at_high = cut_of(axis, near.shape)
    jump = near - facing(axis, own_low, own_high)
    return jnp.where(at_high, high_lift(axis, jump), low_lift(axis, jump))


def inside_lifts(axis, own_low, own_high):
    at_low, at_high = cut_of(axis, own_low.shape)
    low, high = outer(axis, own_low, own_high, own_low)
    low = jnp.where(at_low, 0.0, own_low - low)
    high = jnp.where(at_high, 0.0, own_high - high)
    return low_lift(axis, low), high_lift(axis, high)


def boundary_lifts(axis, own_low, own_high, near):
    at_low, at_high = cut_of(axis, own_low.shape)
    low, high = outer(axis, own_low, own_high, near)
    low = jnp.where(at_low, own_low - low, 0.0)
    high = jnp.where(at_high, own_high - high, 0.0)
    return low_lift(axis, low), high_lift(axis, high)


def face_pair(ref, axis):
    if axis == 0:
        return ref[0:FACE, :], ref[ROWS - FACE : ROWS, :]
    if axis == 1:
        low = [ref[a * FACE : a * FACE + K, :] for a in range(K)]
        high = [ref[a * FACE + FACE - K : a * FACE + FACE, :] for a in range(K)]
        return jnp.concatenate(low, axis=0), jnp.concatenate(high, axis=0)
    return ref[pl.ds(0, FACE, stride=K), :], ref[pl.ds(K - 1, FACE, stride=K), :]


def add_pair(ref, axis, low, high):
    if axis == 0:
        ref[0:FACE, :] += low
        ref[ROWS - FACE : ROWS, :] += high
    elif axis == 1:
        for a in range(K):
            ref[a * FACE : a * FACE + K, :] += low[a * K : a * K + K]
            ref[a * FACE + FACE - K : a * FACE + FACE, :] += high[a * K : a * K + K]
    else:
        ref[pl.ds(0, FACE, stride=K), :] += low
        ref[pl.ds(K - 1, FACE, stride=K), :] += high


def volume_part(state_ref, out_ref, column_ref, extra_ref=None):
    for a in range(K):
        rows = [state_ref[a * FACE + b * K : a * FACE + b * K + K, :] for b in range(K)]
        along_y = [swapped(r, 1) for r in rows]
        along_z = [swapped(r, 2) for r in rows]
        for b in range(K):
            total = rows[b]
            at = a * FACE + b * K
            if extra_ref is not None:
                total = total - extra_ref[at : at + K, :]
            for m in range(K):
                total = total + float(DERIV[b, m]) * along_y[m]
            for m in range(K):
                total = total + column_ref[m * K : m * K + K, :] * jnp.broadcast_to(
                    along_z[b][m : m + 1, :], (K, LANES)
                )
            out_ref[at : at + K, :] = total
    for b in range(K):
        rows = [
            swapped(state_ref[a * FACE + b * K : a * FACE + b * K + K, :], 0) for a in range(K)
        ]
        for a in range(K):
            at = a * FACE + b * K
            total = out_ref[at : at + K, :]
            for m in range(K):
                total = total + float(DERIV[a, m]) * rows[m]
            out_ref[at : at + K, :] = total


def start_kernel(velocity_ref, acoustic_ref, cell_ref, low_ref, high_ref, flow, wave, sems):
    copies = []
    for side, tile in ((0, 0), (1, 3)):
        copies.append((acoustic_ref.at[:, :, tile * LANES : tile * LANES + LANES], wave.at[side]))
    for side, first in ((0, 0), (1, 112)):
        copies.append((velocity_ref.at[:, first : first + 16, :], flow.at[side]))
    copies = [pltpu.make_async_copy(a, b, sems.at[i]) for i, (a, b) in enumerate(copies)]
    for copy in copies:
        copy.start()
    place = jnp.where(cell_matrix(cell_ref), 1.0, 0.0).astype(BF)
    for copy in copies:
        copy.wait()
    faces = jnp.concatenate(
        [
            jnp.where(iota((32, LANES), 1) < FACE, wave[0, :, v, :], wave[1, :, v, :])
            for v in range(4)
        ],
        axis=0,
    )
    turned = jnp.transpose(nn(place, faces.astype(BF))).astype(BF)
    low_ref[XV:, :] = turned[:FACE]
    high_ref[XV:, :] = turned[FACE:]
    for c in range(3):
        low_ref[c * 16 : c * 16 + 16, :] = flow[0, c].astype(BF)
        high_ref[c * 16 : c * 16 + 16, :] = flow[1, c].astype(BF)


def prepare_kernel(
    acoustic_ref,
    cell_ref,
    projection_ref,
    column_ref,
    state_ref,
    base_ref,
    back_ref,
    table_ref,
    faces_ref,
    scratch,
):
    chosen = jnp.where(cell_matrix(cell_ref), 1.0, 0.0)
    place = chosen.astype(BF)
    back_ref[...] = jnp.transpose(chosen).astype(BF)
    high, low = split2(stored_rows(acoustic_ref))
    state_ref[...] = jnp.transpose(nn(place, high) + nn(place, low))
    high, low = split2(projection_ref[...])
    row, column = iota((64, 64), 0), iota((64, 64), 1)
    order = jnp.where(column == (row % 16) * 4 + row // 16, 1.0, 0.0).astype(BF)
    high, low = nn(order, high), nn(order, low)
    whole = jnp.concatenate([high, low, high, jnp.zeros((64, ROWS), F32)], axis=0)
    scratch[0] = jnp.transpose(whole[0:LANES])
    scratch[1] = jnp.transpose(whole[LANES:])
    for i in range(2):
        lane = slice(i * LANES, i * LANES + LANES)
        table_ref[:, lane] = scratch[i].astype(BF)
        for axis in range(3):
            for side, face in enumerate(face_pair(scratch.at[i], axis)):
                faces_ref[2 * axis + side, :, lane] = face.astype(BF)
    volume_part(state_ref, base_ref, column_ref)
    for axis in (1, 2):
        add_pair(base_ref, axis, *inside_lifts(axis, *face_pair(state_ref, axis)))


def y_kernel(
    velocity_ref,
    xlow_ref,
    xhigh_ref,
    state_ref,
    base_ref,
    targets_ref,
    low_ref,
    high_ref,
    out_ref,
    wide,
):
    for c in range(3):
        wide[c, 0:16, :] = xlow_ref[c * 16 : c * 16 + 16, :].astype(F32)
        wide[c, 16:144, :] = velocity_ref[c]
        wide[c, 144:160, :] = xhigh_ref[c * 16 : c * 16 + 16, :].astype(F32)
    own_low, own_high = face_pair(state_ref, 0)
    out_ref[...] = base_ref[...]
    add_pair(
        out_ref,
        0,
        low_lift(0, own_low - xlow_ref[XV:, :].astype(F32)),
        high_lift(0, own_high - xhigh_ref[XV:, :].astype(F32)),
    )
    traces, bases = face_pair(state_ref, 1), face_pair(out_ref, 1)
    spare = jnp.concatenate([targets_ref[...], jnp.zeros((3, LANES), F32)], axis=0)
    for side, (out, first) in enumerate(((low_ref, 0), (high_ref, 6))):
        pieces = []
        for y in range(2):
            for c in range(3):
                pieces.append(wide[c, pl.ds(first + y, 20, stride=8), :])
                pieces.append(spare)
        out[0:YV, :] = jnp.concatenate(pieces, axis=0).astype(BF)
        out[YV : YV + FACE, :] = traces[side].astype(BF)
        out[YV + FACE :, :] = bases[side].astype(BF)


def joined(axis, low, high):
    _, at_high = cut_of(axis, low.shape)
    return jnp.where(at_high, low.astype(F32), high.astype(F32))


def z_kernel(
    velocity_ref,
    xlow_ref,
    xhigh_ref,
    ylow_ref,
    yhigh_ref,
    state_ref,
    base_ref,
    targets_ref,
    wide_ref,
    own_ref,
    low_ref,
    high_ref,
    out_ref,
    near_ref,
    held,
):
    held[0] = ylow_ref[0:YV, :].astype(F32)
    held[1] = yhigh_ref[0:YV, :].astype(F32)
    for c in range(3):
        low = xlow_ref[c * 16 : c * 16 + 16, :].astype(F32)
        high = xhigh_ref[c * 16 : c * 16 + 16, :].astype(F32)
        for x in range(2):
            wide_ref[c, x, 2:10, :] = low[x * 8 : x * 8 + 8]
            wide_ref[c, 18 + x, 2:10, :] = high[x * 8 : x * 8 + 8]
        for x in range(16):
            wide_ref[c, 2 + x, 2:10, :] = velocity_ref[c, x * 8 : x * 8 + 8, :]
        for y in range(2):
            for side in range(2):
                rows = held[side, y * 72 + c * 24 : y * 72 + c * 24 + 20, :]
                wide_ref[c, :, y + 10 * side, :] = rows
        wide_ref[c, :, 12:16, :] = jnp.zeros((20, 4, LANES), F32)
    row, column = iota((16, LANES), 0), iota((16, LANES), 1)
    picks = ((row < 2) & (column == row)) | ((row >= 2) & (row < 4) & (column == row + 124))
    picks = jnp.where(picks, 1.0, 0.0).astype(BF)
    for c in range(3):
        rows = wide_ref[c].reshape(320, LANES).astype(BF)
        own = nt(picks, rows)
        own_ref[c, :, 0:320] = own[0:8]
        own_ref[c, :, 320:384] = jnp.zeros((8, 64), F32)
    near_ref[0:FACE, :] = joined(1, ylow_ref[YV : YV + FACE, :], yhigh_ref[YV : YV + FACE, :])
    near_ref[FACE:, :] = joined(1, ylow_ref[YV + FACE :, :], yhigh_ref[YV + FACE :, :])
    out_ref[...] = base_ref[...]
    add_pair(out_ref, 1, *boundary_lifts(1, *face_pair(state_ref, 1), near_ref[0:FACE, :]))
    traces, bases = face_pair(state_ref, 2), face_pair(out_ref, 2)
    for side, (out, first) in enumerate(((low_ref, 0), (high_ref, 2))):
        pieces = []
        for c in range(3):
            for j in range(3):
                pieces.append(own_ref[c, first : first + 2, j * 128 : j * 128 + 128])
        pieces += [targets_ref[...], jnp.zeros((5, LANES), F32)]
        pieces.append(near_ref[pl.ds(side * (K - 1), K, stride=K), :])
        out[0:ZV, :] = jnp.concatenate(pieces, axis=0).astype(BF)
        out[ZV : ZV + FACE, :] = traces[side].astype(BF)
        out[ZV + FACE :, :] = bases[side].astype(BF)


def differences(low, high):
    return [[high[a][c] - low[a][c] for c in range(3)] for a in range(3)]


def moved_on(centre, low, high, diff):
    scaled = [(-0.5 * FLOW_STEP) * centre[a] for a in range(3)]
    out = []
    for c in range(3):
        spread = (low[0][c] + high[0][c]) + (low[1][c] + high[1][c]) + (low[2][c] + high[2][c])
        carried = scaled[0] * diff[0][c] + scaled[1] * diff[1][c] + scaled[2] * diff[2][c]
        out.append(
            (1.0 - 6.0 * FLOW_STEP * VISCOSITY) * centre[c]
            + (FLOW_STEP * VISCOSITY) * spread
            + carried
        )
    return out


def lamb(centre, diff):
    w = [diff[1][2] - diff[2][1], diff[2][0] - diff[0][2], diff[0][1] - diff[1][0]]
    return [
        w[1] * centre[2] - w[2] * centre[1],
        w[2] * centre[0] - w[0] * centre[2],
        w[0] * centre[1] - w[1] * centre[0],
    ]


def flow_kernel(
    wide_ref,
    own_ref,
    zlow_ref,
    zhigh_ref,
    place_ref,
    out_ref,
    volume_ref,
    ends,
    halo,
    middle,
    sums,
):
    low = zlow_ref[0:ZV, :].astype(F32)
    high = zhigh_ref[0:ZV, :].astype(F32)
    for c in range(3):
        for j in range(3):
            lane = slice(j * 128, j * 128 + 128)
            at = 2 * (3 * c + j)
            ends[c, 0:2, lane] = low[at : at + 2]
            ends[c, 2:6, lane] = own_ref[c, 0:4, lane]
            ends[c, 6:8, lane] = high[at : at + 2]
    row, column = iota((16, LANES), 0), iota((16, LANES), 1)
    spots = ((row == 1) & (column == 0)) | ((row == 6) & (column == 127))
    spots = jnp.where(spots, 1.0, 0.0).astype(BF)
    zeros = jnp.zeros((8, 384), F32)

    def spread_out(values, level):
        for c in range(3):
            both = jnp.concatenate([values[c], zeros], axis=0).astype(BF)
            halo[level, c] = tn(both, spots)[0:320].reshape(20, 16, LANES)

    edge = [ends[c] for c in range(3)]
    spread_out(edge, 0)
    edge_low = [
        [roll(e, 16, 1) for e in edge],
        [roll(e, 1, 1) for e in edge],
        [roll(e, 1, 0) for e in edge],
    ]
    edge_high = [
        [roll(e, -16, 1) for e in edge],
        [roll(e, -1, 1) for e in edge],
        [roll(e, -1, 0) for e in edge],
    ]
    spread_out(
        moved_on(edge, edge_low, edge_high, differences(edge_low, edge_high)), 1
    )

    def along_z(values, edges):
        lane = iota(values[0].shape, values[0].ndim - 1)
        axis = values[0].ndim - 1
        low = [jnp.where(lane == 0, h, roll(v, 1, axis)) for v, h in zip(values, edges)]
        high = [jnp.where(lane == 127, h, roll(v, -1, axis)) for v, h in zip(values, edges)]
        return low, high

    def plane(source, x, level, y):
        centre = [source[c, x, y, :] for c in range(3)]
        zlow, zhigh = along_z(centre, [halo[level, c, x, y, :] for c in range(3)])
        up = slice(y.start + 1, y.stop + 1)
        down = slice(y.start - 1, y.stop - 1)
        low = [
            [source[c, x - 1, y, :] for c in range(3)],
            [source[c, x, down, :] for c in range(3)],
            zlow,
        ]
        high = [
            [source[c, x + 1, y, :] for c in range(3)],
            [source[c, x, up, :] for c in range(3)],
            zhigh,
        ]
        return centre, low, high

    inner = slice(2, 10)
    for y in (1, 10):
        def line(source, first, at):
            return [source[c, first : first + 16, at, :] for c in range(3)]

        centre = line(wide_ref, 2, y)
        zlow, zhigh = along_z(
            centre, [halo[0, c, 2:18, y, :] for c in range(3)]
        )
        low = [line(wide_ref, 1, y), line(wide_ref, 2, y - 1), zlow]
        high = [line(wide_ref, 3, y), line(wide_ref, 2, y + 1), zhigh]
        new = moved_on(centre, low, high, differences(low, high))
        for c in range(3):
            middle[c, 2:18, y, :] = new[c]

    def add_lamb(parts, x, step):
        i, a = (x // 2) // 4, (x // 2) % 4
        for c in range(3):
            at = ((step * 3 + c) * 4 + a) * 8
            sums[i, at : at + 8, :] = parts[c]

    held = None
    for x in range(1, 19):
        centre, low, high = plane(wide_ref, x, 0, inner)
        diff = differences(low, high)
        new = moved_on(centre, low, high, diff)
        for c in range(3):
            middle[c, x, inner, :] = new[c]
        if 2 <= x < 18:
            parts = lamb(centre, diff)
            if x % 2 == 0:
                held = parts
            else:
                add_lamb([p + h for p, h in zip(parts, held)], x - 2, 0)
    for x in range(2, 18):
        centre, low, high = plane(middle, x, 1, inner)
        diff = differences(low, high)
        new = moved_on(centre, low, high, diff)
        for c in range(3):
            out_ref[c, (x - 2) * 8 : (x - 2) * 8 + 8, :] = new[c]
        parts = lamb(centre, diff)
        if x % 2 == 0:
            held = parts
        else:
            add_lamb([p + h for p, h in zip(parts, held)], x - 2, 1)
    both = []
    for i in range(2):
        both.append(sums[i, pl.ds(0, 96, stride=2), :] + sums[i, pl.ds(1, 96, stride=2), :])
    pairs = jnp.concatenate(both, axis=1)
    pairs = jnp.concatenate([pairs, jnp.zeros((32, 256), F32)], axis=0)
    high, low = split2(pairs)
    place = place_ref[...]
    volumes = (nt(place, high) + nt(place, low)) * (1.0 / 16.0)
    lane = iota((256, LANES), 1)
    twice = jnp.where(lane < 48, volumes, roll(volumes, 48, 1)).reshape(4, 8, 8, LANES)
    left = iota((8, 8, LANES), 2) < 48
    for y in range(4):
        part = slice(y * 8, y * 8 + 8)
        volume_ref[part, 0:8, :] = volumes[y * 64 : y * 64 + 64].reshape(8, 8, LANES).astype(BF)
        rows = jnp.where(left, twice[(y + 3) % 4], twice[(y + 1) % 4])
        volume_ref[part, 8:16, :] = rows.astype(BF)
        lower = jnp.concatenate([twice[y, 7:8], twice[y, 0:7]], axis=0)
        upper = jnp.concatenate([twice[y, 1:8], twice[y, 0:1]], axis=0)
        volume_ref[part, 16:24, :] = jnp.where(left, lower, upper).astype(BF)


def gather_matrix(targets, second=None, chosen=None):
    row, column = iota((256, LANES), 0), iota((256, LANES), 1)
    slots = jnp.where(column == (row // 8) * 2 + row % 2, 1.0, 0.0).astype(BF)

    def named(line):
        return nt(slots, jnp.broadcast_to(line, (LANES, LANES)).astype(BF))

    cells = named(targets)
    if second is not None:
        cells = jnp.where(chosen, cells, named(second))
    fits = cells == (column % 32).astype(F32)
    return [
        jnp.where(fits & ((row % 8) // 2 == z), 1.0, 0.0).astype(BF) for z in range(4)
    ]


def near_kernel(
    state_ref,
    base_ref,
    near_ref,
    targets_ref,
    ylow_ref,
    yhigh_ref,
    zlow_ref,
    zhigh_ref,
    out_ref,
    sides_ref,
    gather_ref,
):
    znear = joined(2, zlow_ref[ZV : ZV + FACE, :], zhigh_ref[ZV : ZV + FACE, :])
    own_y, own_z = face_pair(state_ref, 1), face_pair(state_ref, 2)
    out_ref[...] = base_ref[...]
    add_pair(out_ref, 2, *boundary_lifts(2, *own_z, znear))
    ynear = near_ref[0:FACE, :]
    sides_ref[0:FACE, :] = near_ref[FACE:, :] + near_lift(1, ynear, *own_y)
    zbase = joined(2, zlow_ref[ZV + FACE :, :], zhigh_ref[ZV + FACE :, :])
    sides_ref[FACE:, :] = zbase + near_lift(2, znear, *own_z)
    from_low = zlow_ref[0:ZV, :].astype(F32)[24:32]
    from_high = zhigh_ref[0:ZV, :].astype(F32)[24:32]
    at_low, at_high = cut_of(2, (K, LANES))
    jump = near_ref[pl.ds(0, K, stride=K), :] - roll(from_low, -15, 1)
    sides_ref[pl.ds(0, K, stride=K), :] += jnp.where(at_low, low_lift(2, jump), 0.0)
    jump = near_ref[pl.ds(K - 1, K, stride=K), :] - roll(from_high, 15, 1)
    sides_ref[pl.ds(K - 1, K, stride=K), :] += jnp.where(at_high, high_lift(2, jump), 0.0)

    def line(ref, at):
        return ref[0:32, :].astype(F32)[at : at + 1]

    groups = [
        gather_matrix(targets_ref[...]),
        gather_matrix(line(ylow_ref, 20), line(yhigh_ref, 20), cut_of(1, (256, LANES))[1]),
        gather_matrix(line(zlow_ref, 18), line(zhigh_ref, 18), cut_of(2, (256, LANES))[1]),
    ]
    for g, parts in enumerate(groups):
        for z in range(4):
            gather_ref[g, :, z * LANES : z * LANES + LANES] = parts[z]


def stacked(summed, starts):
    kind = iota((16, LANES), 1) // 32
    blocks = []
    for start in starts:
        rows = []
        for z in range(4):
            total = jnp.zeros((16, LANES), F32)
            for c in range(3):
                total = jnp.where(kind == 1 + c, start(summed, c, z), total)
            rows.append(total)
        blocks.append(jnp.concatenate(rows, axis=0))
    high, low = split2(jnp.concatenate(blocks, axis=1) if len(blocks) > 1 else blocks[0])
    return jnp.concatenate([high, high, low, jnp.zeros_like(low)], axis=0)


def at_rows(first):
    def pick(summed, c, z):
        at = first + c * 16
        return summed[at : at + 16, z * LANES : z * LANES + LANES]

    return pick


def by_side(axis):
    def pick(summed, c, z):
        _, at_high = cut_of(axis, (16, LANES))
        return jnp.where(at_high, at_rows(0)(summed, c, z), at_rows(48)(summed, c, z))

    return pick


def send_kernel(arrived_ref, gather_ref, faces_ref, base_ref, low_ref, high_ref, cells_ref):
    rows = arrived_ref[:, 0:8, :].reshape(256, LANES)
    summed = tn(rows, gather_ref[0])
    cells = stacked(summed, (at_rows(0), at_rows(48)))
    cells_ref[...] = cells
    for side, (out, face) in enumerate(zip((low_ref, high_ref), face_pair(base_ref, 0))):
        out[...] = (face - GAIN * nn(faces_ref[side], cells[:, 0:LANES])).astype(BF)


def second_kernel(
    arrived_ref,
    gather_ref,
    table_ref,
    faces_ref,
    cells_ref,
    base_ref,
    sides_ref,
    column_ref,
    back_ref,
    flow_ref,
    out_ref,
    ends_ref,
    flow_out_ref,
    state,
    extra,
    total,
    rows_held,
    sem,
):
    flow_out_ref[...] = flow_ref[...]
    source = GAIN * nn(table_ref[...], cells_ref[...])
    state[...] = base_ref[...] - source[:, 0:LANES]
    extra[...] = source[:, LANES:]
    near = []
    for axis in (1, 2):
        rows = arrived_ref[:, 8 * axis : 8 * axis + 8, :].reshape(256, LANES)
        cells = stacked(tn(rows, gather_ref[axis]), (by_side(axis),))
        at_low, at_high = cut_of(axis, (FACE, LANES))
        face = jnp.where(
            at_high,
            nn(faces_ref[2 * axis + 1], cells),
            nn(faces_ref[2 * axis], cells),
        )
        near.append(sides_ref[(axis - 1) * FACE : axis * FACE, :] - GAIN * face)
    volume_part(state, total, column_ref, extra)
    for axis in (1, 2):
        own_low, own_high = face_pair(state, axis)
        low, high = outer(axis, own_low, own_high, near[axis - 1])
        add_pair(total, axis, low_lift(axis, own_low - low), high_lift(axis, own_high - high))
    own_low, own_high = face_pair(state, 0)
    add_pair(total, 0, low_lift(0, own_low), high_lift(0, own_high))
    high, low = split2(jnp.transpose(total[...]))
    back = back_ref[...]
    rows = nn(back, high) + nn(back, low)
    ends_ref[0] = rows[:, 0:LANES]
    ends_ref[1] = rows[:, 3 * LANES :]
    for v in range(4):
        rows_held[:, v, :] = rows[v * 32 : v * 32 + 32, :]
    copy = pltpu.make_async_copy(rows_held, out_ref, sem)
    copy.start()
    copy.wait()


def last_kernel(
    main_ref, ends_ref, back_ref, low_ref, high_ref, out_ref, held, sems
):
    low, high = low_ref[...].astype(F32), high_ref[...].astype(F32)
    parts = jnp.concatenate([-low_lift(0, low), -high_lift(0, high)], axis=0)
    high, low = split2(jnp.transpose(parts))
    back = back_ref[...]
    rows = nn(back, high) + nn(back, low)
    left = iota((LANES, LANES), 1) < FACE
    copies = []
    for side, tile in ((0, 0), (1, 3)):
        total = ends_ref[side] + jnp.where(left if side == 0 else ~left, rows, 0.0)
        for v in range(4):
            held[side, :, v, :] = total[v * 32 : v * 32 + 32, :]
        copies.append(
            pltpu.make_async_copy(
                held.at[side],
                out_ref.at[:, :, tile * LANES : tile * LANES + LANES],
                sems.at[side],
            )
        )
        copies[-1].start()
    for copy in copies:
        copy.wait()


def both_ways(low, high, axis):
    count = lax.axis_size(axis)
    up = [(i, (i + 1) % count) for i in range(count)]
    down = [(b, a) for a, b in up]
    return lax.ppermute(high, axis, up), lax.ppermute(low, axis, down)


def placement(owner_index):
    owners = owner_index[:, 0]
    order = jnp.arange(32, dtype=jnp.int32)
    same = (owners[:, None] == owners[None, :]) & (order[None, :] < order[:, None])
    slots = owners * 2 + jnp.sum(same.astype(jnp.int32), axis=1)
    row, column = iota((256, 256), 0), iota((256, 256), 1)
    wanted = (row // 8) * 2 + row % 2
    fits = (jnp.repeat(slots, 8)[None, :] == wanted) & ((column % 8) // 2 == (row % 8) // 2)
    return fits.astype(BF)


def slot_cells(slot_element, element_cell):
    element = jnp.arange(32, dtype=jnp.int32)
    named = slot_element[0][:, None] == element[None, :]
    targets = jnp.sum(jnp.where(named, element_cell, 0), axis=1).astype(F32)
    return jnp.concatenate([targets, jnp.zeros((64,), F32)])[None, :]


def on_device(velocity, acoustic, projection, owner_index, slot_element, element_cell):
    velocity = velocity.reshape(3, 128, LANES)
    face = shape(FACE, LANES, dtype=BF)
    state = shape(ROWS, LANES)
    column = jnp.asarray(np.broadcast_to(DERIV.T.reshape(FACE, 1), (FACE, LANES)), F32)
    send = shape(XV + FACE, LANES, dtype=BF)
    xlow, xhigh = call(
        start_kernel,
        (send, send),
        velocity,
        acoustic,
        element_cell,
        far_in=(0, 1),
        scratch=[
            pltpu.VMEM((2, 3, 16, LANES), F32),
            pltpu.VMEM((2, 32, 4, LANES), F32),
            pltpu.SemaphoreType.DMA((4,)),
        ],
    )
    xlow, xhigh = both_ways(xlow, xhigh, "gx")
    first, base, back, table, faces = call(
        prepare_kernel,
        (
            state,
            state,
            shape(LANES, LANES, dtype=BF),
            shape(ROWS, 256, dtype=BF),
            shape(6, FACE, 256, dtype=BF),
        ),
        acoustic,
        element_cell,
        projection,
        column,
        scratch=[pltpu.VMEM((2, ROWS, LANES), F32)],
    )
    place = placement(owner_index)
    targets = slot_cells(slot_element, element_cell)
    send = shape(YV + 2 * FACE, LANES, dtype=BF)
    ylow, yhigh, base = call(
        y_kernel,
        (send, send, state),
        velocity,
        xlow,
        xhigh,
        first,
        base,
        targets,
        scratch=[pltpu.VMEM((3, 160, LANES), F32)],
    )
    ylow, yhigh = both_ways(ylow, yhigh, "gy")
    send = shape(ZV + 2 * FACE, LANES, dtype=BF)
    wide, own, zlow, zhigh, base, near = call(
        z_kernel,
        (shape(3, 20, 16, LANES), shape(3, 8, 384), send, send, state, shape(2 * FACE, LANES)),
        velocity,
        xlow,
        xhigh,
        ylow,
        yhigh,
        first,
        base,
        targets,
        scratch=[pltpu.VMEM((2, YV, LANES), F32)],
    )
    zlow, zhigh = both_ways(zlow, zhigh, "gz")
    flow, volumes = call(
        flow_kernel,
        (shape(3, 128, LANES), shape(32, 24, LANES, dtype=BF)),
        wide,
        own,
        zlow,
        zhigh,
        place,
        scratch=[
            pltpu.VMEM((3, 8, 384), F32),
            pltpu.VMEM((2, 3, 20, 16, LANES), F32),
            pltpu.VMEM((3, 20, 16, LANES), F32),
            pltpu.VMEM((2, 192, LANES), F32),
        ],
    )
    arrived = lax.all_to_all(volumes, ("gy", "gz"), split_axis=0, concat_axis=0, tiled=True)
    base, sides, gather = call(
        near_kernel,
        (state, shape(2 * FACE, LANES), shape(3, 256, 512, dtype=BF)),
        first,
        base,
        near,
        targets,
        ylow,
        yhigh,
        zlow,
        zhigh,
    )
    low, high, cells = call(
        send_kernel, (face, face, shape(256, 256, dtype=BF)), arrived, gather, faces, base
    )
    low, high = both_ways(low, high, "gx")
    main, ends, flow = call(
        second_kernel,
        (shape(*acoustic.shape), shape(2, LANES, LANES), shape(3, 128, LANES)),
        arrived,
        gather,
        table,
        faces,
        cells,
        base,
        sides,
        column,
        back,
        flow,
        far_out=(0,),
        scratch=[pltpu.VMEM((ROWS, LANES), F32)] * 3
        + [pltpu.VMEM(acoustic.shape, F32), pltpu.SemaphoreType.DMA],
    )
    out = call(
        last_kernel,
        shape(*acoustic.shape),
        main,
        ends,
        back,
        low,
        high,
        far_in=(0,),
        far_out=(0,),
        alias={0: 0},
        scratch=[pltpu.VMEM((2, 32, 4, LANES), F32), pltpu.SemaphoreType.DMA((2,))],
    )
    return flow.reshape(3, 16, 8, LANES), out


def solution(mesh):
    whole = P(("gx", "gy", "gz"), None, None)
    rows = P(("gx", "gy", "gz"), None)
    flow = P(None, "gx", "gy", "gz")
    return jax.shard_map(
        on_device,
        mesh=mesh,
        in_specs=(flow, whole, P(), rows, rows, rows),
        out_specs=(flow, whole),
        check_vma=False,
    )
```

```python
import jax
import jax.numpy as jnp
import numpy as np
from jax import lax
from jax.experimental import pallas as pl
from jax.experimental.pallas import tpu as pltpu
from jax.sharding import PartitionSpec as P

F32 = jnp.float32
BF = jnp.bfloat16
ORDER = 7
K = ORDER + 1
LANES = 128
ROWS = K**3
FACE = K * K
FLOW_STEP = 0.1
VISCOSITY = 0.05
WAVE_STEP = 0.02
SOURCE_GAIN = 25.0
GAIN = WAVE_STEP * SOURCE_GAIN
LIFT = WAVE_STEP * 0.5 * ORDER * (ORDER + 1) / 2.0
XV = 48
YV = 144
PARTS = 1
START_GRANT = 56_440_000
ZV = 32


def legendre_table(points, order):
    columns = [points * 0.0 + 1.0, points]
    for degree in range(2, order + 1):
        columns.append(
            ((2 * degree - 1) * points * columns[degree - 1] - (degree - 1) * columns[degree - 2])
            / degree
        )
    return np.stack(columns, axis=1)


def lobatto_tables(order):
    point_count = order + 1
    points = -np.cos(np.pi * np.arange(point_count) / order)
    for _ in range(60):
        legendre = legendre_table(points, order)
        points = points - (points * legendre[:, order] - legendre[:, order - 1]) / (
            point_count * legendre[:, order]
        )
    legendre = legendre_table(points, order)
    highest = legendre[:, order]
    spacing = points[:, None] - points[None, :] + np.eye(point_count)
    derivative = highest[:, None] / (highest[None, :] * spacing)
    derivative = derivative * (1.0 - np.eye(point_count))
    derivative[0, 0] = -order * point_count / 4.0
    derivative[order, order] = order * point_count / 4.0
    return derivative


DERIV = lobatto_tables(ORDER) * (-WAVE_STEP)


def split2(value):
    high = value.astype(BF)
    return high, (value - high.astype(F32)).astype(BF)


def nn(a, b):
    return lax.dot_general(a, b, (((1,), (0,)), ((), ())), preferred_element_type=F32)


def nt(a, b):
    return lax.dot_general(a, b, (((1,), (1,)), ((), ())), preferred_element_type=F32)


def tn(a, b):
    return lax.dot_general(a, b, (((0,), (0,)), ((), ())), preferred_element_type=F32)


def iota(shape, axis):
    return lax.broadcasted_iota(jnp.int32, shape, axis)


def roll(value, shift, axis):
    size = value.shape[axis]
    return pltpu.roll(value, shift % size, axis)


def call(
    kernel, out_shape, *args, scratch=(), far_in=(), far_out=(), alias={}, grant=16 * 2**20
):
    near, far = pl.BlockSpec(memory_space=pltpu.VMEM), pl.BlockSpec(memory_space=pl.ANY)
    outs = [far if i in far_out else near for i in range(len(jax.tree.leaves(out_shape)))]
    return pl.pallas_call(
        kernel,
        out_shape=out_shape,
        in_specs=[far if i in far_in else near for i in range(len(args))],
        out_specs=tuple(outs) if isinstance(out_shape, tuple) else outs[0],
        scratch_shapes=list(scratch),
        input_output_aliases=alias,
        compiler_params=pltpu.CompilerParams(vmem_limit_bytes=grant),
        cost_estimate=pl.CostEstimate(flops=10**6, bytes_accessed=10**6, transcendentals=0),
    )(*args)


def shape(*dims, dtype=F32):
    return jax.ShapeDtypeStruct(dims, dtype)


def stored_rows(acoustic_ref):
    return jnp.concatenate([acoustic_ref[:, v, :] for v in range(4)], axis=0)


def cell_matrix(cell_ref):
    cell = jnp.concatenate([cell_ref[...]] * 4, axis=1)
    cell = jnp.broadcast_to(cell, (LANES, LANES))
    row, column = iota((LANES, LANES), 0), iota((LANES, LANES), 1)
    return (cell == row % 32) & (row // 32 == column // 32)


def swapped(value, axis):
    kind = iota(value.shape, value.ndim - 1) // 32
    shift = 32 * (1 + axis)
    last = value.ndim - 1
    return jnp.where(
        kind == 0,
        roll(value, -shift, last),
        jnp.where(kind == 1 + axis, roll(value, shift, last), 0.0),
    )


def low_lift(axis, jump):
    return -LIFT * (swapped(jump, axis) + jump)


def high_lift(axis, jump):
    return LIFT * (swapped(jump, axis) - jump)


def cut_of(axis, dims):
    lane = iota(dims, 1)
    if axis == 1:
        part = (lane // 16) % 2
        return part == 0, part == 1
    part = lane % 16
    return part == 0, part == 15


def outer(axis, own_low, own_high, near):
    at_low, at_high = cut_of(axis, own_low.shape)
    low = jnp.where(at_high, near, own_high)
    high = jnp.where(at_low, near, own_low)
    wrap = 16 if axis == 1 else 15
    step = 16 if axis == 1 else 1
    return (
        jnp.where(at_low, roll(low, -wrap, 1), roll(low, step, 1)),
        jnp.where(at_high, roll(high, wrap, 1), roll(high, -step, 1)),
    )


def facing(axis, own_low, own_high):
    at_low, at_high = cut_of(axis, own_low.shape)
    wrap = 16 if axis == 1 else 15
    return jnp.where(at_high, roll(own_low, wrap, 1), roll(own_high, -wrap, 1))


def near_lift(axis, near, own_low, own_high):
    _, at_high = cut_of(axis, near.shape)
    jump = near - facing(axis, own_low, own_high)
    return jnp.where(at_high, high_lift(axis, jump), low_lift(axis, jump))


def inside_lifts(axis, own_low, own_high):
    at_low, at_high = cut_of(axis, own_low.shape)
    low, high = outer(axis, own_low, own_high, own_low)
    low = jnp.where(at_low, 0.0, own_low - low)
    high = jnp.where(at_high, 0.0, own_high - high)
    return low_lift(axis, low), high_lift(axis, high)


def boundary_lifts(axis, own_low, own_high, near):
    at_low, at_high = cut_of(axis, own_low.shape)
    low, high = outer(axis, own_low, own_high, near)
    low = jnp.where(at_low, own_low - low, 0.0)
    high = jnp.where(at_high, own_high - high, 0.0)
    return low_lift(axis, low), high_lift(axis, high)


def face_pair(ref, axis):
    if axis == 0:
        return ref[0:FACE, :], ref[ROWS - FACE : ROWS, :]
    if axis == 1:
        low = [ref[a * FACE : a * FACE + K, :] for a in range(K)]
        high = [ref[a * FACE + FACE - K : a * FACE + FACE, :] for a in range(K)]
        return jnp.concatenate(low, axis=0), jnp.concatenate(high, axis=0)
    return ref[pl.ds(0, FACE, stride=K), :], ref[pl.ds(K - 1, FACE, stride=K), :]


def add_pair(ref, axis, low, high):
    if axis == 0:
        ref[0:FACE, :] += low
        ref[ROWS - FACE : ROWS, :] += high
    elif axis == 1:
        for a in range(K):
            ref[a * FACE : a * FACE + K, :] += low[a * K : a * K + K]
            ref[a * FACE + FACE - K : a * FACE + FACE, :] += high[a * K : a * K + K]
    else:
        ref[pl.ds(0, FACE, stride=K), :] += low
        ref[pl.ds(K - 1, FACE, stride=K), :] += high


def volume_part(state_ref, out_ref, column_ref, extra_ref=None):
    for a in range(K):
        rows = [state_ref[a * FACE + b * K : a * FACE + b * K + K, :] for b in range(K)]
        along_y = [swapped(r, 1) for r in rows]
        along_z = [swapped(r, 2) for r in rows]
        for b in range(K):
            total = rows[b]
            at = a * FACE + b * K
            if extra_ref is not None:
                total = total - extra_ref[at : at + K, :]
            for m in range(K):
                total = total + float(DERIV[b, m]) * along_y[m]
            for m in range(K):
                total = total + column_ref[m * K : m * K + K, :] * jnp.broadcast_to(
                    along_z[b][m : m + 1, :], (K, LANES)
                )
            out_ref[at : at + K, :] = total
    for b in range(K):
        rows = [
            swapped(state_ref[a * FACE + b * K : a * FACE + b * K + K, :], 0) for a in range(K)
        ]
        for a in range(K):
            at = a * FACE + b * K
            total = out_ref[at : at + K, :]
            for m in range(K):
                total = total + float(DERIV[a, m]) * rows[m]
            out_ref[at : at + K, :] = total


def load_kernel(velocity_ref, acoustic_ref, lines_ref, faces_ref, flow, wave, sems):
    copies = []
    for side, tile in ((0, 0), (1, 3)):
        copies.append((acoustic_ref.at[:, :, tile * LANES : tile * LANES + LANES], wave.at[side]))
    for side, first in ((0, 0), (1, 112)):
        copies.append((velocity_ref.at[:, first : first + 16, :], flow.at[side]))
    copies = [pltpu.make_async_copy(a, b, sems.at[i]) for i, (a, b) in enumerate(copies)]
    for copy in copies:
        copy.start()
    for copy in copies:
        copy.wait()
    left = iota((32, LANES), 1) < FACE
    for v in range(4):
        rows = jnp.where(left, wave[0, :, v, :], wave[1, :, v, :])
        faces_ref[v * 32 : v * 32 + 32, :] = rows.astype(BF)
    for side in range(2):
        for c in range(3):
            lines_ref[side, c * 16 : c * 16 + 16, :] = flow[side, c].astype(BF)


def start_kernel(lines_ref, faces_ref, cell_ref, low_ref, high_ref, place_ref):
    place = jnp.where(cell_matrix(cell_ref), 1.0, 0.0).astype(BF)
    turned = jnp.transpose(nn(place, faces_ref[...])).astype(BF)
    low_ref[XV:, :] = turned[:FACE]
    high_ref[XV:, :] = turned[FACE:]
    low_ref[0:XV, :] = lines_ref[0]
    high_ref[0:XV, :] = lines_ref[1]
    place_ref[...] = place


def prepare_kernel(
    acoustic_ref,
    place_ref,
    cell_ref,
    slot_ref,
    projection_ref,
    column_ref,
    state_ref,
    base_ref,
    back_ref,
    table_ref,
    faces_ref,
    targets_ref,
    scratch,
):
    slots = jnp.broadcast_to(jnp.concatenate([slot_ref[...]] * 2, axis=1), (32, LANES))
    named = jnp.where(slots == iota((32, LANES), 0), 1.0, 0.0).astype(BF)
    cells = jnp.broadcast_to(cell_ref[...], (16, 32)).astype(F32).astype(BF)
    targets_ref[...] = nn(cells, named)[0:1]
    place = place_ref[...]
    back_ref[...] = jnp.transpose(place.astype(F32)).astype(BF)
    high, low = split2(stored_rows(acoustic_ref))
    state_ref[...] = jnp.transpose(nn(place, high) + nn(place, low))
    high, low = split2(projection_ref[...])
    row, column = iota((64, 64), 0), iota((64, 64), 1)
    order = jnp.where(column == (row % 16) * 4 + row // 16, 1.0, 0.0).astype(BF)
    high, low = nn(order, high), nn(order, low)
    whole = jnp.concatenate([high, low, high, jnp.zeros((64, ROWS), F32)], axis=0)
    scratch[0] = jnp.transpose(whole[0:LANES])
    scratch[1] = jnp.transpose(whole[LANES:])
    for i in range(2):
        lane = slice(i * LANES, i * LANES + LANES)
        table_ref[:, lane] = scratch[i].astype(BF)
        for axis in range(3):
            for side, face in enumerate(face_pair(scratch.at[i], axis)):
                faces_ref[2 * axis + side, :, lane] = face.astype(BF)
    volume_part(state_ref, base_ref, column_ref)
    for axis in (1, 2):
        add_pair(base_ref, axis, *inside_lifts(axis, *face_pair(state_ref, axis)))


def y_kernel(
    velocity_ref,
    xlow_ref,
    xhigh_ref,
    state_ref,
    base_ref,
    targets_ref,
    low_ref,
    high_ref,
    out_ref,
    wide,
):
    for c in range(3):
        wide[c, 0:16, :] = xlow_ref[c * 16 : c * 16 + 16, :].astype(F32)
        wide[c, 16:144, :] = velocity_ref[c]
        wide[c, 144:160, :] = xhigh_ref[c * 16 : c * 16 + 16, :].astype(F32)
    own_low, own_high = face_pair(state_ref, 0)
    out_ref[...] = base_ref[...]
    add_pair(
        out_ref,
        0,
        low_lift(0, own_low - xlow_ref[XV:, :].astype(F32)),
        high_lift(0, own_high - xhigh_ref[XV:, :].astype(F32)),
    )
    faces = packed(1, face_pair(state_ref, 1), face_pair(out_ref, 1))
    spare = jnp.concatenate([targets_ref[...], jnp.zeros((3, LANES), F32)], axis=0)
    for side, (out, first) in enumerate(((low_ref, 0), (high_ref, 6))):
        pieces = []
        for y in range(2):
            for c in range(3):
                pieces.append(wide[c, pl.ds(first + y, 20, stride=8), :])
                pieces.append(spare)
        out[0:YV, :] = jnp.concatenate(pieces, axis=0).astype(BF)
        out[YV:, :] = faces[side]


def packed(axis, traces, bases):
    at_low, at_high = cut_of(axis, traces[0].shape)
    step = 16 if axis == 1 else 1
    return (
        jnp.where(at_low, traces[0], roll(bases[0], step, 1)).astype(BF),
        jnp.where(at_high, traces[1], roll(bases[1], -step, 1)).astype(BF),
    )


def joined(axis, low, high):
    _, at_high = cut_of(axis, low.shape)
    low, high = low.astype(F32), high.astype(F32)
    step = 16 if axis == 1 else 1
    return (
        jnp.where(at_high, low, high),
        jnp.where(at_high, roll(low, step, 1), roll(high, -step, 1)),
    )


def z_kernel(
    velocity_ref,
    xlow_ref,
    xhigh_ref,
    ylow_ref,
    yhigh_ref,
    state_ref,
    base_ref,
    targets_ref,
    wide_ref,
    own_ref,
    low_ref,
    high_ref,
    out_ref,
    near_ref,
    held,
):
    held[0] = ylow_ref[0:YV, :].astype(F32)
    held[1] = yhigh_ref[0:YV, :].astype(F32)
    for c in range(3):
        low = xlow_ref[c * 16 : c * 16 + 16, :].astype(F32)
        high = xhigh_ref[c * 16 : c * 16 + 16, :].astype(F32)
        for x in range(2):
            wide_ref[c, x, 2:10, :] = low[x * 8 : x * 8 + 8]
            wide_ref[c, 18 + x, 2:10, :] = high[x * 8 : x * 8 + 8]
        for x in range(16):
            wide_ref[c, 2 + x, 2:10, :] = velocity_ref[c, x * 8 : x * 8 + 8, :]
        for y in range(2):
            for side in range(2):
                rows = held[side, y * 72 + c * 24 : y * 72 + c * 24 + 20, :]
                wide_ref[c, :, y + 10 * side, :] = rows
        wide_ref[c, :, 12:16, :] = jnp.zeros((20, 4, LANES), F32)
    row, column = iota((16, LANES), 0), iota((16, LANES), 1)
    picks = ((row < 2) & (column == row)) | ((row >= 2) & (row < 4) & (column == row + 124))
    picks = jnp.where(picks, 1.0, 0.0).astype(BF)
    for c in range(3):
        rows = wide_ref[c].reshape(320, LANES).astype(BF)
        own = nt(picks, rows)
        own_ref[c, :, 0:320] = own[0:8]
        own_ref[c, :, 320:384] = jnp.zeros((8, 64), F32)
    trace, base = joined(1, ylow_ref[YV:, :], yhigh_ref[YV:, :])
    near_ref[0:FACE, :] = trace
    near_ref[FACE:, :] = base
    out_ref[...] = base_ref[...]
    add_pair(out_ref, 1, *boundary_lifts(1, *face_pair(state_ref, 1), near_ref[0:FACE, :]))
    faces = packed(2, face_pair(state_ref, 2), face_pair(out_ref, 2))
    for side, (out, first) in enumerate(((low_ref, 0), (high_ref, 2))):
        pieces = []
        for c in range(3):
            for j in range(3):
                pieces.append(own_ref[c, first : first + 2, j * 128 : j * 128 + 128])
        pieces += [targets_ref[...], jnp.zeros((5, LANES), F32)]
        pieces.append(near_ref[pl.ds(side * (K - 1), K, stride=K), :])
        out[0:ZV, :] = jnp.concatenate(pieces, axis=0).astype(BF)
        out[ZV:, :] = faces[side]


def differences(low, high):
    return [[high[a][c] - low[a][c] for c in range(3)] for a in range(3)]


def moved_on(centre, low, high, diff):
    scaled = [(-0.5 * FLOW_STEP) * centre[a] for a in range(3)]
    out = []
    for c in range(3):
        spread = (low[0][c] + high[0][c]) + (low[1][c] + high[1][c]) + (low[2][c] + high[2][c])
        carried = scaled[0] * diff[0][c] + scaled[1] * diff[1][c] + scaled[2] * diff[2][c]
        out.append(
            (1.0 - 6.0 * FLOW_STEP * VISCOSITY) * centre[c]
            + (FLOW_STEP * VISCOSITY) * spread
            + carried
        )
    return out


def lamb(centre, diff):
    w = [diff[1][2] - diff[2][1], diff[2][0] - diff[0][2], diff[0][1] - diff[1][0]]
    return [
        w[1] * centre[2] - w[2] * centre[1],
        w[2] * centre[0] - w[0] * centre[2],
        w[0] * centre[1] - w[1] * centre[0],
    ]


INNER = slice(2, 10)


def along_z(values, low_edge, high_edge):
    axis = values[0].ndim - 1
    lane = iota(values[0].shape, axis)
    low = [jnp.where(lane == 0, h, roll(v, 1, axis)) for v, h in zip(values, low_edge)]
    high = [jnp.where(lane == 127, h, roll(v, -1, axis)) for v, h in zip(values, high_edge)]
    return low, high


def plane(source, x, edges):
    centre = [source[c, x, INNER, :] for c in range(3)]
    zlow, zhigh = along_z(centre, edges, edges)
    low = [
        [source[c, x - 1, INNER, :] for c in range(3)],
        [source[c, x, 1:9, :] for c in range(3)],
        zlow,
    ]
    high = [
        [source[c, x + 1, INNER, :] for c in range(3)],
        [source[c, x, 3:11, :] for c in range(3)],
        zhigh,
    ]
    return centre, low, high


def add_lamb(sums, parts, x, first):
    i, a = (x // 2) // 4, (x // 2) % 4
    for c in range(3):
        at = first + (c * 4 + a) * 8
        sums[i, at : at + 8, :] = parts[c]


def inner_flow_kernel(wide_ref, middle_ref, sums_ref):
    for y in (1, 10):

        def row(first, at):
            return [wide_ref[c, first : first + 16, at, :] for c in range(3)]

        centre = row(2, y)
        nothing = [0.0] * 3
        zlow, zhigh = along_z(centre, nothing, nothing)
        low = [row(1, y), row(2, y - 1), zlow]
        high = [row(3, y), row(2, y + 1), zhigh]
        new = moved_on(centre, low, high, differences(low, high))
        for c in range(3):
            middle_ref[c, 2:18, y, :] = new[c]
    held = None
    for x in range(1, 19):
        centre, low, high = plane(wide_ref, x, [0.0] * 3)
        diff = differences(low, high)
        new = moved_on(centre, low, high, diff)
        for c in range(3):
            middle_ref[c, x, INNER, :] = new[c]
        if 2 <= x < 18:
            parts = lamb(centre, diff)
            if x % 2 == 0:
                held = parts
            else:
                add_lamb(sums_ref, [p + h for p, h in zip(parts, held)], x - 2, 0)


def flow_kernel(
    wide_ref,
    own_ref,
    zlow_ref,
    zhigh_ref,
    place_ref,
    inner_ref,
    inner_sums_ref,
    state_ref,
    base_ref,
    near_ref,
    side_ref,
    out_ref,
    volume_ref,
    base_out_ref,
    sides_ref,
    gather_ref,
    ends,
    halo,
    middle,
    sums,
):
    low = zlow_ref[0:ZV, :].astype(F32)
    high = zhigh_ref[0:ZV, :].astype(F32)
    for c in range(3):
        for j in range(3):
            lane = slice(j * 128, j * 128 + 128)
            at = 2 * (3 * c + j)
            ends[c, 0:2, lane] = low[at : at + 2]
            ends[c, 2:6, lane] = own_ref[c, 0:4, lane]
            ends[c, 6:8, lane] = high[at : at + 2]
    row, column = iota((16, LANES), 0), iota((16, LANES), 1)
    spots = ((row == 1) & (column == 0)) | ((row == 6) & (column == 127))
    spots = jnp.where(spots, 1.0, 0.0).astype(BF)
    zeros = jnp.zeros((8, 384), F32)

    def spread_out(values, level):
        for c in range(3):
            both = jnp.concatenate([values[c], zeros], axis=0).astype(BF)
            halo[level, c] = tn(both, spots)[0:320].reshape(20, 16, LANES)

    edge = [ends[c] for c in range(3)]
    spread_out(edge, 0)
    edge_low = [
        [roll(e, 16, 1) for e in edge],
        [roll(e, 1, 1) for e in edge],
        [roll(e, 1, 0) for e in edge],
    ]
    edge_high = [
        [roll(e, -16, 1) for e in edge],
        [roll(e, -1, 1) for e in edge],
        [roll(e, -1, 0) for e in edge],
    ]
    spread_out(
        moved_on(edge, edge_low, edge_high, differences(edge_low, edge_high)), 1
    )
    end_faces(
        state_ref,
        base_ref,
        near_ref,
        side_ref,
        zlow_ref,
        zhigh_ref,
        base_out_ref,
        sides_ref,
        gather_ref,
    )

    def sign(dims):
        return jnp.where(iota(dims, len(dims) - 1) == 0, -1.0, 1.0)

    def growth(speed, signs):
        return FLOW_STEP * VISCOSITY - (0.5 * FLOW_STEP) * (signs * speed)

    for y in (1, 10):
        rate = growth(wide_ref[2, 2:18, y, :], sign((16, LANES)))
        for c in range(3):
            middle[c, 2:18, y, :] = inner_ref[c, 2:18, y, :] + rate * halo[0, c, 2:18, y, :]
    held = None
    signs = sign((8, LANES))
    for x in range(1, 19):
        centre = [wide_ref[c, x, INNER, :] for c in range(3)]
        edges = [halo[0, c, x, INNER, :] for c in range(3)]
        rate = growth(centre[2], signs)
        for c in range(3):
            middle[c, x, INNER, :] = inner_ref[c, x, INNER, :] + rate * edges[c]
        if 2 <= x < 18:
            first, second = signs * edges[0], signs * edges[1]
            parts = [
                first * centre[2],
                second * centre[2],
                -(second * centre[1]) - first * centre[0],
            ]
            if x % 2 == 0:
                held = parts
            else:
                i, a = ((x - 2) // 2) // 4, ((x - 2) // 2) % 4
                for c in range(3):
                    at = (c * 4 + a) * 8
                    sums[i, at : at + 8, :] = inner_sums_ref[i, at : at + 8, :] + (
                        parts[c] + held[c]
                    )
    for x in range(2, 18):
        centre, low, high = plane(middle, x, [halo[1, c, x, INNER, :] for c in range(3)])
        diff = differences(low, high)
        new = moved_on(centre, low, high, diff)
        for c in range(3):
            out_ref[c, (x - 2) * 8 : (x - 2) * 8 + 8, :] = new[c]
        parts = lamb(centre, diff)
        if x % 2 == 0:
            held = parts
        else:
            add_lamb(sums, [p + h for p, h in zip(parts, held)], x - 2, 96)
    both = []
    for i in range(2):
        both.append(sums[i, pl.ds(0, 96, stride=2), :] + sums[i, pl.ds(1, 96, stride=2), :])
    pairs = jnp.concatenate(both, axis=1)
    pairs = jnp.concatenate([pairs, jnp.zeros((32, 256), F32)], axis=0)
    high, low = split2(pairs)
    place = place_ref[...]
    volumes = (nt(place, high) + nt(place, low)) * (1.0 / 16.0)
    lane = iota((256, LANES), 1)
    twice = jnp.where(lane < 48, volumes, roll(volumes, 48, 1)).reshape(4, 8, 8, LANES)
    left = iota((8, 8, LANES), 2) < 48
    for y in range(4):
        part = slice(y * 8, y * 8 + 8)
        volume_ref[part, 0:8, :] = volumes[y * 64 : y * 64 + 64].reshape(8, 8, LANES).astype(BF)
        rows = jnp.where(left, twice[(y + 3) % 4], twice[(y + 1) % 4])
        volume_ref[part, 8:16, :] = rows.astype(BF)
        lower = jnp.concatenate([twice[y, 7:8], twice[y, 0:7]], axis=0)
        upper = jnp.concatenate([twice[y, 1:8], twice[y, 0:1]], axis=0)
        volume_ref[part, 16:24, :] = jnp.where(left, lower, upper).astype(BF)


def gather_matrix(targets, second=None, chosen=None):
    row, column = iota((256, LANES), 0), iota((256, LANES), 1)
    slots = jnp.where(column == (row // 8) * 2 + row % 2, 1.0, 0.0).astype(BF)

    def named(line):
        return nt(slots, jnp.broadcast_to(line, (LANES, LANES)).astype(BF))

    cells = named(targets)
    if second is not None:
        cells = jnp.where(chosen, cells, named(second))
    fits = cells == (column % 32).astype(F32)
    return [
        jnp.where(fits & ((row % 8) // 2 == z), 1.0, 0.0).astype(BF) for z in range(4)
    ]


def line(ref, at):
    return ref[0:32, :].astype(F32)[at : at + 1]


def placement(owner_ref):
    owner = jnp.concatenate([owner_ref[...]] * 4, axis=1).astype(F32)
    across = jnp.broadcast_to(owner, (LANES, LANES))
    row, column = iota((32, LANES), 0), iota((32, LANES), 1)
    down = nt(jnp.where(row == column, 1.0, 0.0).astype(BF), across.astype(BF))
    earlier = jnp.where((across[0:32] == down) & (column < row), 1.0, 0.0)
    slots = 2.0 * down + jnp.sum(earlier, axis=1, keepdims=True)
    spread = jnp.where(iota((32, 256), 1) // 8 == iota((32, 256), 0), 1.0, 0.0).astype(BF)
    slots = tn(slots.astype(BF), spread)
    slots = jnp.concatenate([slots, slots], axis=0)
    row, column = iota((256, 256), 0), iota((256, 256), 1)
    wanted = ((row // 8) * 2 + row % 2).astype(F32)
    fits = (slots == wanted) & ((column % 8) // 2 == (row % 8) // 2)
    return jnp.where(fits, 1.0, 0.0).astype(BF)


def near_kernel(
    state_ref, near_ref, targets_ref, ylow_ref, yhigh_ref, owner_ref, sides_ref, gather_ref, place_ref
):
    place_ref[...] = placement(owner_ref)
    sides_ref[...] = near_ref[FACE:, :] + near_lift(1, near_ref[0:FACE, :], *face_pair(state_ref, 1))
    groups = [
        gather_matrix(targets_ref[...]),
        gather_matrix(line(ylow_ref, 20), line(yhigh_ref, 20), cut_of(1, (256, LANES))[1]),
    ]
    for g, parts in enumerate(groups):
        for z in range(4):
            gather_ref[g, :, z * LANES : z * LANES + LANES] = parts[z]


def end_faces(
    state_ref, base_ref, near_ref, side_ref, zlow_ref, zhigh_ref, out_ref, sides_ref, gather_ref
):
    trace, base = joined(2, zlow_ref[ZV:, :], zhigh_ref[ZV:, :])
    own = face_pair(state_ref, 2)
    out_ref[...] = base_ref[...]
    add_pair(out_ref, 2, *boundary_lifts(2, *own, trace))
    sides_ref[0:FACE, :] = side_ref[...]
    sides_ref[FACE:, :] = base + near_lift(2, trace, *own)
    from_low = zlow_ref[0:ZV, :].astype(F32)[24:32]
    from_high = zhigh_ref[0:ZV, :].astype(F32)[24:32]
    at_low, at_high = cut_of(2, (K, LANES))
    jump = near_ref[pl.ds(0, K, stride=K), :] - roll(from_low, -15, 1)
    sides_ref[pl.ds(0, K, stride=K), :] += jnp.where(at_low, low_lift(2, jump), 0.0)
    jump = near_ref[pl.ds(K - 1, K, stride=K), :] - roll(from_high, 15, 1)
    sides_ref[pl.ds(K - 1, K, stride=K), :] += jnp.where(at_high, high_lift(2, jump), 0.0)
    parts = gather_matrix(line(zlow_ref, 18), line(zhigh_ref, 18), cut_of(2, (256, LANES))[1])
    for z in range(4):
        gather_ref[:, z * LANES : z * LANES + LANES] = parts[z]


def stacked(summed, starts):
    kind = iota((16, LANES), 1) // 32
    blocks = []
    for start in starts:
        rows = []
        for z in range(4):
            total = jnp.zeros((16, LANES), F32)
            for c in range(3):
                total = jnp.where(kind == 1 + c, start(summed, c, z), total)
            rows.append(total)
        blocks.append(jnp.concatenate(rows, axis=0))
    high, low = split2(jnp.concatenate(blocks, axis=1) if len(blocks) > 1 else blocks[0])
    return jnp.concatenate([high, high, low, jnp.zeros_like(low)], axis=0)


def at_rows(first):
    def pick(summed, c, z):
        at = first + c * 16
        return summed[at : at + 16, z * LANES : z * LANES + LANES]

    return pick


def by_side(axis):
    def pick(summed, c, z):
        _, at_high = cut_of(axis, (16, LANES))
        return jnp.where(at_high, at_rows(0)(summed, c, z), at_rows(48)(summed, c, z))

    return pick


def send_kernel(arrived_ref, gather_ref, faces_ref, base_ref, low_ref, high_ref, cells_ref):
    rows = arrived_ref[:, 0:8, :].reshape(256, LANES)
    summed = tn(rows, gather_ref[0])
    cells = stacked(summed, (at_rows(0), at_rows(48)))
    cells_ref[...] = cells
    for side, (out, face) in enumerate(zip((low_ref, high_ref), face_pair(base_ref, 0))):
        out[...] = (face - GAIN * nn(faces_ref[side], cells[:, 0:LANES])).astype(BF)


def second_kernel(
    arrived_ref,
    gather_ref,
    end_gather_ref,
    table_ref,
    faces_ref,
    cells_ref,
    base_ref,
    sides_ref,
    column_ref,
    back_ref,
    flow_ref,
    out_ref,
    ends_ref,
    flow_out_ref,
    state,
    extra,
    total,
    rows_held,
    sems,
):
    flow_copy = pltpu.make_async_copy(flow_ref, flow_out_ref, sems.at[0])
    flow_copy.start()
    source = GAIN * nn(table_ref[...], cells_ref[...])
    state[...] = base_ref[...] - source[:, 0:LANES]
    extra[...] = source[:, LANES:]
    near = []
    for axis in (1, 2):
        rows = arrived_ref[:, 8 * axis : 8 * axis + 8, :].reshape(256, LANES)
        gather = gather_ref[1] if axis == 1 else end_gather_ref[...]
        cells = stacked(tn(rows, gather), (by_side(axis),))
        at_low, at_high = cut_of(axis, (FACE, LANES))
        face = jnp.where(
            at_high,
            nn(faces_ref[2 * axis + 1], cells),
            nn(faces_ref[2 * axis], cells),
        )
        near.append(sides_ref[(axis - 1) * FACE : axis * FACE, :] - GAIN * face)
    volume_part(state, total, column_ref, extra)
    for axis in (1, 2):
        own_low, own_high = face_pair(state, axis)
        low, high = outer(axis, own_low, own_high, near[axis - 1])
        add_pair(total, axis, low_lift(axis, own_low - low), high_lift(axis, own_high - high))
    own_low, own_high = face_pair(state, 0)
    add_pair(total, 0, low_lift(0, own_low), high_lift(0, own_high))
    back = back_ref[...]

    def turned(first, last):
        high, low = split2(jnp.transpose(total[first:last, :]))
        return nn(back, high) + nn(back, low)

    rows = turned(LANES, 3 * LANES)
    for v in range(4):
        rows_held[:, v, :] = rows[v * 32 : v * 32 + 32, :]
    copy = pltpu.make_async_copy(rows_held, out_ref.at[:, :, LANES : 3 * LANES], sems.at[1])
    copy.start()
    ends_ref[0] = turned(0, LANES)
    ends_ref[1] = turned(3 * LANES, ROWS)
    flow_copy.wait()
    copy.wait()


def last_kernel(
    main_ref, ends_ref, back_ref, low_ref, high_ref, out_ref, held, sems
):
    low, high = low_ref[...].astype(F32), high_ref[...].astype(F32)
    parts = jnp.concatenate([-low_lift(0, low), -high_lift(0, high)], axis=0)
    high, low = split2(jnp.transpose(parts))
    back = back_ref[...]
    rows = nn(back, high) + nn(back, low)
    left = iota((LANES, LANES), 1) < FACE
    copies = []
    for side, tile in ((0, 0), (1, 3)):
        total = ends_ref[side] + jnp.where(left if side == 0 else ~left, rows, 0.0)
        for v in range(4):
            held[side, :, v, :] = total[v * 32 : v * 32 + 32, :]
        for part in range(PARTS):
            some = slice(part * 32 // PARTS, (part + 1) * 32 // PARTS)
            copies.append(
                pltpu.make_async_copy(
                    held.at[side, some],
                    out_ref.at[some, :, tile * LANES : tile * LANES + LANES],
                    sems.at[side * PARTS + part],
                )
            )
            copies[-1].start()
    for copy in copies:
        copy.wait()


def both_ways(low, high, axis):
    count = lax.axis_size(axis)
    up = [(i, (i + 1) % count) for i in range(count)]
    down = [(b, a) for a, b in up]
    return lax.ppermute(high, axis, up), lax.ppermute(low, axis, down)


def on_device(velocity, acoustic, projection, owner_index, slot_element, element_cell):
    velocity = velocity.reshape(3, 128, LANES)
    face = shape(FACE, LANES, dtype=BF)
    state = shape(ROWS, LANES)
    column = jnp.asarray(np.broadcast_to(DERIV.T.reshape(FACE, 1), (FACE, LANES)), F32)
    send = shape(XV + FACE, LANES, dtype=BF)
    chosen = shape(LANES, LANES, dtype=BF)
    lines, faces = call(
        load_kernel,
        (shape(2, XV, LANES, dtype=BF), shape(LANES, LANES, dtype=BF)),
        velocity,
        acoustic,
        far_in=(0, 1),
        grant=START_GRANT,
        scratch=[
            pltpu.VMEM((2, 3, 16, LANES), F32),
            pltpu.VMEM((2, 32, 4, LANES), F32),
            pltpu.SemaphoreType.DMA((4,)),
        ],
    )
    chosen = shape(LANES, LANES, dtype=BF)
    xlow, xhigh, chosen = call(start_kernel, (send, send, chosen), lines, faces, element_cell)
    xlow, xhigh = both_ways(xlow, xhigh, "gx")
    first, base, back, table, faces, targets = call(
        prepare_kernel,
        (
            state,
            state,
            shape(LANES, LANES, dtype=BF),
            shape(ROWS, 256, dtype=BF),
            shape(6, FACE, 256, dtype=BF),
            shape(1, LANES),
        ),
        acoustic,
        chosen,
        element_cell,
        slot_element,
        projection,
        column,
        scratch=[pltpu.VMEM((2, ROWS, LANES), F32)],
    )
    send = shape(YV + FACE, LANES, dtype=BF)
    ylow, yhigh, base = call(
        y_kernel,
        (send, send, state),
        velocity,
        xlow,
        xhigh,
        first,
        base,
        targets,
        scratch=[pltpu.VMEM((3, 160, LANES), F32)],
    )
    ylow, yhigh = both_ways(ylow, yhigh, "gy")
    send = shape(ZV + FACE, LANES, dtype=BF)
    wide, own, zlow, zhigh, base, near = call(
        z_kernel,
        (shape(3, 20, 16, LANES), shape(3, 8, 384), send, send, state, shape(2 * FACE, LANES)),
        velocity,
        xlow,
        xhigh,
        ylow,
        yhigh,
        first,
        base,
        targets,
        scratch=[pltpu.VMEM((2, YV, LANES), F32)],
    )
    zlow, zhigh = both_ways(zlow, zhigh, "gz")
    middle, sums = call(
        inner_flow_kernel, (shape(3, 20, 16, LANES), shape(2, 96, LANES)), wide
    )
    side, gather, place = call(
        near_kernel,
        (shape(FACE, LANES), shape(2, 256, 512, dtype=BF), shape(256, 256, dtype=BF)),
        first,
        near,
        targets,
        ylow,
        yhigh,
        owner_index.reshape(1, 32),
    )
    flow, volumes, base, sides, end_gather = call(
        flow_kernel,
        (
            shape(3, 128, LANES),
            shape(32, 24, LANES, dtype=BF),
            state,
            shape(2 * FACE, LANES),
            shape(256, 512, dtype=BF),
        ),
        wide,
        own,
        zlow,
        zhigh,
        place,
        middle,
        sums,
        first,
        base,
        near,
        side,
        scratch=[
            pltpu.VMEM((3, 8, 384), F32),
            pltpu.VMEM((2, 3, 20, 16, LANES), F32),
            pltpu.VMEM((3, 20, 16, LANES), F32),
            pltpu.VMEM((2, 192, LANES), F32),
        ],
    )
    arrived = lax.all_to_all(volumes, ("gy", "gz"), split_axis=0, concat_axis=0, tiled=True)
    low, high, cells = call(
        send_kernel, (face, face, shape(256, 256, dtype=BF)), arrived, gather, faces, base
    )
    low, high = both_ways(low, high, "gx")
    main, ends, flow = call(
        second_kernel,
        (shape(*acoustic.shape), shape(2, LANES, LANES), shape(3, 128, LANES)),
        arrived,
        gather,
        end_gather,
        table,
        faces,
        cells,
        base,
        sides,
        column,
        back,
        flow,
        far_out=(0, 2),
        scratch=[pltpu.VMEM((ROWS, LANES), F32)] * 3
        + [pltpu.VMEM((32, 4, 2 * LANES), F32), pltpu.SemaphoreType.DMA((2,))],
    )
    out = call(
        last_kernel,
        shape(*acoustic.shape),
        main,
        ends,
        back,
        low,
        high,
        far_in=(0,),
        far_out=(0,),
        alias={0: 0},
        scratch=[pltpu.VMEM((2, 32, 4, LANES), F32), pltpu.SemaphoreType.DMA((2 * PARTS,))],
    )
    return flow.reshape(3, 16, 8, LANES), out


def solution(mesh):
    whole = P(("gx", "gy", "gz"), None, None)
    rows = P(("gx", "gy", "gz"), None)
    flow = P(None, "gx", "gy", "gz")
    return jax.shard_map(
        on_device,
        mesh=mesh,
        in_specs=(flow, whole, P(), rows, rows, rows),
        out_specs=(flow, whole),
        check_vma=False,
    )
```

```python
import jax
import jax.numpy as jnp
import numpy as np
from jax import lax
from jax.experimental import pallas as pl
from jax.experimental.pallas import tpu as pltpu
from jax.sharding import PartitionSpec as P

F32 = jnp.float32
BF = jnp.bfloat16
ORDER = 7
K = ORDER + 1
LANES = 128
ROWS = K**3
FACE = K * K
FLOW_STEP = 0.1
VISCOSITY = 0.05
WAVE_STEP = 0.02
SOURCE_GAIN = 25.0
GAIN = WAVE_STEP * SOURCE_GAIN
LIFT = WAVE_STEP * 0.5 * ORDER * (ORDER + 1) / 2.0
XV = 48
YV = 120
PARTS = 1
START_GRANT = 56_440_000
ZV = 32


def legendre_table(points, order):
    columns = [points * 0.0 + 1.0, points]
    for degree in range(2, order + 1):
        columns.append(
            ((2 * degree - 1) * points * columns[degree - 1] - (degree - 1) * columns[degree - 2])
            / degree
        )
    return np.stack(columns, axis=1)


def lobatto_tables(order):
    point_count = order + 1
    points = -np.cos(np.pi * np.arange(point_count) / order)
    for _ in range(60):
        legendre = legendre_table(points, order)
        points = points - (points * legendre[:, order] - legendre[:, order - 1]) / (
            point_count * legendre[:, order]
        )
    legendre = legendre_table(points, order)
    highest = legendre[:, order]
    spacing = points[:, None] - points[None, :] + np.eye(point_count)
    derivative = highest[:, None] / (highest[None, :] * spacing)
    derivative = derivative * (1.0 - np.eye(point_count))
    derivative[0, 0] = -order * point_count / 4.0
    derivative[order, order] = order * point_count / 4.0
    return derivative


DERIV = lobatto_tables(ORDER) * (-WAVE_STEP)


def split2(value):
    high = value.astype(BF)
    return high, (value - high.astype(F32)).astype(BF)


def nn(a, b):
    return lax.dot_general(a, b, (((1,), (0,)), ((), ())), preferred_element_type=F32)


def nt(a, b):
    return lax.dot_general(a, b, (((1,), (1,)), ((), ())), preferred_element_type=F32)


def tn(a, b):
    return lax.dot_general(a, b, (((0,), (0,)), ((), ())), preferred_element_type=F32)


def iota(shape, axis):
    return lax.broadcasted_iota(jnp.int32, shape, axis)


def roll(value, shift, axis):
    size = value.shape[axis]
    return pltpu.roll(value, shift % size, axis)


def call(
    kernel, out_shape, *args, scratch=(), far_in=(), far_out=(), alias={}, grant=16 * 2**20
):
    near, far = pl.BlockSpec(memory_space=pltpu.VMEM), pl.BlockSpec(memory_space=pl.ANY)
    outs = [far if i in far_out else near for i in range(len(jax.tree.leaves(out_shape)))]
    return pl.pallas_call(
        kernel,
        out_shape=out_shape,
        in_specs=[far if i in far_in else near for i in range(len(args))],
        out_specs=tuple(outs) if isinstance(out_shape, tuple) else outs[0],
        scratch_shapes=list(scratch),
        input_output_aliases=alias,
        compiler_params=pltpu.CompilerParams(vmem_limit_bytes=grant),
        cost_estimate=pl.CostEstimate(flops=10**6, bytes_accessed=10**6, transcendentals=0),
    )(*args)


def shape(*dims, dtype=F32):
    return jax.ShapeDtypeStruct(dims, dtype)


def stored_rows(acoustic_ref):
    return jnp.concatenate([acoustic_ref[:, v, :] for v in range(4)], axis=0)


def cell_matrix(cell_ref):
    cell = jnp.concatenate([cell_ref[...]] * 4, axis=1)
    cell = jnp.broadcast_to(cell, (LANES, LANES))
    row, column = iota((LANES, LANES), 0), iota((LANES, LANES), 1)
    return (cell == row % 32) & (row // 32 == column // 32)


def swapped(value, axis):
    kind = iota(value.shape, value.ndim - 1) // 32
    shift = 32 * (1 + axis)
    last = value.ndim - 1
    return jnp.where(
        kind == 0,
        roll(value, -shift, last),
        jnp.where(kind == 1 + axis, roll(value, shift, last), 0.0),
    )


def low_lift(axis, jump):
    return -LIFT * (swapped(jump, axis) + jump)


def high_lift(axis, jump):
    return LIFT * (swapped(jump, axis) - jump)


def cut_of(axis, dims):
    lane = iota(dims, 1)
    if axis == 1:
        part = (lane // 16) % 2
        return part == 0, part == 1
    part = lane % 16
    return part == 0, part == 15


def outer(axis, own_low, own_high, near):
    at_low, at_high = cut_of(axis, own_low.shape)
    low = jnp.where(at_high, near, own_high)
    high = jnp.where(at_low, near, own_low)
    wrap = 16 if axis == 1 else 15
    step = 16 if axis == 1 else 1
    return (
        jnp.where(at_low, roll(low, -wrap, 1), roll(low, step, 1)),
        jnp.where(at_high, roll(high, wrap, 1), roll(high, -step, 1)),
    )


def facing(axis, own_low, own_high):
    at_low, at_high = cut_of(axis, own_low.shape)
    wrap = 16 if axis == 1 else 15
    return jnp.where(at_high, roll(own_low, wrap, 1), roll(own_high, -wrap, 1))


def near_lift(axis, near, own_low, own_high):
    _, at_high = cut_of(axis, near.shape)
    jump = near - facing(axis, own_low, own_high)
    return jnp.where(at_high, high_lift(axis, jump), low_lift(axis, jump))


def inside_lifts(axis, own_low, own_high):
    at_low, at_high = cut_of(axis, own_low.shape)
    low, high = outer(axis, own_low, own_high, own_low)
    low = jnp.where(at_low, 0.0, own_low - low)
    high = jnp.where(at_high, 0.0, own_high - high)
    return low_lift(axis, low), high_lift(axis, high)


def boundary_lifts(axis, own_low, own_high, near):
    at_low, at_high = cut_of(axis, own_low.shape)
    low, high = outer(axis, own_low, own_high, near)
    low = jnp.where(at_low, own_low - low, 0.0)
    high = jnp.where(at_high, own_high - high, 0.0)
    return low_lift(axis, low), high_lift(axis, high)


def face_pair(ref, axis):
    if axis == 0:
        return ref[0:FACE, :], ref[ROWS - FACE : ROWS, :]
    if axis == 1:
        low = [ref[a * FACE : a * FACE + K, :] for a in range(K)]
        high = [ref[a * FACE + FACE - K : a * FACE + FACE, :] for a in range(K)]
        return jnp.concatenate(low, axis=0), jnp.concatenate(high, axis=0)
    return ref[pl.ds(0, FACE, stride=K), :], ref[pl.ds(K - 1, FACE, stride=K), :]


def add_pair(ref, axis, low, high):
    if axis == 0:
        ref[0:FACE, :] += low
        ref[ROWS - FACE : ROWS, :] += high
    elif axis == 1:
        for a in range(K):
            ref[a * FACE : a * FACE + K, :] += low[a * K : a * K + K]
            ref[a * FACE + FACE - K : a * FACE + FACE, :] += high[a * K : a * K + K]
    else:
        ref[pl.ds(0, FACE, stride=K), :] += low
        ref[pl.ds(K - 1, FACE, stride=K), :] += high


def volume_part(state_ref, out_ref, column_ref, extra_ref=None):
    for a in range(K):
        rows = [state_ref[a * FACE + b * K : a * FACE + b * K + K, :] for b in range(K)]
        along_y = [swapped(r, 1) for r in rows]
        along_z = [swapped(r, 2) for r in rows]
        for b in range(K):
            total = rows[b]
            at = a * FACE + b * K
            if extra_ref is not None:
                total = total - extra_ref[at : at + K, :]
            for m in range(K):
                total = total + float(DERIV[b, m]) * along_y[m]
            for m in range(K):
                total = total + column_ref[m * K : m * K + K, :] * jnp.broadcast_to(
                    along_z[b][m : m + 1, :], (K, LANES)
                )
            out_ref[at : at + K, :] = total
    for b in range(K):
        rows = [
            swapped(state_ref[a * FACE + b * K : a * FACE + b * K + K, :], 0) for a in range(K)
        ]
        for a in range(K):
            at = a * FACE + b * K
            total = out_ref[at : at + K, :]
            for m in range(K):
                total = total + float(DERIV[a, m]) * rows[m]
            out_ref[at : at + K, :] = total


def load_kernel(velocity_ref, acoustic_ref, lines_ref, faces_ref, flow, wave, sems):
    copies = []
    for side, tile in ((0, 0), (1, 3)):
        copies.append((acoustic_ref.at[:, :, tile * LANES : tile * LANES + LANES], wave.at[side]))
    for side, first in ((0, 0), (1, 112)):
        copies.append((velocity_ref.at[:, first : first + 16, :], flow.at[side]))
    copies = [pltpu.make_async_copy(a, b, sems.at[i]) for i, (a, b) in enumerate(copies)]
    for copy in copies:
        copy.start()
    for copy in copies:
        copy.wait()
    left = iota((32, LANES), 1) < FACE
    for v in range(4):
        rows = jnp.where(left, wave[0, :, v, :], wave[1, :, v, :])
        faces_ref[v * 32 : v * 32 + 32, :] = rows.astype(BF)
    for side in range(2):
        for c in range(3):
            lines_ref[side, c * 16 : c * 16 + 16, :] = flow[side, c].astype(BF)


def start_kernel(lines_ref, faces_ref, cell_ref, low_ref, high_ref, place_ref):
    place = jnp.where(cell_matrix(cell_ref), 1.0, 0.0).astype(BF)
    turned = jnp.transpose(nn(place, faces_ref[...])).astype(BF)
    low_ref[XV:, :] = turned[:FACE]
    high_ref[XV:, :] = turned[FACE:]
    low_ref[0:XV, :] = lines_ref[0]
    high_ref[0:XV, :] = lines_ref[1]
    place_ref[...] = place


def prepare_kernel(
    acoustic_ref,
    place_ref,
    cell_ref,
    slot_ref,
    column_ref,
    state_ref,
    base_ref,
    targets_ref,
):
    slots = jnp.broadcast_to(jnp.concatenate([slot_ref[...]] * 2, axis=1), (32, LANES))
    named = jnp.where(slots == iota((32, LANES), 0), 1.0, 0.0).astype(BF)
    cells = jnp.broadcast_to(cell_ref[...], (16, 32)).astype(F32).astype(BF)
    targets_ref[...] = nn(cells, named)[0:1]
    place = place_ref[...]
    high, low = split2(stored_rows(acoustic_ref))
    state_ref[...] = jnp.transpose(nn(place, high) + nn(place, low))
    volume_part(state_ref, base_ref, column_ref)
    for axis in (1, 2):
        add_pair(base_ref, axis, *inside_lifts(axis, *face_pair(state_ref, axis)))


def chunk_matrix(rows, low_row, high_row):
    row, column = iota((rows, 9 * LANES), 0), iota((rows, 9 * LANES), 1)
    chunk, lane = column // LANES, column % LANES
    fits = ((row == low_row(chunk)) & (lane == 0)) | ((row == high_row(chunk)) & (lane == 127))
    return jnp.where(fits, 1.0, 0.0).astype(BF)


def table_kernel(
    order_ref,
    chosen_ref,
    projection_ref,
    owner_ref,
    back_ref,
    table_ref,
    faces_ref,
    place_ref,
    first_ref,
    second_ref,
    scratch,
):
    del order_ref
    back_ref[...] = jnp.transpose(chosen_ref[...].astype(F32)).astype(BF)
    place_ref[...] = placement(owner_ref)
    first_ref[...] = chunk_matrix(2 * ZV, lambda m: 2 * m + 1, lambda m: ZV + 2 * m)
    second_ref[...] = chunk_matrix(80, lambda m: 8 * m + 1, lambda m: 8 * m + 6)
    high, low = split2(projection_ref[...])
    row, column = iota((64, 64), 0), iota((64, 64), 1)
    order = jnp.where(column == (row % 16) * 4 + row // 16, 1.0, 0.0).astype(BF)
    high, low = nn(order, high), nn(order, low)
    whole = jnp.concatenate([high, low, high, jnp.zeros((64, ROWS), F32)], axis=0)
    scratch[0] = jnp.transpose(whole[0:LANES])
    scratch[1] = jnp.transpose(whole[LANES:])
    for i in range(2):
        lane = slice(i * LANES, i * LANES + LANES)
        table_ref[:, lane] = scratch[i].astype(BF)
        for axis in range(3):
            for side, face in enumerate(face_pair(scratch.at[i], axis)):
                faces_ref[2 * axis + side, :, lane] = face.astype(BF)


def y_kernel(
    velocity_ref,
    xlow_ref,
    xhigh_ref,
    state_ref,
    base_ref,
    targets_ref,
    low_ref,
    high_ref,
    out_ref,
    wide,
):
    for c in range(3):
        wide[c, 0:16, :] = xlow_ref[c * 16 : c * 16 + 16, :].astype(F32)
        wide[c, 16:144, :] = velocity_ref[c]
        wide[c, 144:160, :] = xhigh_ref[c * 16 : c * 16 + 16, :].astype(F32)
    own_low, own_high = face_pair(state_ref, 0)
    out_ref[...] = base_ref[...]
    add_pair(
        out_ref,
        0,
        low_lift(0, own_low - xlow_ref[XV:, :].astype(F32)),
        high_lift(0, own_high - xhigh_ref[XV:, :].astype(F32)),
    )
    faces = packed(1, face_pair(state_ref, 1), face_pair(out_ref, 1))
    spare = jnp.concatenate([targets_ref[...], jnp.zeros((5, LANES), F32)], axis=0)
    for side, (out, near, far) in enumerate(((low_ref, 0, 1), (high_ref, 7, 6))):
        pieces = []
        for c in range(3):
            pieces.append(wide[c, pl.ds(8 + near, 18, stride=8), :])
            pieces.append(spare)
            pieces.append(wide[c, pl.ds(16 + far, 16, stride=8), :])
        out[0:YV, :] = jnp.concatenate(pieces, axis=0).astype(BF)
        out[YV:, :] = faces[side]


def packed(axis, traces, bases):
    at_low, at_high = cut_of(axis, traces[0].shape)
    step = 16 if axis == 1 else 1
    return (
        jnp.where(at_low, traces[0], roll(bases[0], step, 1)).astype(BF),
        jnp.where(at_high, traces[1], roll(bases[1], -step, 1)).astype(BF),
    )


def joined(axis, low, high):
    _, at_high = cut_of(axis, low.shape)
    low, high = low.astype(F32), high.astype(F32)
    step = 16 if axis == 1 else 1
    return (
        jnp.where(at_high, low, high),
        jnp.where(at_high, roll(low, step, 1), roll(high, -step, 1)),
    )


def z_kernel(
    order_ref,
    velocity_ref,
    xlow_ref,
    xhigh_ref,
    ylow_ref,
    yhigh_ref,
    state_ref,
    base_ref,
    targets_ref,
    wide_ref,
    own_ref,
    low_ref,
    high_ref,
    out_ref,
    near_ref,
    held,
):
    del order_ref
    held[0] = ylow_ref[0:YV, :].astype(F32)
    held[1] = yhigh_ref[0:YV, :].astype(F32)
    for c in range(3):
        low = xlow_ref[c * 16 : c * 16 + 16, :].astype(F32)
        high = xhigh_ref[c * 16 : c * 16 + 16, :].astype(F32)
        for x in range(2):
            wide_ref[c, x, 2:10, :] = low[x * 8 : x * 8 + 8]
            wide_ref[c, 18 + x, 2:10, :] = high[x * 8 : x * 8 + 8]
        for x in range(16):
            wide_ref[c, 2 + x, 2:10, :] = velocity_ref[c, x * 8 : x * 8 + 8, :]
        for x in (0, 1, 18, 19):
            wide_ref[c, x, 0:2, :] = jnp.zeros((2, LANES), F32)
            wide_ref[c, x, 10:12, :] = jnp.zeros((2, LANES), F32)
        for side in range(2):
            at = c * 40
            wide_ref[c, 1:19, 1 + 9 * side, :] = held[side, at : at + 18, :]
            wide_ref[c, 2:18, 11 * side, :] = held[side, at + 24 : at + 40, :]
        wide_ref[c, :, 12:16, :] = jnp.zeros((20, 4, LANES), F32)
    row, column = iota((16, LANES), 0), iota((16, LANES), 1)
    picks = ((row < 2) & (column == row)) | ((row >= 2) & (row < 4) & (column == row + 124))
    picks = jnp.where(picks, 1.0, 0.0).astype(BF)
    for c in range(3):
        rows = wide_ref[c].reshape(320, LANES).astype(BF)
        own = nt(picks, rows)
        own_ref[c, :, 0:320] = own[0:8]
        own_ref[c, :, 320:384] = jnp.zeros((8, 64), F32)
    trace, base = joined(1, ylow_ref[YV:, :], yhigh_ref[YV:, :])
    near_ref[0:FACE, :] = trace
    near_ref[FACE:, :] = base
    out_ref[...] = base_ref[...]
    add_pair(out_ref, 1, *boundary_lifts(1, *face_pair(state_ref, 1), near_ref[0:FACE, :]))
    faces = packed(2, face_pair(state_ref, 2), face_pair(out_ref, 2))
    for side, (out, first) in enumerate(((low_ref, 0), (high_ref, 2))):
        pieces = []
        for c in range(3):
            for j in range(3):
                pieces.append(own_ref[c, first : first + 2, j * 128 : j * 128 + 128])
        pieces += [targets_ref[...], jnp.zeros((5, LANES), F32)]
        pieces.append(near_ref[pl.ds(side * (K - 1), K, stride=K), :])
        out[0:ZV, :] = jnp.concatenate(pieces, axis=0).astype(BF)
        out[ZV:, :] = faces[side]


def differences(low, high):
    return [[high[a][c] - low[a][c] for c in range(3)] for a in range(3)]


def moved_on(centre, low, high, diff):
    scaled = [(-0.5 * FLOW_STEP) * centre[a] for a in range(3)]
    out = []
    for c in range(3):
        spread = (low[0][c] + high[0][c]) + (low[1][c] + high[1][c]) + (low[2][c] + high[2][c])
        carried = scaled[0] * diff[0][c] + scaled[1] * diff[1][c] + scaled[2] * diff[2][c]
        out.append(
            (1.0 - 6.0 * FLOW_STEP * VISCOSITY) * centre[c]
            + (FLOW_STEP * VISCOSITY) * spread
            + carried
        )
    return out


def lamb(centre, diff):
    w = [diff[1][2] - diff[2][1], diff[2][0] - diff[0][2], diff[0][1] - diff[1][0]]
    return [
        w[1] * centre[2] - w[2] * centre[1],
        w[2] * centre[0] - w[0] * centre[2],
        w[0] * centre[1] - w[1] * centre[0],
    ]


INNER = slice(2, 10)


def along_z(values, low_edge, high_edge):
    axis = values[0].ndim - 1
    lane = iota(values[0].shape, axis)
    low = [jnp.where(lane == 0, h, roll(v, 1, axis)) for v, h in zip(values, low_edge)]
    high = [jnp.where(lane == 127, h, roll(v, -1, axis)) for v, h in zip(values, high_edge)]
    return low, high


def plane(source, x, edges):
    centre = [source[c, x, INNER, :] for c in range(3)]
    zlow, zhigh = along_z(centre, edges, edges)
    low = [
        [source[c, x - 1, INNER, :] for c in range(3)],
        [source[c, x, 1:9, :] for c in range(3)],
        zlow,
    ]
    high = [
        [source[c, x + 1, INNER, :] for c in range(3)],
        [source[c, x, 3:11, :] for c in range(3)],
        zhigh,
    ]
    return centre, low, high


def add_lamb(sums, parts, x, first):
    i, a = (x // 2) // 4, (x // 2) % 4
    for c in range(3):
        at = first + (c * 4 + a) * 8
        sums[i, at : at + 8, :] = parts[c]


def inner_flow_kernel(wide_ref, middle_ref, sums_ref):
    for y in (1, 10):

        def row(first, at):
            return [wide_ref[c, first : first + 16, at, :] for c in range(3)]

        centre = row(2, y)
        nothing = [0.0] * 3
        zlow, zhigh = along_z(centre, nothing, nothing)
        low = [row(1, y), row(2, y - 1), zlow]
        high = [row(3, y), row(2, y + 1), zhigh]
        new = moved_on(centre, low, high, differences(low, high))
        for c in range(3):
            middle_ref[c, 2:18, y, :] = new[c]
    held = None
    for x in range(1, 19):
        centre, low, high = plane(wide_ref, x, [0.0] * 3)
        diff = differences(low, high)
        new = moved_on(centre, low, high, diff)
        for c in range(3):
            middle_ref[c, x, INNER, :] = new[c]
        if 2 <= x < 18:
            parts = lamb(centre, diff)
            if x % 2 == 0:
                held = parts
            else:
                add_lamb(sums_ref, [p + h for p, h in zip(parts, held)], x - 2, 0)


def flow_kernel(
    wide_ref,
    own_ref,
    zlow_ref,
    zhigh_ref,
    place_ref,
    inner_ref,
    inner_sums_ref,
    state_ref,
    base_ref,
    first_ref,
    second_ref,
    out_ref,
    volume_ref,
    base_out_ref,
    ends,
    halo,
    middle,
    sums,
):
    low = zlow_ref[0:ZV, :].astype(F32)
    high = zhigh_ref[0:ZV, :].astype(F32)
    for c in range(3):
        for j in range(3):
            lane = slice(j * 128, j * 128 + 128)
            at = 2 * (3 * c + j)
            ends[c, 0:2, lane] = low[at : at + 2]
            ends[c, 2:6, lane] = own_ref[c, 0:4, lane]
            ends[c, 6:8, lane] = high[at : at + 2]

    def spread_out(rows, spots, level):
        values = tn(rows, spots)
        for c in range(3):
            for j in range(3):
                at = (3 * c + j) * LANES
                part = values[:, at : at + LANES].reshape(8, 16, LANES)
                halo[level, c, j * 8 : j * 8 + 8] = part

    both = jnp.concatenate([zlow_ref[0:ZV, :], zhigh_ref[0:ZV, :]], axis=0)
    spread_out(both, first_ref[...], 0)
    edge = [ends[c] for c in range(3)]
    edge_low = [
        [roll(e, 16, 1) for e in edge],
        [roll(e, 1, 1) for e in edge],
        [roll(e, 1, 0) for e in edge],
    ]
    edge_high = [
        [roll(e, -16, 1) for e in edge],
        [roll(e, -1, 1) for e in edge],
        [roll(e, -1, 0) for e in edge],
    ]
    new = moved_on(edge, edge_low, edge_high, differences(edge_low, edge_high))
    rows = [new[c][:, j * LANES : j * LANES + LANES] for c in range(3) for j in range(3)]
    rows = jnp.concatenate(rows + [jnp.zeros((8, LANES), F32)], axis=0)
    spread_out(rows.astype(BF), second_ref[...], 1)
    trace, _ = joined(2, zlow_ref[ZV:, :], zhigh_ref[ZV:, :])
    base_out_ref[...] = base_ref[...]
    add_pair(base_out_ref, 2, *boundary_lifts(2, *face_pair(state_ref, 2), trace))

    def sign(dims):
        return jnp.where(iota(dims, len(dims) - 1) == 0, -1.0, 1.0)

    def growth(speed, signs):
        return FLOW_STEP * VISCOSITY - (0.5 * FLOW_STEP) * (signs * speed)

    for y in (1, 10):
        rate = growth(wide_ref[2, 2:18, y, :], sign((16, LANES)))
        for c in range(3):
            middle[c, 2:18, y, :] = inner_ref[c, 2:18, y, :] + rate * halo[0, c, 2:18, y, :]
    held = None
    signs = sign((8, LANES))
    for x in range(1, 19):
        centre = [wide_ref[c, x, INNER, :] for c in range(3)]
        edges = [halo[0, c, x, INNER, :] for c in range(3)]
        rate = growth(centre[2], signs)
        for c in range(3):
            middle[c, x, INNER, :] = inner_ref[c, x, INNER, :] + rate * edges[c]
        if 2 <= x < 18:
            first, second = signs * edges[0], signs * edges[1]
            parts = [
                first * centre[2],
                second * centre[2],
                -(second * centre[1]) - first * centre[0],
            ]
            if x % 2 == 0:
                held = parts
            else:
                i, a = ((x - 2) // 2) // 4, ((x - 2) // 2) % 4
                for c in range(3):
                    at = (c * 4 + a) * 8
                    sums[i, at : at + 8, :] = inner_sums_ref[i, at : at + 8, :] + (
                        parts[c] + held[c]
                    )
    for x in range(2, 18):
        centre, low, high = plane(middle, x, [halo[1, c, x, INNER, :] for c in range(3)])
        diff = differences(low, high)
        new = moved_on(centre, low, high, diff)
        for c in range(3):
            out_ref[c, (x - 2) * 8 : (x - 2) * 8 + 8, :] = new[c]
        parts = lamb(centre, diff)
        if x % 2 == 0:
            held = parts
        else:
            add_lamb(sums, [p + h for p, h in zip(parts, held)], x - 2, 96)
    both = []
    for i in range(2):
        both.append(sums[i, pl.ds(0, 96, stride=2), :] + sums[i, pl.ds(1, 96, stride=2), :])
    pairs = jnp.concatenate(both, axis=1)
    pairs = jnp.concatenate([pairs, jnp.zeros((32, 256), F32)], axis=0)
    high, low = split2(pairs)
    place = place_ref[...]
    volumes = (nt(place, high) + nt(place, low)) * (1.0 / 16.0)
    lane = iota((256, LANES), 1)
    twice = jnp.where(lane < 48, volumes, roll(volumes, 48, 1)).reshape(4, 8, 8, LANES)
    left = iota((8, 8, LANES), 2) < 48
    for y in range(4):
        part = slice(y * 8, y * 8 + 8)
        volume_ref[part, 0:8, :] = volumes[y * 64 : y * 64 + 64].reshape(8, 8, LANES).astype(BF)
        rows = jnp.where(left, twice[(y + 3) % 4], twice[(y + 1) % 4])
        volume_ref[part, 8:16, :] = rows.astype(BF)
        lower = jnp.concatenate([twice[y, 7:8], twice[y, 0:7]], axis=0)
        upper = jnp.concatenate([twice[y, 1:8], twice[y, 0:1]], axis=0)
        volume_ref[part, 16:24, :] = jnp.where(left, lower, upper).astype(BF)


def gather_matrix(targets, second=None, chosen=None):
    row, column = iota((256, LANES), 0), iota((256, LANES), 1)
    slots = jnp.where(column == (row // 8) * 2 + row % 2, 1.0, 0.0).astype(BF)

    def named(line):
        return nt(slots, jnp.broadcast_to(line, (LANES, LANES)).astype(BF))

    cells = named(targets)
    if second is not None:
        cells = jnp.where(chosen, cells, named(second))
    fits = cells == (column % 32).astype(F32)
    return [
        jnp.where(fits & ((row % 8) // 2 == z), 1.0, 0.0).astype(BF) for z in range(4)
    ]


def line(ref, at):
    return ref[0:32, :].astype(F32)[at : at + 1]


def placement(owner_ref):
    owner = jnp.concatenate([owner_ref[...]] * 4, axis=1).astype(F32)
    across = jnp.broadcast_to(owner, (LANES, LANES))
    row, column = iota((32, LANES), 0), iota((32, LANES), 1)
    down = nt(jnp.where(row == column, 1.0, 0.0).astype(BF), across.astype(BF))
    earlier = jnp.where((across[0:32] == down) & (column < row), 1.0, 0.0)
    slots = 2.0 * down + jnp.sum(earlier, axis=1, keepdims=True)
    spread = jnp.where(iota((32, 256), 1) // 8 == iota((32, 256), 0), 1.0, 0.0).astype(BF)
    slots = tn(slots.astype(BF), spread)
    slots = jnp.concatenate([slots, slots], axis=0)
    row, column = iota((256, 256), 0), iota((256, 256), 1)
    wanted = ((row // 8) * 2 + row % 2).astype(F32)
    fits = (slots == wanted) & ((column % 8) // 2 == (row % 8) // 2)
    return jnp.where(fits, 1.0, 0.0).astype(BF)


def near_kernel(state_ref, near_ref, targets_ref, ylow_ref, yhigh_ref, sides_ref, gather_ref):
    sides_ref[...] = near_ref[FACE:, :] + near_lift(1, near_ref[0:FACE, :], *face_pair(state_ref, 1))
    groups = [
        gather_matrix(targets_ref[...]),
        gather_matrix(line(ylow_ref, 18), line(yhigh_ref, 18), cut_of(1, (256, LANES))[1]),
    ]
    for g, parts in enumerate(groups):
        for z in range(4):
            gather_ref[g, :, z * LANES : z * LANES + LANES] = parts[z]


def end_faces(state_ref, near_ref, side_ref, zlow_ref, zhigh_ref, sides_ref):
    trace, base = joined(2, zlow_ref[ZV:, :], zhigh_ref[ZV:, :])
    sides_ref[0:FACE, :] = side_ref[...]
    sides_ref[FACE:, :] = base + near_lift(2, trace, *face_pair(state_ref, 2))
    from_low = zlow_ref[0:ZV, :].astype(F32)[24:32]
    from_high = zhigh_ref[0:ZV, :].astype(F32)[24:32]
    at_low, at_high = cut_of(2, (K, LANES))
    jump = near_ref[pl.ds(0, K, stride=K), :] - roll(from_low, -15, 1)
    sides_ref[pl.ds(0, K, stride=K), :] += jnp.where(at_low, low_lift(2, jump), 0.0)
    jump = near_ref[pl.ds(K - 1, K, stride=K), :] - roll(from_high, 15, 1)
    sides_ref[pl.ds(K - 1, K, stride=K), :] += jnp.where(at_high, high_lift(2, jump), 0.0)
    parts = gather_matrix(line(zlow_ref, 18), line(zhigh_ref, 18), cut_of(2, (256, LANES))[1])
    return jnp.concatenate(parts, axis=1)


def stacked(summed, starts):
    kind = iota((16, LANES), 1) // 32
    blocks = []
    for start in starts:
        rows = []
        for z in range(4):
            total = jnp.zeros((16, LANES), F32)
            for c in range(3):
                total = jnp.where(kind == 1 + c, start(summed, c, z), total)
            rows.append(total)
        blocks.append(jnp.concatenate(rows, axis=0))
    high, low = split2(jnp.concatenate(blocks, axis=1) if len(blocks) > 1 else blocks[0])
    return jnp.concatenate([high, high, low, jnp.zeros_like(low)], axis=0)


def at_rows(first):
    def pick(summed, c, z):
        at = first + c * 16
        return summed[at : at + 16, z * LANES : z * LANES + LANES]

    return pick


def by_side(axis):
    def pick(summed, c, z):
        _, at_high = cut_of(axis, (16, LANES))
        return jnp.where(at_high, at_rows(0)(summed, c, z), at_rows(48)(summed, c, z))

    return pick


def send_kernel(arrived_ref, gather_ref, faces_ref, base_ref, low_ref, high_ref, cells_ref):
    rows = arrived_ref[:, 0:8, :].reshape(256, LANES)
    summed = tn(rows, gather_ref[0])
    cells = stacked(summed, (at_rows(0), at_rows(48)))
    cells_ref[...] = cells
    for side, (out, face) in enumerate(zip((low_ref, high_ref), face_pair(base_ref, 0))):
        out[...] = (face - GAIN * nn(faces_ref[side], cells[:, 0:LANES])).astype(BF)


def second_kernel(
    arrived_ref,
    gather_ref,
    table_ref,
    faces_ref,
    cells_ref,
    base_ref,
    first_ref,
    near_ref,
    side_ref,
    zlow_ref,
    zhigh_ref,
    column_ref,
    back_ref,
    flow_ref,
    out_ref,
    ends_ref,
    flow_out_ref,
    sides_ref,
    state,
    extra,
    total,
    rows_held,
    sems,
):
    flow_copy = pltpu.make_async_copy(flow_ref, flow_out_ref, sems.at[0])
    flow_copy.start()
    end_gather = end_faces(first_ref, near_ref, side_ref, zlow_ref, zhigh_ref, sides_ref)
    source = GAIN * nn(table_ref[...], cells_ref[...])
    state[...] = base_ref[...] - source[:, 0:LANES]
    extra[...] = source[:, LANES:]
    near = []
    for axis in (1, 2):
        rows = arrived_ref[:, 8 * axis : 8 * axis + 8, :].reshape(256, LANES)
        gather = gather_ref[1] if axis == 1 else end_gather
        cells = stacked(tn(rows, gather), (by_side(axis),))
        at_low, at_high = cut_of(axis, (FACE, LANES))
        face = jnp.where(
            at_high,
            nn(faces_ref[2 * axis + 1], cells),
            nn(faces_ref[2 * axis], cells),
        )
        near.append(sides_ref[(axis - 1) * FACE : axis * FACE, :] - GAIN * face)
    volume_part(state, total, column_ref, extra)
    for axis in (1, 2):
        own_low, own_high = face_pair(state, axis)
        low, high = outer(axis, own_low, own_high, near[axis - 1])
        add_pair(total, axis, low_lift(axis, own_low - low), high_lift(axis, own_high - high))
    own_low, own_high = face_pair(state, 0)
    add_pair(total, 0, low_lift(0, own_low), high_lift(0, own_high))
    back = back_ref[...]

    def turned(first, last):
        high, low = split2(jnp.transpose(total[first:last, :]))
        return nn(back, high) + nn(back, low)

    rows = turned(LANES, 3 * LANES)
    for v in range(4):
        rows_held[:, v, :] = rows[v * 32 : v * 32 + 32, :]
    copy = pltpu.make_async_copy(rows_held, out_ref.at[:, :, LANES : 3 * LANES], sems.at[1])
    copy.start()
    ends_ref[0] = turned(0, LANES)
    ends_ref[1] = turned(3 * LANES, ROWS)
    flow_copy.wait()
    copy.wait()


def last_kernel(
    main_ref, ends_ref, back_ref, low_ref, high_ref, out_ref, held, sems
):
    rows = nt(back_ref[...], jnp.concatenate([low_ref[...], high_ref[...]], axis=0))
    across = jnp.concatenate([rows[32:64], rows[0:32], jnp.zeros((64, LANES), F32)], axis=0)
    rows = LIFT * (rows + jnp.where(iota((LANES, LANES), 1) < FACE, across, -across))
    left = iota((LANES, LANES), 1) < FACE
    copies = []
    for side, tile in ((0, 0), (1, 3)):
        total = ends_ref[side] + jnp.where(left if side == 0 else ~left, rows, 0.0)
        for v in range(4):
            held[side, :, v, :] = total[v * 32 : v * 32 + 32, :]
        for part in range(PARTS):
            some = slice(part * 32 // PARTS, (part + 1) * 32 // PARTS)
            copies.append(
                pltpu.make_async_copy(
                    held.at[side, some],
                    out_ref.at[some, :, tile * LANES : tile * LANES + LANES],
                    sems.at[side * PARTS + part],
                )
            )
            copies[-1].start()
    for copy in copies:
        copy.wait()


def both_ways(low, high, axis):
    count = lax.axis_size(axis)
    up = [(i, (i + 1) % count) for i in range(count)]
    down = [(b, a) for a, b in up]
    return lax.ppermute(high, axis, up), lax.ppermute(low, axis, down)


def on_device(velocity, acoustic, projection, owner_index, slot_element, element_cell):
    velocity = velocity.reshape(3, 128, LANES)
    face = shape(FACE, LANES, dtype=BF)
    state = shape(ROWS, LANES)
    column = jnp.asarray(np.broadcast_to(DERIV.T.reshape(FACE, 1), (FACE, LANES)), F32)
    send = shape(XV + FACE, LANES, dtype=BF)
    chosen = shape(LANES, LANES, dtype=BF)
    lines, faces = call(
        load_kernel,
        (shape(2, XV, LANES, dtype=BF), shape(LANES, LANES, dtype=BF)),
        velocity,
        acoustic,
        far_in=(0, 1),
        grant=START_GRANT,
        scratch=[
            pltpu.VMEM((2, 3, 16, LANES), F32),
            pltpu.VMEM((2, 32, 4, LANES), F32),
            pltpu.SemaphoreType.DMA((4,)),
        ],
    )
    chosen = shape(LANES, LANES, dtype=BF)
    xlow, xhigh, chosen = call(start_kernel, (send, send, chosen), lines, faces, element_cell)
    xlow, xhigh = both_ways(xlow, xhigh, "gx")
    first, base, targets = call(
        prepare_kernel,
        (state, state, shape(1, LANES)),
        acoustic,
        chosen,
        element_cell,
        slot_element,
        column,
    )
    send = shape(YV + FACE, LANES, dtype=BF)
    ylow, yhigh, base = call(
        y_kernel,
        (send, send, state),
        velocity,
        xlow,
        xhigh,
        first,
        base,
        targets,
        scratch=[pltpu.VMEM((3, 160, LANES), F32)],
    )
    ylow, yhigh = both_ways(ylow, yhigh, "gy")
    back, table, faces, place, spots, later_spots = call(
        table_kernel,
        (
            shape(LANES, LANES, dtype=BF),
            shape(ROWS, 256, dtype=BF),
            shape(6, FACE, 256, dtype=BF),
            shape(256, 256, dtype=BF),
            shape(2 * ZV, 9 * LANES, dtype=BF),
            shape(80, 9 * LANES, dtype=BF),
        ),
        base,
        chosen,
        projection,
        owner_index.reshape(1, 32),
        far_in=(0,),
        scratch=[pltpu.VMEM((2, ROWS, LANES), F32)],
    )
    send = shape(ZV + FACE, LANES, dtype=BF)
    wide, own, zlow, zhigh, base, near = call(
        z_kernel,
        (shape(3, 20, 16, LANES), shape(3, 8, 384), send, send, state, shape(2 * FACE, LANES)),
        spots,
        velocity,
        xlow,
        xhigh,
        ylow,
        yhigh,
        first,
        base,
        targets,
        far_in=(0,),
        scratch=[pltpu.VMEM((2, YV, LANES), F32)],
    )
    zlow, zhigh = both_ways(zlow, zhigh, "gz")
    middle, sums = call(
        inner_flow_kernel, (shape(3, 20, 16, LANES), shape(2, 96, LANES)), wide
    )
    side, gather = call(
        near_kernel,
        (shape(FACE, LANES), shape(2, 256, 512, dtype=BF)),
        first,
        near,
        targets,
        ylow,
        yhigh,
    )
    flow, volumes, base = call(
        flow_kernel,
        (shape(3, 128, LANES), shape(32, 24, LANES, dtype=BF), state),
        wide,
        own,
        zlow,
        zhigh,
        place,
        middle,
        sums,
        first,
        base,
        spots,
        later_spots,
        scratch=[
            pltpu.VMEM((3, 8, 384), F32),
            pltpu.VMEM((2, 3, 24, 16, LANES), F32),
            pltpu.VMEM((3, 20, 16, LANES), F32),
            pltpu.VMEM((2, 192, LANES), F32),
        ],
    )
    volumes, side, gather = lax.optimization_barrier((volumes, side, gather))
    arrived = lax.all_to_all(volumes, ("gy", "gz"), split_axis=0, concat_axis=0, tiled=True)
    low, high, cells = call(
        send_kernel, (face, face, shape(256, 256, dtype=BF)), arrived, gather, faces, base
    )
    low, high = both_ways(low, high, "gx")
    main, ends, flow = call(
        second_kernel,
        (shape(*acoustic.shape), shape(2, LANES, LANES), shape(3, 128, LANES)),
        arrived,
        gather,
        table,
        faces,
        cells,
        base,
        first,
        near,
        side,
        zlow,
        zhigh,
        column,
        back,
        flow,
        far_out=(0, 2),
        scratch=[pltpu.VMEM((2 * FACE, LANES), F32)]
        + [pltpu.VMEM((ROWS, LANES), F32)] * 3
        + [pltpu.VMEM((32, 4, 2 * LANES), F32), pltpu.SemaphoreType.DMA((2,))],
    )
    out = call(
        last_kernel,
        shape(*acoustic.shape),
        main,
        ends,
        back,
        low,
        high,
        far_in=(0,),
        far_out=(0,),
        alias={0: 0},
        scratch=[pltpu.VMEM((2, 32, 4, LANES), F32), pltpu.SemaphoreType.DMA((2 * PARTS,))],
    )
    return flow.reshape(3, 16, 8, LANES), out


def solution(mesh):
    whole = P(("gx", "gy", "gz"), None, None)
    rows = P(("gx", "gy", "gz"), None)
    flow = P(None, "gx", "gy", "gz")
    return jax.shard_map(
        on_device,
        mesh=mesh,
        in_specs=(flow, whole, P(), rows, rows, rows),
        out_specs=(flow, whole),
        check_vma=False,
    )
```

```python
import jax
import jax.numpy as jnp
import numpy as np
from jax import lax
from jax.experimental import pallas as pl
from jax.experimental.pallas import tpu as pltpu
from jax.sharding import PartitionSpec as P

F32 = jnp.float32
BF = jnp.bfloat16
ORDER = 7
K = ORDER + 1
LANES = 128
ROWS = K**3
FACE = K * K
FLOW_STEP = 0.1
VISCOSITY = 0.05
WAVE_STEP = 0.02
SOURCE_GAIN = 25.0
GAIN = WAVE_STEP * SOURCE_GAIN
LIFT = WAVE_STEP * 0.5 * ORDER * (ORDER + 1) / 2.0
XV = 96
YV = 240
PARTS = 1
START_GRANT = 56_440_000
ZV = 64


def legendre_table(points, order):
    columns = [points * 0.0 + 1.0, points]
    for degree in range(2, order + 1):
        columns.append(
            ((2 * degree - 1) * points * columns[degree - 1] - (degree - 1) * columns[degree - 2])
            / degree
        )
    return np.stack(columns, axis=1)


def lobatto_tables(order):
    point_count = order + 1
    points = -np.cos(np.pi * np.arange(point_count) / order)
    for _ in range(60):
        legendre = legendre_table(points, order)
        points = points - (points * legendre[:, order] - legendre[:, order - 1]) / (
            point_count * legendre[:, order]
        )
    legendre = legendre_table(points, order)
    highest = legendre[:, order]
    spacing = points[:, None] - points[None, :] + np.eye(point_count)
    derivative = highest[:, None] / (highest[None, :] * spacing)
    derivative = derivative * (1.0 - np.eye(point_count))
    derivative[0, 0] = -order * point_count / 4.0
    derivative[order, order] = order * point_count / 4.0
    return derivative


DERIV = lobatto_tables(ORDER) * (-WAVE_STEP)


def split2(value):
    high = value.astype(BF)
    return high, (value - high.astype(F32)).astype(BF)


def restored(ref, rows, first, count):
    high = ref[first : first + count, :].astype(F32)
    return high + ref[rows // 2 + first : rows // 2 + first + count, :].astype(F32)


def nn(a, b):
    return lax.dot_general(a, b, (((1,), (0,)), ((), ())), preferred_element_type=F32)


def nt(a, b):
    return lax.dot_general(a, b, (((1,), (1,)), ((), ())), preferred_element_type=F32)


def tn(a, b):
    return lax.dot_general(a, b, (((0,), (0,)), ((), ())), preferred_element_type=F32)


def iota(shape, axis):
    return lax.broadcasted_iota(jnp.int32, shape, axis)


def roll(value, shift, axis):
    size = value.shape[axis]
    return pltpu.roll(value, shift % size, axis)


def call(
    kernel, out_shape, *args, scratch=(), far_in=(), far_out=(), alias={}, grant=16 * 2**20
):
    near, far = pl.BlockSpec(memory_space=pltpu.VMEM), pl.BlockSpec(memory_space=pl.ANY)
    outs = [far if i in far_out else near for i in range(len(jax.tree.leaves(out_shape)))]
    return pl.pallas_call(
        kernel,
        out_shape=out_shape,
        in_specs=[far if i in far_in else near for i in range(len(args))],
        out_specs=tuple(outs) if isinstance(out_shape, tuple) else outs[0],
        scratch_shapes=list(scratch),
        input_output_aliases=alias,
        compiler_params=pltpu.CompilerParams(vmem_limit_bytes=grant),
        cost_estimate=pl.CostEstimate(flops=10**6, bytes_accessed=10**6, transcendentals=0),
    )(*args)


def shape(*dims, dtype=F32):
    return jax.ShapeDtypeStruct(dims, dtype)


def stored_rows(acoustic_ref):
    return jnp.concatenate([acoustic_ref[:, v, :] for v in range(4)], axis=0)


def cell_matrix(cell_ref):
    cell = jnp.concatenate([cell_ref[...]] * 4, axis=1)
    cell = jnp.broadcast_to(cell, (LANES, LANES))
    row, column = iota((LANES, LANES), 0), iota((LANES, LANES), 1)
    return (cell == row % 32) & (row // 32 == column // 32)


def swapped(value, axis):
    kind = iota(value.shape, value.ndim - 1) // 32
    shift = 32 * (1 + axis)
    last = value.ndim - 1
    return jnp.where(
        kind == 0,
        roll(value, -shift, last),
        jnp.where(kind == 1 + axis, roll(value, shift, last), 0.0),
    )


def low_lift(axis, jump):
    return -LIFT * (swapped(jump, axis) + jump)


def high_lift(axis, jump):
    return LIFT * (swapped(jump, axis) - jump)


def cut_of(axis, dims):
    lane = iota(dims, 1)
    if axis == 1:
        part = (lane // 16) % 2
        return part == 0, part == 1
    part = lane % 16
    return part == 0, part == 15


def outer(axis, own_low, own_high, near):
    at_low, at_high = cut_of(axis, own_low.shape)
    low = jnp.where(at_high, near, own_high)
    high = jnp.where(at_low, near, own_low)
    wrap = 16 if axis == 1 else 15
    step = 16 if axis == 1 else 1
    return (
        jnp.where(at_low, roll(low, -wrap, 1), roll(low, step, 1)),
        jnp.where(at_high, roll(high, wrap, 1), roll(high, -step, 1)),
    )


def facing(axis, own_low, own_high):
    at_low, at_high = cut_of(axis, own_low.shape)
    wrap = 16 if axis == 1 else 15
    return jnp.where(at_high, roll(own_low, wrap, 1), roll(own_high, -wrap, 1))


def near_lift(axis, near, own_low, own_high):
    _, at_high = cut_of(axis, near.shape)
    jump = near - facing(axis, own_low, own_high)
    return jnp.where(at_high, high_lift(axis, jump), low_lift(axis, jump))


def inside_lifts(axis, own_low, own_high):
    at_low, at_high = cut_of(axis, own_low.shape)
    low, high = outer(axis, own_low, own_high, own_low)
    low = jnp.where(at_low, 0.0, own_low - low)
    high = jnp.where(at_high, 0.0, own_high - high)
    return low_lift(axis, low), high_lift(axis, high)


def boundary_lifts(axis, own_low, own_high, near):
    at_low, at_high = cut_of(axis, own_low.shape)
    low, high = outer(axis, own_low, own_high, near)
    low = jnp.where(at_low, own_low - low, 0.0)
    high = jnp.where(at_high, own_high - high, 0.0)
    return low_lift(axis, low), high_lift(axis, high)


def face_pair(ref, axis):
    if axis == 0:
        return ref[0:FACE, :], ref[ROWS - FACE : ROWS, :]
    if axis == 1:
        low = [ref[a * FACE : a * FACE + K, :] for a in range(K)]
        high = [ref[a * FACE + FACE - K : a * FACE + FACE, :] for a in range(K)]
        return jnp.concatenate(low, axis=0), jnp.concatenate(high, axis=0)
    return ref[pl.ds(0, FACE, stride=K), :], ref[pl.ds(K - 1, FACE, stride=K), :]


def add_pair(ref, axis, low, high):
    if axis == 0:
        ref[0:FACE, :] += low
        ref[ROWS - FACE : ROWS, :] += high
    elif axis == 1:
        for a in range(K):
            ref[a * FACE : a * FACE + K, :] += low[a * K : a * K + K]
            ref[a * FACE + FACE - K : a * FACE + FACE, :] += high[a * K : a * K + K]
    else:
        ref[pl.ds(0, FACE, stride=K), :] += low
        ref[pl.ds(K - 1, FACE, stride=K), :] += high


def derivative_columns():
    row = iota((K, LANES), 0)
    columns = []
    for m in range(K):
        column = jnp.zeros((K, LANES), F32)
        for b in range(K):
            column = jnp.where(row == b, float(DERIV[b, m]), column)
        columns.append(column)
    return columns


def volume_part(state_ref, out_ref, extra_ref=None):
    columns = derivative_columns()
    for a in range(K):
        rows = [state_ref[a * FACE + b * K : a * FACE + b * K + K, :] for b in range(K)]
        along_y = [swapped(r, 1) for r in rows]
        along_z = [swapped(r, 2) for r in rows]
        for b in range(K):
            total = rows[b]
            at = a * FACE + b * K
            if extra_ref is not None:
                total = total - extra_ref[at : at + K, :]
            for m in range(K):
                total = total + float(DERIV[b, m]) * along_y[m]
            for m in range(K):
                total = total + columns[m] * jnp.broadcast_to(
                    along_z[b][m : m + 1, :], (K, LANES)
                )
            out_ref[at : at + K, :] = total
    for b in range(K):
        rows = [
            swapped(state_ref[a * FACE + b * K : a * FACE + b * K + K, :], 0) for a in range(K)
        ]
        for a in range(K):
            at = a * FACE + b * K
            total = out_ref[at : at + K, :]
            for m in range(K):
                total = total + float(DERIV[a, m]) * rows[m]
            out_ref[at : at + K, :] = total


def load_kernel(velocity_ref, acoustic_ref, lines_ref, faces_ref, flow, wave, sems):
    copies = []
    for side, tile in ((0, 0), (1, 3)):
        copies.append((acoustic_ref.at[:, :, tile * LANES : tile * LANES + LANES], wave.at[side]))
    for side, first in ((0, 0), (1, 112)):
        copies.append((velocity_ref.at[:, first : first + 16, :], flow.at[side]))
    copies = [pltpu.make_async_copy(a, b, sems.at[i]) for i, (a, b) in enumerate(copies)]
    for copy in copies:
        copy.start()
    for copy in copies:
        copy.wait()
    left = iota((32, LANES), 1) < FACE
    for v in range(4):
        rows = jnp.where(left, wave[0, :, v, :], wave[1, :, v, :])
        faces_ref[v * 32 : v * 32 + 32, :] = rows.astype(BF)
    for side in range(2):
        for c in range(3):
            high, low = split2(flow[side, c])
            lines_ref[side, c * 16 : c * 16 + 16, :] = high
            lines_ref[side, XV // 2 + c * 16 : XV // 2 + c * 16 + 16, :] = low


def start_kernel(lines_ref, faces_ref, cell_ref, low_ref, high_ref, place_ref):
    place = jnp.where(cell_matrix(cell_ref), 1.0, 0.0).astype(BF)
    turned = jnp.transpose(nn(place, faces_ref[...])).astype(BF)
    low_ref[XV:, :] = turned[:FACE]
    high_ref[XV:, :] = turned[FACE:]
    low_ref[0:XV, :] = lines_ref[0]
    high_ref[0:XV, :] = lines_ref[1]
    place_ref[...] = place


def prepare_kernel(
    acoustic_ref,
    place_ref,
    cell_ref,
    slot_ref,
    state_ref,
    base_ref,
    targets_ref,
):
    slots = jnp.broadcast_to(jnp.concatenate([slot_ref[...]] * 2, axis=1), (32, LANES))
    named = jnp.where(slots == iota((32, LANES), 0), 1.0, 0.0).astype(BF)
    cells = jnp.broadcast_to(cell_ref[...], (16, 32)).astype(F32).astype(BF)
    targets_ref[...] = nn(cells, named)[0:1]
    place = place_ref[...]
    high, low = split2(stored_rows(acoustic_ref))
    state_ref[...] = jnp.transpose(nn(place, high) + nn(place, low))
    volume_part(state_ref, base_ref)
    for axis in (1, 2):
        add_pair(base_ref, axis, *inside_lifts(axis, *face_pair(state_ref, axis)))


def chunk_matrix(out_ref, held, low_rows, high_rows):
    rows = out_ref.shape[0]
    held[0:rows, :] = jnp.zeros((rows, 9 * LANES), F32)
    lane = iota((1, LANES), 1)
    for places, at in ((low_rows, 0), (high_rows, LANES - 1)):
        spot = jnp.where(lane == at, 1.0, 0.0)
        for m in range(9):
            for row in places(m):
                held[row : row + 1, m * LANES : m * LANES + LANES] = spot
    out_ref[...] = held[0:rows, :].astype(BF)


def table_kernel(
    order_ref,
    chosen_ref,
    projection_ref,
    owner_ref,
    back_ref,
    table_ref,
    faces_ref,
    place_ref,
    first_ref,
    second_ref,
    scratch,
    held,
):
    del order_ref
    back_ref[...] = jnp.transpose(chosen_ref[...].astype(F32)).astype(BF)
    place_ref[...] = placement(owner_ref)
    half = ZV // 2
    chunk_matrix(
        first_ref,
        held,
        lambda m: (2 * m + 1, half + 2 * m + 1),
        lambda m: (ZV + 2 * m, ZV + half + 2 * m),
    )
    chunk_matrix(
        second_ref,
        held,
        lambda m: (8 * m + 1, 80 + 8 * m + 1),
        lambda m: (8 * m + 6, 80 + 8 * m + 6),
    )
    high, low = split2(projection_ref[...])
    row, column = iota((64, 64), 0), iota((64, 64), 1)
    order = jnp.where(column == (row % 16) * 4 + row // 16, 1.0, 0.0).astype(BF)
    high, low = nn(order, high), nn(order, low)
    whole = jnp.concatenate([high, low, high, jnp.zeros((64, ROWS), F32)], axis=0)
    scratch[0] = jnp.transpose(whole[0:LANES])
    scratch[1] = jnp.transpose(whole[LANES:])
    for i in range(2):
        lane = slice(i * LANES, i * LANES + LANES)
        table_ref[:, lane] = scratch[i].astype(BF)
        for axis in range(3):
            for side, face in enumerate(face_pair(scratch.at[i], axis)):
                faces_ref[2 * axis + side, :, lane] = face.astype(BF)


def y_kernel(
    velocity_ref,
    xlow_ref,
    xhigh_ref,
    state_ref,
    base_ref,
    targets_ref,
    low_ref,
    high_ref,
    out_ref,
    wide,
):
    for c in range(3):
        wide[c, 0:16, :] = restored(xlow_ref, XV, c * 16, 16)
        wide[c, 16:144, :] = velocity_ref[c]
        wide[c, 144:160, :] = restored(xhigh_ref, XV, c * 16, 16)
    own_low, own_high = face_pair(state_ref, 0)
    out_ref[...] = base_ref[...]
    add_pair(
        out_ref,
        0,
        low_lift(0, own_low - xlow_ref[XV:, :].astype(F32)),
        high_lift(0, own_high - xhigh_ref[XV:, :].astype(F32)),
    )
    faces = packed(1, face_pair(state_ref, 1), face_pair(out_ref, 1))
    spare = jnp.concatenate([targets_ref[...], jnp.zeros((5, LANES), F32)], axis=0)
    for side, (out, near, far) in enumerate(((low_ref, 0, 1), (high_ref, 7, 6))):
        pieces = []
        for c in range(3):
            pieces.append(wide[c, pl.ds(8 + near, 18, stride=8), :])
            pieces.append(spare)
            pieces.append(wide[c, pl.ds(16 + far, 16, stride=8), :])
        high, low = split2(jnp.concatenate(pieces, axis=0))
        out[0 : YV // 2, :] = high
        out[YV // 2 : YV, :] = low
        out[YV:, :] = faces[side]


def packed(axis, traces, bases):
    at_low, at_high = cut_of(axis, traces[0].shape)
    step = 16 if axis == 1 else 1
    return (
        jnp.where(at_low, traces[0], roll(bases[0], step, 1)).astype(BF),
        jnp.where(at_high, traces[1], roll(bases[1], -step, 1)).astype(BF),
    )


def joined(axis, low, high):
    _, at_high = cut_of(axis, low.shape)
    low, high = low.astype(F32), high.astype(F32)
    step = 16 if axis == 1 else 1
    return (
        jnp.where(at_high, low, high),
        jnp.where(at_high, roll(low, step, 1), roll(high, -step, 1)),
    )


def z_kernel(
    order_ref,
    velocity_ref,
    xlow_ref,
    xhigh_ref,
    ylow_ref,
    yhigh_ref,
    state_ref,
    base_ref,
    targets_ref,
    wide_ref,
    own_ref,
    low_ref,
    high_ref,
    out_ref,
    near_ref,
    held,
):
    del order_ref
    held[0] = restored(ylow_ref, YV, 0, YV // 2)
    held[1] = restored(yhigh_ref, YV, 0, YV // 2)
    for c in range(3):
        low = restored(xlow_ref, XV, c * 16, 16)
        high = restored(xhigh_ref, XV, c * 16, 16)
        for x in range(2):
            wide_ref[c, x, 2:10, :] = low[x * 8 : x * 8 + 8]
            wide_ref[c, 18 + x, 2:10, :] = high[x * 8 : x * 8 + 8]
        for x in range(16):
            wide_ref[c, 2 + x, 2:10, :] = velocity_ref[c, x * 8 : x * 8 + 8, :]
        for x in (0, 1, 18, 19):
            wide_ref[c, x, 0:2, :] = jnp.zeros((2, LANES), F32)
            wide_ref[c, x, 10:12, :] = jnp.zeros((2, LANES), F32)
        for side in range(2):
            at = c * 40
            wide_ref[c, 1:19, 1 + 9 * side, :] = held[side, at : at + 18, :]
            wide_ref[c, 2:18, 11 * side, :] = held[side, at + 24 : at + 40, :]
        wide_ref[c, :, 12:16, :] = jnp.zeros((20, 4, LANES), F32)
    row, column = iota((16, LANES), 0), iota((16, LANES), 1)
    picks = ((row < 2) & (column == row)) | ((row >= 2) & (row < 4) & (column == row + 124))
    picks = jnp.where(picks, 1.0, 0.0).astype(BF)
    for c in range(3):
        high, low = split2(wide_ref[c].reshape(320, LANES))
        own = nt(picks, high) + nt(picks, low)
        own_ref[c, :, 0:320] = own[0:8]
        own_ref[c, :, 320:384] = jnp.zeros((8, 64), F32)
    trace, base = joined(1, ylow_ref[YV:, :], yhigh_ref[YV:, :])
    near_ref[0:FACE, :] = trace
    near_ref[FACE:, :] = base
    out_ref[...] = base_ref[...]
    add_pair(out_ref, 1, *boundary_lifts(1, *face_pair(state_ref, 1), near_ref[0:FACE, :]))
    faces = packed(2, face_pair(state_ref, 2), face_pair(out_ref, 2))
    for side, (out, first) in enumerate(((low_ref, 0), (high_ref, 2))):
        pieces = []
        for c in range(3):
            for j in range(3):
                pieces.append(own_ref[c, first : first + 2, j * 128 : j * 128 + 128])
        pieces += [targets_ref[...], jnp.zeros((5, LANES), F32)]
        pieces.append(near_ref[pl.ds(side * (K - 1), K, stride=K), :])
        high, low = split2(jnp.concatenate(pieces, axis=0))
        out[0 : ZV // 2, :] = high
        out[ZV // 2 : ZV, :] = low
        out[ZV:, :] = faces[side]


def differences(low, high):
    return [[high[a][c] - low[a][c] for c in range(3)] for a in range(3)]


def moved_on(centre, low, high, diff):
    scaled = [(-0.5 * FLOW_STEP) * centre[a] for a in range(3)]
    out = []
    for c in range(3):
        spread = (low[0][c] + high[0][c]) + (low[1][c] + high[1][c]) + (low[2][c] + high[2][c])
        carried = scaled[0] * diff[0][c] + scaled[1] * diff[1][c] + scaled[2] * diff[2][c]
        out.append(
            (1.0 - 6.0 * FLOW_STEP * VISCOSITY) * centre[c]
            + (FLOW_STEP * VISCOSITY) * spread
            + carried
        )
    return out


def lamb(centre, diff):
    w = [diff[1][2] - diff[2][1], diff[2][0] - diff[0][2], diff[0][1] - diff[1][0]]
    return [
        w[1] * centre[2] - w[2] * centre[1],
        w[2] * centre[0] - w[0] * centre[2],
        w[0] * centre[1] - w[1] * centre[0],
    ]


INNER = slice(2, 10)


def along_z(values, low_edge, high_edge):
    axis = values[0].ndim - 1
    lane = iota(values[0].shape, axis)
    low = [jnp.where(lane == 0, h, roll(v, 1, axis)) for v, h in zip(values, low_edge)]
    high = [jnp.where(lane == 127, h, roll(v, -1, axis)) for v, h in zip(values, high_edge)]
    return low, high


def plane(source, x, edges):
    centre = [source[c, x, INNER, :] for c in range(3)]
    zlow, zhigh = along_z(centre, edges, edges)
    low = [
        [source[c, x - 1, INNER, :] for c in range(3)],
        [source[c, x, 1:9, :] for c in range(3)],
        zlow,
    ]
    high = [
        [source[c, x + 1, INNER, :] for c in range(3)],
        [source[c, x, 3:11, :] for c in range(3)],
        zhigh,
    ]
    return centre, low, high


def add_lamb(sums, parts, x, first):
    i, a = (x // 2) // 4, (x // 2) % 4
    for c in range(3):
        at = first + (c * 4 + a) * 8
        sums[i, at : at + 8, :] = parts[c]


def inner_flow_kernel(wide_ref, middle_ref, sums_ref):
    for y in (1, 10):

        def row(first, at):
            return [wide_ref[c, first : first + 16, at, :] for c in range(3)]

        centre = row(2, y)
        nothing = [0.0] * 3
        zlow, zhigh = along_z(centre, nothing, nothing)
        low = [row(1, y), row(2, y - 1), zlow]
        high = [row(3, y), row(2, y + 1), zhigh]
        new = moved_on(centre, low, high, differences(low, high))
        for c in range(3):
            middle_ref[c, 2:18, y, :] = new[c]
    held = None
    for x in range(1, 19):
        centre, low, high = plane(wide_ref, x, [0.0] * 3)
        diff = differences(low, high)
        new = moved_on(centre, low, high, diff)
        for c in range(3):
            middle_ref[c, x, INNER, :] = new[c]
        if 2 <= x < 18:
            parts = lamb(centre, diff)
            if x % 2 == 0:
                held = parts
            else:
                add_lamb(sums_ref, [p + h for p, h in zip(parts, held)], x - 2, 0)


def flow_kernel(
    wide_ref,
    own_ref,
    zlow_ref,
    zhigh_ref,
    place_ref,
    inner_ref,
    inner_sums_ref,
    state_ref,
    base_ref,
    first_ref,
    second_ref,
    out_ref,
    volume_ref,
    base_out_ref,
    ends,
    halo,
    middle,
    sums,
):
    low = restored(zlow_ref, ZV, 0, ZV // 2)
    high = restored(zhigh_ref, ZV, 0, ZV // 2)
    for c in range(3):
        for j in range(3):
            lane = slice(j * 128, j * 128 + 128)
            at = 2 * (3 * c + j)
            ends[c, 0:2, lane] = low[at : at + 2]
            ends[c, 2:6, lane] = own_ref[c, 0:4, lane]
            ends[c, 6:8, lane] = high[at : at + 2]

    def spread_out(rows, spots, level):
        values = tn(rows, spots)
        for c in range(3):
            for j in range(3):
                at = (3 * c + j) * LANES
                part = values[:, at : at + LANES].reshape(8, 16, LANES)
                halo[level, c, j * 8 : j * 8 + 8] = part

    both = jnp.concatenate([zlow_ref[0:ZV, :], zhigh_ref[0:ZV, :]], axis=0)
    spread_out(both, first_ref[...], 0)
    edge = [ends[c] for c in range(3)]
    edge_low = [
        [roll(e, 16, 1) for e in edge],
        [roll(e, 1, 1) for e in edge],
        [roll(e, 1, 0) for e in edge],
    ]
    edge_high = [
        [roll(e, -16, 1) for e in edge],
        [roll(e, -1, 1) for e in edge],
        [roll(e, -1, 0) for e in edge],
    ]
    new = moved_on(edge, edge_low, edge_high, differences(edge_low, edge_high))
    rows = [new[c][:, j * LANES : j * LANES + LANES] for c in range(3) for j in range(3)]
    rows = jnp.concatenate(rows + [jnp.zeros((8, LANES), F32)], axis=0)
    spread_out(jnp.concatenate(split2(rows), axis=0), second_ref[...], 1)
    trace, _ = joined(2, zlow_ref[ZV:, :], zhigh_ref[ZV:, :])
    base_out_ref[...] = base_ref[...]
    add_pair(base_out_ref, 2, *boundary_lifts(2, *face_pair(state_ref, 2), trace))

    def sign(dims):
        return jnp.where(iota(dims, len(dims) - 1) == 0, -1.0, 1.0)

    def growth(speed, signs):
        return FLOW_STEP * VISCOSITY - (0.5 * FLOW_STEP) * (signs * speed)

    for y in (1, 10):
        rate = growth(wide_ref[2, 2:18, y, :], sign((16, LANES)))
        for c in range(3):
            middle[c, 2:18, y, :] = inner_ref[c, 2:18, y, :] + rate * halo[0, c, 2:18, y, :]
    held = None
    signs = sign((8, LANES))
    for x in range(1, 19):
        centre = [wide_ref[c, x, INNER, :] for c in range(3)]
        edges = [halo[0, c, x, INNER, :] for c in range(3)]
        rate = growth(centre[2], signs)
        for c in range(3):
            middle[c, x, INNER, :] = inner_ref[c, x, INNER, :] + rate * edges[c]
        if 2 <= x < 18:
            first, second = signs * edges[0], signs * edges[1]
            parts = [
                first * centre[2],
                second * centre[2],
                -(second * centre[1]) - first * centre[0],
            ]
            if x % 2 == 0:
                held = parts
            else:
                i, a = ((x - 2) // 2) // 4, ((x - 2) // 2) % 4
                for c in range(3):
                    at = (c * 4 + a) * 8
                    sums[i, at : at + 8, :] = inner_sums_ref[i, at : at + 8, :] + (
                        parts[c] + held[c]
                    )
    for x in range(2, 18):
        centre, low, high = plane(middle, x, [halo[1, c, x, INNER, :] for c in range(3)])
        diff = differences(low, high)
        new = moved_on(centre, low, high, diff)
        for c in range(3):
            out_ref[c, (x - 2) * 8 : (x - 2) * 8 + 8, :] = new[c]
        parts = lamb(centre, diff)
        if x % 2 == 0:
            held = parts
        else:
            add_lamb(sums, [p + h for p, h in zip(parts, held)], x - 2, 96)
    both = []
    for i in range(2):
        both.append(sums[i, pl.ds(0, 96, stride=2), :] + sums[i, pl.ds(1, 96, stride=2), :])
    pairs = jnp.concatenate(both, axis=1)
    pairs = jnp.concatenate([pairs, jnp.zeros((32, 256), F32)], axis=0)
    high, low = split2(pairs)
    place = place_ref[...]
    volumes = (nt(place, high) + nt(place, low)) * (1.0 / 16.0)
    lane = iota((256, LANES), 1)
    twice = jnp.where(lane < 48, volumes, roll(volumes, 48, 1)).reshape(4, 8, 8, LANES)
    left = iota((8, 8, LANES), 2) < 48
    for y in range(4):
        part = slice(y * 8, y * 8 + 8)
        volume_ref[part, 0:8, :] = volumes[y * 64 : y * 64 + 64].reshape(8, 8, LANES).astype(BF)
        rows = jnp.where(left, twice[(y + 3) % 4], twice[(y + 1) % 4])
        volume_ref[part, 8:16, :] = rows.astype(BF)
        lower = jnp.concatenate([twice[y, 7:8], twice[y, 0:7]], axis=0)
        upper = jnp.concatenate([twice[y, 1:8], twice[y, 0:1]], axis=0)
        volume_ref[part, 16:24, :] = jnp.where(left, lower, upper).astype(BF)


def gather_matrix(targets, second=None, chosen=None):
    row, column = iota((256, LANES), 0), iota((256, LANES), 1)
    slots = jnp.where(column == (row // 8) * 2 + row % 2, 1.0, 0.0).astype(BF)

    def named(line):
        return nt(slots, jnp.broadcast_to(line, (LANES, LANES)).astype(BF))

    cells = named(targets)
    if second is not None:
        cells = jnp.where(chosen, cells, named(second))
    fits = cells == (column % 32).astype(F32)
    return [
        jnp.where(fits & ((row % 8) // 2 == z), 1.0, 0.0).astype(BF) for z in range(4)
    ]


def line(ref, at):
    return ref[0:32, :].astype(F32)[at : at + 1]


def placement(owner_ref):
    owner = jnp.concatenate([owner_ref[...]] * 4, axis=1).astype(F32)
    across = jnp.broadcast_to(owner, (LANES, LANES))
    row, column = iota((32, LANES), 0), iota((32, LANES), 1)
    down = nt(jnp.where(row == column, 1.0, 0.0).astype(BF), across.astype(BF))
    earlier = jnp.where((across[0:32] == down) & (column < row), 1.0, 0.0)
    slots = 2.0 * down + jnp.sum(earlier, axis=1, keepdims=True)
    spread = jnp.where(iota((32, 256), 1) // 8 == iota((32, 256), 0), 1.0, 0.0).astype(BF)
    slots = tn(slots.astype(BF), spread)
    slots = jnp.concatenate([slots, slots], axis=0)
    row, column = iota((256, 256), 0), iota((256, 256), 1)
    wanted = ((row // 8) * 2 + row % 2).astype(F32)
    fits = (slots == wanted) & ((column % 8) // 2 == (row % 8) // 2)
    return jnp.where(fits, 1.0, 0.0).astype(BF)


def near_kernel(state_ref, near_ref, targets_ref, ylow_ref, yhigh_ref, sides_ref, gather_ref):
    sides_ref[...] = near_ref[FACE:, :] + near_lift(1, near_ref[0:FACE, :], *face_pair(state_ref, 1))
    groups = [
        gather_matrix(targets_ref[...]),
        gather_matrix(line(ylow_ref, 18), line(yhigh_ref, 18), cut_of(1, (256, LANES))[1]),
    ]
    for g, parts in enumerate(groups):
        for z in range(4):
            gather_ref[g, :, z * LANES : z * LANES + LANES] = parts[z]


def end_faces(state_ref, near_ref, side_ref, zlow_ref, zhigh_ref, sides_ref):
    trace, base = joined(2, zlow_ref[ZV:, :], zhigh_ref[ZV:, :])
    sides_ref[0:FACE, :] = side_ref[...]
    sides_ref[FACE:, :] = base + near_lift(2, trace, *face_pair(state_ref, 2))
    from_low = zlow_ref[0:32, :].astype(F32)[24:32]
    from_high = zhigh_ref[0:32, :].astype(F32)[24:32]
    at_low, at_high = cut_of(2, (K, LANES))
    jump = near_ref[pl.ds(0, K, stride=K), :] - roll(from_low, -15, 1)
    sides_ref[pl.ds(0, K, stride=K), :] += jnp.where(at_low, low_lift(2, jump), 0.0)
    jump = near_ref[pl.ds(K - 1, K, stride=K), :] - roll(from_high, 15, 1)
    sides_ref[pl.ds(K - 1, K, stride=K), :] += jnp.where(at_high, high_lift(2, jump), 0.0)
    parts = gather_matrix(line(zlow_ref, 18), line(zhigh_ref, 18), cut_of(2, (256, LANES))[1])
    return jnp.concatenate(parts, axis=1)


def stacked(summed, starts):
    kind = iota((16, LANES), 1) // 32
    blocks = []
    for start in starts:
        rows = []
        for z in range(4):
            total = jnp.zeros((16, LANES), F32)
            for c in range(3):
                total = jnp.where(kind == 1 + c, start(summed, c, z), total)
            rows.append(total)
        blocks.append(jnp.concatenate(rows, axis=0))
    high, low = split2(jnp.concatenate(blocks, axis=1) if len(blocks) > 1 else blocks[0])
    return jnp.concatenate([high, high, low, jnp.zeros_like(low)], axis=0)


def at_rows(first):
    def pick(summed, c, z):
        at = first + c * 16
        return summed[at : at + 16, z * LANES : z * LANES + LANES]

    return pick


def by_side(axis):
    def pick(summed, c, z):
        _, at_high = cut_of(axis, (16, LANES))
        return jnp.where(at_high, at_rows(0)(summed, c, z), at_rows(48)(summed, c, z))

    return pick


def send_kernel(arrived_ref, gather_ref, faces_ref, base_ref, low_ref, high_ref, cells_ref):
    rows = arrived_ref[:, 0:8, :].reshape(256, LANES)
    summed = tn(rows, gather_ref[0])
    cells = stacked(summed, (at_rows(0), at_rows(48)))
    cells_ref[...] = cells
    for side, (out, face) in enumerate(zip((low_ref, high_ref), face_pair(base_ref, 0))):
        out[...] = (face - GAIN * nn(faces_ref[side], cells[:, 0:LANES])).astype(BF)


def second_kernel(
    arrived_ref,
    gather_ref,
    table_ref,
    faces_ref,
    cells_ref,
    base_ref,
    first_ref,
    near_ref,
    side_ref,
    zlow_ref,
    zhigh_ref,
    back_ref,
    flow_ref,
    out_ref,
    ends_ref,
    flow_out_ref,
    sides_ref,
    state,
    extra,
    total,
    rows_held,
    sems,
):
    flow_copy = pltpu.make_async_copy(flow_ref, flow_out_ref, sems.at[0])
    flow_copy.start()
    end_gather = end_faces(first_ref, near_ref, side_ref, zlow_ref, zhigh_ref, sides_ref)
    source = GAIN * nn(table_ref[...], cells_ref[...])
    state[...] = base_ref[...] - source[:, 0:LANES]
    extra[...] = source[:, LANES:]
    near = []
    for axis in (1, 2):
        rows = arrived_ref[:, 8 * axis : 8 * axis + 8, :].reshape(256, LANES)
        gather = gather_ref[1] if axis == 1 else end_gather
        cells = stacked(tn(rows, gather), (by_side(axis),))
        at_low, at_high = cut_of(axis, (FACE, LANES))
        face = jnp.where(
            at_high,
            nn(faces_ref[2 * axis + 1], cells),
            nn(faces_ref[2 * axis], cells),
        )
        near.append(sides_ref[(axis - 1) * FACE : axis * FACE, :] - GAIN * face)
    volume_part(state, total, extra)
    for axis in (1, 2):
        own_low, own_high = face_pair(state, axis)
        low, high = outer(axis, own_low, own_high, near[axis - 1])
        add_pair(total, axis, low_lift(axis, own_low - low), high_lift(axis, own_high - high))
    own_low, own_high = face_pair(state, 0)
    add_pair(total, 0, low_lift(0, own_low), high_lift(0, own_high))
    back = back_ref[...]

    def turned(first, last):
        high, low = split2(jnp.transpose(total[first:last, :]))
        return nn(back, high) + nn(back, low)

    rows = turned(LANES, 3 * LANES)
    for v in range(4):
        rows_held[:, v, :] = rows[v * 32 : v * 32 + 32, :]
    copy = pltpu.make_async_copy(rows_held, out_ref.at[:, :, LANES : 3 * LANES], sems.at[1])
    copy.start()
    ends_ref[0] = turned(0, LANES)
    ends_ref[1] = turned(3 * LANES, ROWS)
    flow_copy.wait()
    copy.wait()


def last_kernel(
    main_ref, ends_ref, back_ref, low_ref, high_ref, out_ref, held, sems
):
    rows = nt(back_ref[...], jnp.concatenate([low_ref[...], high_ref[...]], axis=0))
    across = jnp.concatenate([rows[32:64], rows[0:32], jnp.zeros((64, LANES), F32)], axis=0)
    rows = LIFT * (rows + jnp.where(iota((LANES, LANES), 1) < FACE, across, -across))
    left = iota((LANES, LANES), 1) < FACE
    copies = []
    for side, tile in ((0, 0), (1, 3)):
        total = ends_ref[side] + jnp.where(left if side == 0 else ~left, rows, 0.0)
        for v in range(4):
            held[side, :, v, :] = total[v * 32 : v * 32 + 32, :]
        for part in range(PARTS):
            some = slice(part * 32 // PARTS, (part + 1) * 32 // PARTS)
            copies.append(
                pltpu.make_async_copy(
                    held.at[side, some],
                    out_ref.at[some, :, tile * LANES : tile * LANES + LANES],
                    sems.at[side * PARTS + part],
                )
            )
            copies[-1].start()
    for copy in copies:
        copy.wait()


def both_ways(low, high, axis):
    count = lax.axis_size(axis)
    up = [(i, (i + 1) % count) for i in range(count)]
    down = [(b, a) for a, b in up]
    return lax.ppermute(high, axis, up), lax.ppermute(low, axis, down)


def on_device(velocity, acoustic, projection, owner_index, slot_element, element_cell):
    velocity = velocity.reshape(3, 128, LANES)
    face = shape(FACE, LANES, dtype=BF)
    state = shape(ROWS, LANES)
    send = shape(XV + FACE, LANES, dtype=BF)
    chosen = shape(LANES, LANES, dtype=BF)
    lines, faces = call(
        load_kernel,
        (shape(2, XV, LANES, dtype=BF), shape(LANES, LANES, dtype=BF)),
        velocity,
        acoustic,
        far_in=(0, 1),
        grant=START_GRANT,
        scratch=[
            pltpu.VMEM((2, 3, 16, LANES), F32),
            pltpu.VMEM((2, 32, 4, LANES), F32),
            pltpu.SemaphoreType.DMA((4,)),
        ],
    )
    chosen = shape(LANES, LANES, dtype=BF)
    xlow, xhigh, chosen = call(start_kernel, (send, send, chosen), lines, faces, element_cell)
    xlow, xhigh = both_ways(xlow, xhigh, "gx")
    first, base, targets = call(
        prepare_kernel,
        (state, state, shape(1, LANES)),
        acoustic,
        chosen,
        element_cell,
        slot_element,
    )
    send = shape(YV + FACE, LANES, dtype=BF)
    ylow, yhigh, base = call(
        y_kernel,
        (send, send, state),
        velocity,
        xlow,
        xhigh,
        first,
        base,
        targets,
        scratch=[pltpu.VMEM((3, 160, LANES), F32)],
    )
    ylow, yhigh = both_ways(ylow, yhigh, "gy")
    back, table, faces, place, spots, later_spots = call(
        table_kernel,
        (
            shape(LANES, LANES, dtype=BF),
            shape(ROWS, 256, dtype=BF),
            shape(6, FACE, 256, dtype=BF),
            shape(256, 256, dtype=BF),
            shape(2 * ZV, 9 * LANES, dtype=BF),
            shape(160, 9 * LANES, dtype=BF),
        ),
        base,
        chosen,
        projection,
        owner_index.reshape(1, 32),
        far_in=(0,),
        scratch=[pltpu.VMEM((2, ROWS, LANES), F32), pltpu.VMEM((160, 9 * LANES), F32)],
    )
    send = shape(ZV + FACE, LANES, dtype=BF)
    wide, own, zlow, zhigh, base, near = call(
        z_kernel,
        (shape(3, 20, 16, LANES), shape(3, 8, 384), send, send, state, shape(2 * FACE, LANES)),
        spots,
        velocity,
        xlow,
        xhigh,
        ylow,
        yhigh,
        first,
        base,
        targets,
        far_in=(0,),
        scratch=[pltpu.VMEM((2, YV // 2, LANES), F32)],
    )
    zlow, zhigh = both_ways(zlow, zhigh, "gz")
    middle, sums = call(
        inner_flow_kernel, (shape(3, 20, 16, LANES), shape(2, 96, LANES)), wide
    )
    side, gather = call(
        near_kernel,
        (shape(FACE, LANES), shape(2, 256, 512, dtype=BF)),
        first,
        near,
        targets,
        ylow,
        yhigh,
    )
    flow, volumes, base = call(
        flow_kernel,
        (shape(3, 128, LANES), shape(32, 24, LANES, dtype=BF), state),
        wide,
        own,
        zlow,
        zhigh,
        place,
        middle,
        sums,
        first,
        base,
        spots,
        later_spots,
        scratch=[
            pltpu.VMEM((3, 8, 384), F32),
            pltpu.VMEM((2, 3, 24, 16, LANES), F32),
            pltpu.VMEM((3, 20, 16, LANES), F32),
            pltpu.VMEM((2, 192, LANES), F32),
        ],
    )
    volumes, side, gather = lax.optimization_barrier((volumes, side, gather))
    arrived = lax.all_to_all(volumes, ("gy", "gz"), split_axis=0, concat_axis=0, tiled=True)
    low, high, cells = call(
        send_kernel, (face, face, shape(256, 256, dtype=BF)), arrived, gather, faces, base
    )
    low, high = both_ways(low, high, "gx")
    main, ends, flow = call(
        second_kernel,
        (shape(*acoustic.shape), shape(2, LANES, LANES), shape(3, 128, LANES)),
        arrived,
        gather,
        table,
        faces,
        cells,
        base,
        first,
        near,
        side,
        zlow,
        zhigh,
        back,
        flow,
        far_out=(0, 2),
        scratch=[pltpu.VMEM((2 * FACE, LANES), F32)]
        + [pltpu.VMEM((ROWS, LANES), F32)] * 3
        + [pltpu.VMEM((32, 4, 2 * LANES), F32), pltpu.SemaphoreType.DMA((2,))],
    )
    out = call(
        last_kernel,
        shape(*acoustic.shape),
        main,
        ends,
        back,
        low,
        high,
        far_in=(0,),
        far_out=(0,),
        alias={0: 0},
        scratch=[pltpu.VMEM((2, 32, 4, LANES), F32), pltpu.SemaphoreType.DMA((2 * PARTS,))],
    )
    return flow.reshape(3, 16, 8, LANES), out


def solution(mesh):
    whole = P(("gx", "gy", "gz"), None, None)
    rows = P(("gx", "gy", "gz"), None)
    flow = P(None, "gx", "gy", "gz")
    return jax.shard_map(
        on_device,
        mesh=mesh,
        in_specs=(flow, whole, P(), rows, rows, rows),
        out_specs=(flow, whole),
        check_vma=False,
    )
```

```python
import jax
import jax.numpy as jnp
import numpy as np
from jax import lax
from jax.experimental import pallas as pl
from jax.experimental.pallas import tpu as pltpu
from jax.sharding import PartitionSpec as P

F32 = jnp.float32
BF = jnp.bfloat16
ORDER = 7
K = ORDER + 1
LANES = 128
ROWS = K**3
FACE = K * K
FLOW_STEP = 0.1
VISCOSITY = 0.05
WAVE_STEP = 0.02
SOURCE_GAIN = 25.0
GAIN = WAVE_STEP * SOURCE_GAIN
LIFT = WAVE_STEP * 0.5 * ORDER * (ORDER + 1) / 2.0
XV = 96
YV = 240
PARTS = 1
START_GRANT = 56_440_000
ZV = 64


def legendre_table(points, order):
    columns = [points * 0.0 + 1.0, points]
    for degree in range(2, order + 1):
        columns.append(
            ((2 * degree - 1) * points * columns[degree - 1] - (degree - 1) * columns[degree - 2])
            / degree
        )
    return np.stack(columns, axis=1)


def lobatto_tables(order):
    point_count = order + 1
    points = -np.cos(np.pi * np.arange(point_count) / order)
    for _ in range(60):
        legendre = legendre_table(points, order)
        points = points - (points * legendre[:, order] - legendre[:, order - 1]) / (
            point_count * legendre[:, order]
        )
    legendre = legendre_table(points, order)
    highest = legendre[:, order]
    spacing = points[:, None] - points[None, :] + np.eye(point_count)
    derivative = highest[:, None] / (highest[None, :] * spacing)
    derivative = derivative * (1.0 - np.eye(point_count))
    derivative[0, 0] = -order * point_count / 4.0
    derivative[order, order] = order * point_count / 4.0
    return derivative


DERIV = lobatto_tables(ORDER) * (-WAVE_STEP)


def split2(value):
    high = value.astype(BF)
    return high, (value - high.astype(F32)).astype(BF)


def restored(ref, rows, first, count):
    high = ref[first : first + count, :].astype(F32)
    return high + ref[rows // 2 + first : rows // 2 + first + count, :].astype(F32)


def nn(a, b):
    return lax.dot_general(a, b, (((1,), (0,)), ((), ())), preferred_element_type=F32)


def nt(a, b):
    return lax.dot_general(a, b, (((1,), (1,)), ((), ())), preferred_element_type=F32)


def tn(a, b):
    return lax.dot_general(a, b, (((0,), (0,)), ((), ())), preferred_element_type=F32)


def iota(shape, axis):
    return lax.broadcasted_iota(jnp.int32, shape, axis)


def roll(value, shift, axis):
    size = value.shape[axis]
    return pltpu.roll(value, shift % size, axis)


def call(
    kernel, out_shape, *args, scratch=(), far_in=(), far_out=(), alias={}, grant=16 * 2**20
):
    near, far = pl.BlockSpec(memory_space=pltpu.VMEM), pl.BlockSpec(memory_space=pl.ANY)
    outs = [far if i in far_out else near for i in range(len(jax.tree.leaves(out_shape)))]
    return pl.pallas_call(
        kernel,
        out_shape=out_shape,
        in_specs=[far if i in far_in else near for i in range(len(args))],
        out_specs=tuple(outs) if isinstance(out_shape, tuple) else outs[0],
        scratch_shapes=list(scratch),
        input_output_aliases=alias,
        compiler_params=pltpu.CompilerParams(vmem_limit_bytes=grant),
        cost_estimate=pl.CostEstimate(flops=10**6, bytes_accessed=10**6, transcendentals=0),
    )(*args)


def shape(*dims, dtype=F32):
    return jax.ShapeDtypeStruct(dims, dtype)


def stored_rows(acoustic_ref):
    return jnp.concatenate([acoustic_ref[:, v, :] for v in range(4)], axis=0)


def cell_matrix(cell_ref):
    cell = jnp.concatenate([cell_ref[...]] * 4, axis=1)
    cell = jnp.broadcast_to(cell, (LANES, LANES))
    row, column = iota((LANES, LANES), 0), iota((LANES, LANES), 1)
    return (cell == row % 32) & (row // 32 == column // 32)


def swapped(value, axis):
    kind = iota(value.shape, value.ndim - 1) // 32
    shift = 32 * (1 + axis)
    last = value.ndim - 1
    return jnp.where(
        kind == 0,
        roll(value, -shift, last),
        jnp.where(kind == 1 + axis, roll(value, shift, last), 0.0),
    )


def low_lift(axis, jump):
    return -LIFT * (swapped(jump, axis) + jump)


def high_lift(axis, jump):
    return LIFT * (swapped(jump, axis) - jump)


def cut_of(axis, dims):
    lane = iota(dims, 1)
    if axis == 1:
        part = (lane // 16) % 2
        return part == 0, part == 1
    part = lane % 16
    return part == 0, part == 15


def outer(axis, own_low, own_high, near):
    at_low, at_high = cut_of(axis, own_low.shape)
    low = jnp.where(at_high, near, own_high)
    high = jnp.where(at_low, near, own_low)
    wrap = 16 if axis == 1 else 15
    step = 16 if axis == 1 else 1
    return (
        jnp.where(at_low, roll(low, -wrap, 1), roll(low, step, 1)),
        jnp.where(at_high, roll(high, wrap, 1), roll(high, -step, 1)),
    )


def facing(axis, own_low, own_high):
    at_low, at_high = cut_of(axis, own_low.shape)
    wrap = 16 if axis == 1 else 15
    return jnp.where(at_high, roll(own_low, wrap, 1), roll(own_high, -wrap, 1))


def near_lift(axis, near, own_low, own_high):
    _, at_high = cut_of(axis, near.shape)
    jump = near - facing(axis, own_low, own_high)
    return jnp.where(at_high, high_lift(axis, jump), low_lift(axis, jump))


def inside_lifts(axis, own_low, own_high):
    at_low, at_high = cut_of(axis, own_low.shape)
    low, high = outer(axis, own_low, own_high, own_low)
    low = jnp.where(at_low, 0.0, own_low - low)
    high = jnp.where(at_high, 0.0, own_high - high)
    return low_lift(axis, low), high_lift(axis, high)


def boundary_lifts(axis, own_low, own_high, near):
    at_low, at_high = cut_of(axis, own_low.shape)
    low, high = outer(axis, own_low, own_high, near)
    low = jnp.where(at_low, own_low - low, 0.0)
    high = jnp.where(at_high, own_high - high, 0.0)
    return low_lift(axis, low), high_lift(axis, high)


def face_pair(ref, axis):
    if axis == 0:
        return ref[0:FACE, :], ref[ROWS - FACE : ROWS, :]
    if axis == 1:
        low = [ref[a * FACE : a * FACE + K, :] for a in range(K)]
        high = [ref[a * FACE + FACE - K : a * FACE + FACE, :] for a in range(K)]
        return jnp.concatenate(low, axis=0), jnp.concatenate(high, axis=0)
    return ref[pl.ds(0, FACE, stride=K), :], ref[pl.ds(K - 1, FACE, stride=K), :]


def add_pair(ref, axis, low, high):
    if axis == 0:
        ref[0:FACE, :] += low
        ref[ROWS - FACE : ROWS, :] += high
    elif axis == 1:
        for a in range(K):
            ref[a * FACE : a * FACE + K, :] += low[a * K : a * K + K]
            ref[a * FACE + FACE - K : a * FACE + FACE, :] += high[a * K : a * K + K]
    else:
        ref[pl.ds(0, FACE, stride=K), :] += low
        ref[pl.ds(K - 1, FACE, stride=K), :] += high


def derivative_columns():
    row = iota((K, LANES), 0)
    columns = []
    for m in range(K):
        column = jnp.zeros((K, LANES), F32)
        for b in range(K):
            column = jnp.where(row == b, float(DERIV[b, m]), column)
        columns.append(column)
    return columns


def volume_part(state_ref, out_ref, extra_ref=None):
    columns = derivative_columns()
    for a in range(K):
        rows = [state_ref[a * FACE + b * K : a * FACE + b * K + K, :] for b in range(K)]
        along_y = [swapped(r, 1) for r in rows]
        along_z = [swapped(r, 2) for r in rows]
        for b in range(K):
            total = rows[b]
            at = a * FACE + b * K
            if extra_ref is not None:
                total = total - extra_ref[at : at + K, :]
            for m in range(K):
                total = total + float(DERIV[b, m]) * along_y[m]
            for m in range(K):
                total = total + columns[m] * jnp.broadcast_to(
                    along_z[b][m : m + 1, :], (K, LANES)
                )
            out_ref[at : at + K, :] = total
    for b in range(K):
        rows = [
            swapped(state_ref[a * FACE + b * K : a * FACE + b * K + K, :], 0) for a in range(K)
        ]
        for a in range(K):
            at = a * FACE + b * K
            total = out_ref[at : at + K, :]
            for m in range(K):
                total = total + float(DERIV[a, m]) * rows[m]
            out_ref[at : at + K, :] = total


def load_kernel(velocity_ref, acoustic_ref, lines_ref, faces_ref, flow, wave, sems):
    copies = []
    for side, tile in ((0, 0), (1, 3)):
        copies.append((acoustic_ref.at[:, :, tile * LANES : tile * LANES + LANES], wave.at[side]))
    for side, first in ((0, 0), (1, 112)):
        copies.append((velocity_ref.at[:, first : first + 16, :], flow.at[side]))
    copies = [pltpu.make_async_copy(a, b, sems.at[i]) for i, (a, b) in enumerate(copies)]
    for copy in copies:
        copy.start()
    for copy in copies:
        copy.wait()
    left = iota((32, LANES), 1) < FACE
    for v in range(4):
        rows = jnp.where(left, wave[0, :, v, :], wave[1, :, v, :])
        faces_ref[v * 32 : v * 32 + 32, :] = rows.astype(BF)
    for side in range(2):
        for c in range(3):
            high, low = split2(flow[side, c])
            lines_ref[side, c * 16 : c * 16 + 16, :] = high
            lines_ref[side, XV // 2 + c * 16 : XV // 2 + c * 16 + 16, :] = low


def start_kernel(lines_ref, faces_ref, cell_ref, low_ref, high_ref, place_ref):
    place = jnp.where(cell_matrix(cell_ref), 1.0, 0.0).astype(BF)
    turned = jnp.transpose(nn(place, faces_ref[...])).astype(BF)
    low_ref[XV:, :] = turned[:FACE]
    high_ref[XV:, :] = turned[FACE:]
    low_ref[0:XV, :] = lines_ref[0]
    high_ref[0:XV, :] = lines_ref[1]
    place_ref[...] = place


def prepare_kernel(
    acoustic_ref,
    place_ref,
    cell_ref,
    slot_ref,
    state_ref,
    base_ref,
    targets_ref,
):
    slots = jnp.broadcast_to(jnp.concatenate([slot_ref[...]] * 2, axis=1), (32, LANES))
    named = jnp.where(slots == iota((32, LANES), 0), 1.0, 0.0).astype(BF)
    cells = jnp.broadcast_to(cell_ref[...], (16, 32)).astype(F32).astype(BF)
    targets_ref[...] = nn(cells, named)[0:1]
    place = place_ref[...]
    high, low = split2(stored_rows(acoustic_ref))
    state_ref[...] = jnp.transpose(nn(place, high) + nn(place, low))
    volume_part(state_ref, base_ref)
    for axis in (1, 2):
        add_pair(base_ref, axis, *inside_lifts(axis, *face_pair(state_ref, axis)))


def chunk_matrix(out_ref, held, low_rows, high_rows):
    rows = out_ref.shape[0]
    held[0:rows, :] = jnp.zeros((rows, 9 * LANES), F32)
    lane = iota((1, LANES), 1)
    for places, at in ((low_rows, 0), (high_rows, LANES - 1)):
        spot = jnp.where(lane == at, 1.0, 0.0)
        for m in range(9):
            for row in places(m):
                held[row : row + 1, m * LANES : m * LANES + LANES] = spot
    out_ref[...] = held[0:rows, :].astype(BF)


def table_kernel(
    order_ref,
    chosen_ref,
    projection_ref,
    owner_ref,
    back_ref,
    table_ref,
    faces_ref,
    place_ref,
    first_ref,
    second_ref,
    scratch,
    held,
):
    del order_ref
    back_ref[...] = jnp.transpose(chosen_ref[...].astype(F32)).astype(BF)
    place_ref[...] = placement(owner_ref)
    half = ZV // 2
    chunk_matrix(
        first_ref,
        held,
        lambda m: (2 * m + 1, half + 2 * m + 1),
        lambda m: (ZV + 2 * m, ZV + half + 2 * m),
    )
    chunk_matrix(
        second_ref,
        held,
        lambda m: (8 * m + 1, 80 + 8 * m + 1),
        lambda m: (8 * m + 6, 80 + 8 * m + 6),
    )
    high, low = split2(projection_ref[...])
    row, column = iota((64, 64), 0), iota((64, 64), 1)
    order = jnp.where(column == (row % 16) * 4 + row // 16, 1.0, 0.0).astype(BF)
    high, low = nn(order, high), nn(order, low)
    whole = jnp.concatenate([high, low, high, jnp.zeros((64, ROWS), F32)], axis=0)
    scratch[0] = jnp.transpose(whole[0:LANES])
    scratch[1] = jnp.transpose(whole[LANES:])
    for i in range(2):
        lane = slice(i * LANES, i * LANES + LANES)
        table_ref[:, lane] = scratch[i].astype(BF)
        for axis in range(3):
            for side, face in enumerate(face_pair(scratch.at[i], axis)):
                faces_ref[2 * axis + side, :, lane] = face.astype(BF)


def y_kernel(
    velocity_ref,
    xlow_ref,
    xhigh_ref,
    state_ref,
    base_ref,
    targets_ref,
    low_ref,
    high_ref,
    out_ref,
    wide,
):
    for c in range(3):
        wide[c, 0:16, :] = restored(xlow_ref, XV, c * 16, 16)
        wide[c, 16:144, :] = velocity_ref[c]
        wide[c, 144:160, :] = restored(xhigh_ref, XV, c * 16, 16)
    own_low, own_high = face_pair(state_ref, 0)
    out_ref[...] = base_ref[...]
    add_pair(
        out_ref,
        0,
        low_lift(0, own_low - xlow_ref[XV:, :].astype(F32)),
        high_lift(0, own_high - xhigh_ref[XV:, :].astype(F32)),
    )
    faces = packed(1, face_pair(state_ref, 1), face_pair(out_ref, 1))
    spare = jnp.concatenate([targets_ref[...], jnp.zeros((5, LANES), F32)], axis=0)
    for side, (out, near, far) in enumerate(((low_ref, 0, 1), (high_ref, 7, 6))):
        pieces = []
        for c in range(3):
            pieces.append(wide[c, pl.ds(8 + near, 18, stride=8), :])
            pieces.append(spare)
            pieces.append(wide[c, pl.ds(16 + far, 16, stride=8), :])
        high, low = split2(jnp.concatenate(pieces, axis=0))
        out[0 : YV // 2, :] = high
        out[YV // 2 : YV, :] = low
        out[YV:, :] = faces[side]


def packed(axis, traces, bases):
    at_low, at_high = cut_of(axis, traces[0].shape)
    step = 16 if axis == 1 else 1
    return (
        jnp.where(at_low, traces[0], roll(bases[0], step, 1)).astype(BF),
        jnp.where(at_high, traces[1], roll(bases[1], -step, 1)).astype(BF),
    )


def joined(axis, low, high):
    _, at_high = cut_of(axis, low.shape)
    low, high = low.astype(F32), high.astype(F32)
    step = 16 if axis == 1 else 1
    return (
        jnp.where(at_high, low, high),
        jnp.where(at_high, roll(low, step, 1), roll(high, -step, 1)),
    )


def z_kernel(
    order_ref,
    velocity_ref,
    xlow_ref,
    xhigh_ref,
    ylow_ref,
    yhigh_ref,
    state_ref,
    base_ref,
    targets_ref,
    wide_ref,
    own_ref,
    low_ref,
    high_ref,
    out_ref,
    near_ref,
    held,
):
    del order_ref
    held[0] = restored(ylow_ref, YV, 0, YV // 2)
    held[1] = restored(yhigh_ref, YV, 0, YV // 2)
    for c in range(3):
        low = restored(xlow_ref, XV, c * 16, 16)
        high = restored(xhigh_ref, XV, c * 16, 16)
        for x in range(2):
            wide_ref[c, x, 2:10, :] = low[x * 8 : x * 8 + 8]
            wide_ref[c, 18 + x, 2:10, :] = high[x * 8 : x * 8 + 8]
        for x in range(16):
            wide_ref[c, 2 + x, 2:10, :] = velocity_ref[c, x * 8 : x * 8 + 8, :]
        for x in (0, 1, 18, 19):
            wide_ref[c, x, 0:2, :] = jnp.zeros((2, LANES), F32)
            wide_ref[c, x, 10:12, :] = jnp.zeros((2, LANES), F32)
        for side in range(2):
            at = c * 40
            row = 1 + 9 * side
            wide_ref[c, 1:17, row, :] = held[side, at : at + 16, :]
            for x in (17, 18):
                wide_ref[c, x, row : row + 1, :] = held[side, at + x - 1 : at + x, :]
            wide_ref[c, 2:18, 11 * side, :] = held[side, at + 24 : at + 40, :]
        wide_ref[c, :, 12:16, :] = jnp.zeros((20, 4, LANES), F32)
    row, column = iota((16, LANES), 0), iota((16, LANES), 1)
    picks = ((row < 2) & (column == row)) | ((row >= 2) & (row < 4) & (column == row + 124))
    picks = jnp.where(picks, 1.0, 0.0).astype(BF)
    for c in range(3):
        high, low = split2(wide_ref[c].reshape(320, LANES))
        own = nt(picks, high) + nt(picks, low)
        own_ref[c, :, 0:320] = own[0:8]
        own_ref[c, :, 320:384] = jnp.zeros((8, 64), F32)
    trace, base = joined(1, ylow_ref[YV:, :], yhigh_ref[YV:, :])
    near_ref[0:FACE, :] = trace
    near_ref[FACE:, :] = base
    out_ref[...] = base_ref[...]
    add_pair(out_ref, 1, *boundary_lifts(1, *face_pair(state_ref, 1), near_ref[0:FACE, :]))
    faces = packed(2, face_pair(state_ref, 2), face_pair(out_ref, 2))
    for side, (out, first) in enumerate(((low_ref, 0), (high_ref, 2))):
        pieces = []
        for c in range(3):
            for j in range(3):
                pieces.append(own_ref[c, first : first + 2, j * 128 : j * 128 + 128])
        pieces += [targets_ref[...], jnp.zeros((5, LANES), F32)]
        pieces.append(near_ref[pl.ds(side * (K - 1), K, stride=K), :])
        high, low = split2(jnp.concatenate(pieces, axis=0))
        out[0 : ZV // 2, :] = high
        out[ZV // 2 : ZV, :] = low
        out[ZV:, :] = faces[side]


def differences(low, high):
    return [[high[a][c] - low[a][c] for c in range(3)] for a in range(3)]


def moved_on(centre, low, high, diff):
    scaled = [(-0.5 * FLOW_STEP) * centre[a] for a in range(3)]
    out = []
    for c in range(3):
        spread = (low[0][c] + high[0][c]) + (low[1][c] + high[1][c]) + (low[2][c] + high[2][c])
        carried = scaled[0] * diff[0][c] + scaled[1] * diff[1][c] + scaled[2] * diff[2][c]
        out.append(
            (1.0 - 6.0 * FLOW_STEP * VISCOSITY) * centre[c]
            + (FLOW_STEP * VISCOSITY) * spread
            + carried
        )
    return out


def lamb(centre, diff):
    w = [diff[1][2] - diff[2][1], diff[2][0] - diff[0][2], diff[0][1] - diff[1][0]]
    return [
        w[1] * centre[2] - w[2] * centre[1],
        w[2] * centre[0] - w[0] * centre[2],
        w[0] * centre[1] - w[1] * centre[0],
    ]


INNER = slice(2, 10)


def along_z(values, low_edge, high_edge):
    axis = values[0].ndim - 1
    lane = iota(values[0].shape, axis)
    low = [jnp.where(lane == 0, h, roll(v, 1, axis)) for v, h in zip(values, low_edge)]
    high = [jnp.where(lane == 127, h, roll(v, -1, axis)) for v, h in zip(values, high_edge)]
    return low, high


def plane(source, x, edges):
    centre = [source[c, x, INNER, :] for c in range(3)]
    zlow, zhigh = along_z(centre, edges, edges)
    low = [
        [source[c, x - 1, INNER, :] for c in range(3)],
        [source[c, x, 1:9, :] for c in range(3)],
        zlow,
    ]
    high = [
        [source[c, x + 1, INNER, :] for c in range(3)],
        [source[c, x, 3:11, :] for c in range(3)],
        zhigh,
    ]
    return centre, low, high


def add_lamb(sums, parts, x, first):
    i, a = (x // 2) // 4, (x // 2) % 4
    for c in range(3):
        at = first + (c * 4 + a) * 8
        sums[i, at : at + 8, :] = parts[c]


def inner_flow_kernel(wide_ref, middle_ref, sums_ref):
    for y in (1, 10):

        def row(first, at):
            return [wide_ref[c, first : first + 16, at, :] for c in range(3)]

        centre = row(2, y)
        nothing = [0.0] * 3
        zlow, zhigh = along_z(centre, nothing, nothing)
        low = [row(1, y), row(2, y - 1), zlow]
        high = [row(3, y), row(2, y + 1), zhigh]
        new = moved_on(centre, low, high, differences(low, high))
        for c in range(3):
            middle_ref[c, 2:18, y, :] = new[c]
    held = None
    for x in range(1, 19):
        centre, low, high = plane(wide_ref, x, [0.0] * 3)
        diff = differences(low, high)
        new = moved_on(centre, low, high, diff)
        for c in range(3):
            middle_ref[c, x, INNER, :] = new[c]
        if 2 <= x < 18:
            parts = lamb(centre, diff)
            if x % 2 == 0:
                held = parts
            else:
                add_lamb(sums_ref, [p + h for p, h in zip(parts, held)], x - 2, 0)


def flow_kernel(
    wide_ref,
    own_ref,
    zlow_ref,
    zhigh_ref,
    place_ref,
    inner_ref,
    inner_sums_ref,
    state_ref,
    base_ref,
    first_ref,
    second_ref,
    out_ref,
    volume_ref,
    base_out_ref,
    ends,
    halo,
    middle,
    sums,
):
    low = restored(zlow_ref, ZV, 0, ZV // 2)
    high = restored(zhigh_ref, ZV, 0, ZV // 2)
    for c in range(3):
        for j in range(3):
            lane = slice(j * 128, j * 128 + 128)
            at = 2 * (3 * c + j)
            ends[c, 0:2, lane] = low[at : at + 2]
            ends[c, 2:6, lane] = own_ref[c, 0:4, lane]
            ends[c, 6:8, lane] = high[at : at + 2]

    def spread_out(rows, spots, level):
        values = tn(rows, spots)
        for c in range(3):
            for j in range(3):
                at = (3 * c + j) * LANES
                part = values[:, at : at + LANES].reshape(8, 16, LANES)
                halo[level, c, j * 8 : j * 8 + 8] = part

    both = jnp.concatenate([zlow_ref[0:ZV, :], zhigh_ref[0:ZV, :]], axis=0)
    spread_out(both, first_ref[...], 0)
    edge = [ends[c] for c in range(3)]
    edge_low = [
        [roll(e, 16, 1) for e in edge],
        [roll(e, 1, 1) for e in edge],
        [roll(e, 1, 0) for e in edge],
    ]
    edge_high = [
        [roll(e, -16, 1) for e in edge],
        [roll(e, -1, 1) for e in edge],
        [roll(e, -1, 0) for e in edge],
    ]
    new = moved_on(edge, edge_low, edge_high, differences(edge_low, edge_high))
    rows = [new[c][:, j * LANES : j * LANES + LANES] for c in range(3) for j in range(3)]
    rows = jnp.concatenate(rows + [jnp.zeros((8, LANES), F32)], axis=0)
    spread_out(jnp.concatenate(split2(rows), axis=0), second_ref[...], 1)
    trace, _ = joined(2, zlow_ref[ZV:, :], zhigh_ref[ZV:, :])
    base_out_ref[...] = base_ref[...]
    add_pair(base_out_ref, 2, *boundary_lifts(2, *face_pair(state_ref, 2), trace))

    def sign(dims):
        return jnp.where(iota(dims, len(dims) - 1) == 0, -1.0, 1.0)

    def growth(speed, signs):
        return FLOW_STEP * VISCOSITY - (0.5 * FLOW_STEP) * (signs * speed)

    for y in (1, 10):
        rate = growth(wide_ref[2, 2:18, y, :], sign((16, LANES)))
        for c in range(3):
            middle[c, 2:18, y, :] = inner_ref[c, 2:18, y, :] + rate * halo[0, c, 2:18, y, :]
    held = None
    signs = sign((8, LANES))
    for x in range(1, 19):
        centre = [wide_ref[c, x, INNER, :] for c in range(3)]
        edges = [halo[0, c, x, INNER, :] for c in range(3)]
        rate = growth(centre[2], signs)
        for c in range(3):
            middle[c, x, INNER, :] = inner_ref[c, x, INNER, :] + rate * edges[c]
        if 2 <= x < 18:
            first, second = signs * edges[0], signs * edges[1]
            parts = [
                first * centre[2],
                second * centre[2],
                -(second * centre[1]) - first * centre[0],
            ]
            if x % 2 == 0:
                held = parts
            else:
                i, a = ((x - 2) // 2) // 4, ((x - 2) // 2) % 4
                for c in range(3):
                    at = (c * 4 + a) * 8
                    sums[i, at : at + 8, :] = inner_sums_ref[i, at : at + 8, :] + (
                        parts[c] + held[c]
                    )
    for x in range(2, 18):
        centre, low, high = plane(middle, x, [halo[1, c, x, INNER, :] for c in range(3)])
        diff = differences(low, high)
        new = moved_on(centre, low, high, diff)
        for c in range(3):
            out_ref[c, (x - 2) * 8 : (x - 2) * 8 + 8, :] = new[c]
        parts = lamb(centre, diff)
        if x % 2 == 0:
            held = parts
        else:
            add_lamb(sums, [p + h for p, h in zip(parts, held)], x - 2, 96)
    both = []
    for i in range(2):
        both.append(sums[i, pl.ds(0, 96, stride=2), :] + sums[i, pl.ds(1, 96, stride=2), :])
    pairs = jnp.concatenate(both, axis=1)
    pairs = jnp.concatenate([pairs, jnp.zeros((32, 256), F32)], axis=0)
    high, low = split2(pairs)
    place = place_ref[...]
    volumes = (nt(place, high) + nt(place, low)) * (1.0 / 16.0)
    lane = iota((256, LANES), 1)
    twice = jnp.where(lane < 48, volumes, roll(volumes, 48, 1)).reshape(4, 8, 8, LANES)
    left = iota((8, 8, LANES), 2) < 48
    for y in range(4):
        part = slice(y * 8, y * 8 + 8)
        volume_ref[part, 0:8, :] = volumes[y * 64 : y * 64 + 64].reshape(8, 8, LANES).astype(BF)
        rows = jnp.where(left, twice[(y + 3) % 4], twice[(y + 1) % 4])
        volume_ref[part, 8:16, :] = rows.astype(BF)
        lower = jnp.concatenate([twice[y, 7:8], twice[y, 0:7]], axis=0)
        upper = jnp.concatenate([twice[y, 1:8], twice[y, 0:1]], axis=0)
        volume_ref[part, 16:24, :] = jnp.where(left, lower, upper).astype(BF)


def gather_matrix(targets, second=None, chosen=None):
    row, column = iota((256, LANES), 0), iota((256, LANES), 1)
    slots = jnp.where(column == (row // 8) * 2 + row % 2, 1.0, 0.0).astype(BF)

    def named(line):
        return nt(slots, jnp.broadcast_to(line, (LANES, LANES)).astype(BF))

    cells = named(targets)
    if second is not None:
        cells = jnp.where(chosen, cells, named(second))
    fits = cells == (column % 32).astype(F32)
    return [
        jnp.where(fits & ((row % 8) // 2 == z), 1.0, 0.0).astype(BF) for z in range(4)
    ]


def line(ref, at):
    return ref[0:32, :].astype(F32)[at : at + 1]


def placement(owner_ref):
    owner = jnp.concatenate([owner_ref[...]] * 4, axis=1).astype(F32)
    across = jnp.broadcast_to(owner, (LANES, LANES))
    row, column = iota((32, LANES), 0), iota((32, LANES), 1)
    down = nt(jnp.where(row == column, 1.0, 0.0).astype(BF), across.astype(BF))
    earlier = jnp.where((across[0:32] == down) & (column < row), 1.0, 0.0)
    slots = 2.0 * down + jnp.sum(earlier, axis=1, keepdims=True)
    spread = jnp.where(iota((32, 256), 1) // 8 == iota((32, 256), 0), 1.0, 0.0).astype(BF)
    slots = tn(slots.astype(BF), spread)
    slots = jnp.concatenate([slots, slots], axis=0)
    row, column = iota((256, 256), 0), iota((256, 256), 1)
    wanted = ((row // 8) * 2 + row % 2).astype(F32)
    fits = (slots == wanted) & ((column % 8) // 2 == (row % 8) // 2)
    return jnp.where(fits, 1.0, 0.0).astype(BF)


def near_kernel(state_ref, near_ref, targets_ref, ylow_ref, yhigh_ref, sides_ref, gather_ref):
    sides_ref[...] = near_ref[FACE:, :] + near_lift(1, near_ref[0:FACE, :], *face_pair(state_ref, 1))
    groups = [
        gather_matrix(targets_ref[...]),
        gather_matrix(line(ylow_ref, 18), line(yhigh_ref, 18), cut_of(1, (256, LANES))[1]),
    ]
    for g, parts in enumerate(groups):
        for z in range(4):
            gather_ref[g, :, z * LANES : z * LANES + LANES] = parts[z]


def end_faces(state_ref, near_ref, side_ref, zlow_ref, zhigh_ref, sides_ref):
    trace, base = joined(2, zlow_ref[ZV:, :], zhigh_ref[ZV:, :])
    sides_ref[0:FACE, :] = side_ref[...]
    sides_ref[FACE:, :] = base + near_lift(2, trace, *face_pair(state_ref, 2))
    from_low = zlow_ref[0:32, :].astype(F32)[24:32]
    from_high = zhigh_ref[0:32, :].astype(F32)[24:32]
    at_low, at_high = cut_of(2, (K, LANES))
    jump = near_ref[pl.ds(0, K, stride=K), :] - roll(from_low, -15, 1)
    sides_ref[pl.ds(0, K, stride=K), :] += jnp.where(at_low, low_lift(2, jump), 0.0)
    jump = near_ref[pl.ds(K - 1, K, stride=K), :] - roll(from_high, 15, 1)
    sides_ref[pl.ds(K - 1, K, stride=K), :] += jnp.where(at_high, high_lift(2, jump), 0.0)
    parts = gather_matrix(line(zlow_ref, 18), line(zhigh_ref, 18), cut_of(2, (256, LANES))[1])
    return jnp.concatenate(parts, axis=1)


def stacked(summed, starts):
    kind = iota((16, LANES), 1) // 32
    blocks = []
    for start in starts:
        rows = []
        for z in range(4):
            total = jnp.zeros((16, LANES), F32)
            for c in range(3):
                total = jnp.where(kind == 1 + c, start(summed, c, z), total)
            rows.append(total)
        blocks.append(jnp.concatenate(rows, axis=0))
    high, low = split2(jnp.concatenate(blocks, axis=1) if len(blocks) > 1 else blocks[0])
    return jnp.concatenate([high, high, low, jnp.zeros_like(low)], axis=0)


def at_rows(first):
    def pick(summed, c, z):
        at = first + c * 16
        return summed[at : at + 16, z * LANES : z * LANES + LANES]

    return pick


def by_side(axis):
    def pick(summed, c, z):
        _, at_high = cut_of(axis, (16, LANES))
        return jnp.where(at_high, at_rows(0)(summed, c, z), at_rows(48)(summed, c, z))

    return pick


def send_kernel(arrived_ref, gather_ref, faces_ref, base_ref, low_ref, high_ref, cells_ref):
    rows = arrived_ref[:, 0:8, :].reshape(256, LANES)
    summed = tn(rows, gather_ref[0])
    cells = stacked(summed, (at_rows(0), at_rows(48)))
    cells_ref[...] = cells
    for side, (out, face) in enumerate(zip((low_ref, high_ref), face_pair(base_ref, 0))):
        out[...] = (face - GAIN * nn(faces_ref[side], cells[:, 0:LANES])).astype(BF)


def second_kernel(
    arrived_ref,
    gather_ref,
    table_ref,
    faces_ref,
    cells_ref,
    base_ref,
    first_ref,
    near_ref,
    side_ref,
    zlow_ref,
    zhigh_ref,
    back_ref,
    flow_ref,
    out_ref,
    ends_ref,
    flow_out_ref,
    sides_ref,
    state,
    extra,
    total,
    rows_held,
    sems,
):
    flow_copy = pltpu.make_async_copy(flow_ref, flow_out_ref, sems.at[0])
    flow_copy.start()
    end_gather = end_faces(first_ref, near_ref, side_ref, zlow_ref, zhigh_ref, sides_ref)
    source = GAIN * nn(table_ref[...], cells_ref[...])
    state[...] = base_ref[...] - source[:, 0:LANES]
    extra[...] = source[:, LANES:]
    near = []
    for axis in (1, 2):
        rows = arrived_ref[:, 8 * axis : 8 * axis + 8, :].reshape(256, LANES)
        gather = gather_ref[1] if axis == 1 else end_gather
        cells = stacked(tn(rows, gather), (by_side(axis),))
        at_low, at_high = cut_of(axis, (FACE, LANES))
        face = jnp.where(
            at_high,
            nn(faces_ref[2 * axis + 1], cells),
            nn(faces_ref[2 * axis], cells),
        )
        near.append(sides_ref[(axis - 1) * FACE : axis * FACE, :] - GAIN * face)
    volume_part(state, total, extra)
    for axis in (1, 2):
        own_low, own_high = face_pair(state, axis)
        low, high = outer(axis, own_low, own_high, near[axis - 1])
        add_pair(total, axis, low_lift(axis, own_low - low), high_lift(axis, own_high - high))
    own_low, own_high = face_pair(state, 0)
    add_pair(total, 0, low_lift(0, own_low), high_lift(0, own_high))
    back = back_ref[...]

    def turned(first, last):
        high, low = split2(jnp.transpose(total[first:last, :]))
        return nn(back, high) + nn(back, low)

    rows = turned(LANES, 3 * LANES)
    for v in range(4):
        rows_held[:, v, :] = rows[v * 32 : v * 32 + 32, :]
    copy = pltpu.make_async_copy(rows_held, out_ref.at[:, :, LANES : 3 * LANES], sems.at[1])
    copy.start()
    ends_ref[0] = turned(0, LANES)
    ends_ref[1] = turned(3 * LANES, ROWS)
    flow_copy.wait()
    copy.wait()


def last_kernel(
    main_ref, ends_ref, back_ref, low_ref, high_ref, out_ref, held, sems
):
    rows = nt(back_ref[...], jnp.concatenate([low_ref[...], high_ref[...]], axis=0))
    across = jnp.concatenate([rows[32:64], rows[0:32], jnp.zeros((64, LANES), F32)], axis=0)
    rows = LIFT * (rows + jnp.where(iota((LANES, LANES), 1) < FACE, across, -across))
    left = iota((LANES, LANES), 1) < FACE
    copies = []
    for side, tile in ((0, 0), (1, 3)):
        total = ends_ref[side] + jnp.where(left if side == 0 else ~left, rows, 0.0)
        for v in range(4):
            held[side, :, v, :] = total[v * 32 : v * 32 + 32, :]
        for part in range(PARTS):
            some = slice(part * 32 // PARTS, (part + 1) * 32 // PARTS)
            copies.append(
                pltpu.make_async_copy(
                    held.at[side, some],
                    out_ref.at[some, :, tile * LANES : tile * LANES + LANES],
                    sems.at[side * PARTS + part],
                )
            )
            copies[-1].start()
    for copy in copies:
        copy.wait()


def both_ways(low, high, axis):
    count = lax.axis_size(axis)
    up = [(i, (i + 1) % count) for i in range(count)]
    down = [(b, a) for a, b in up]
    return lax.ppermute(high, axis, up), lax.ppermute(low, axis, down)


def on_device(velocity, acoustic, projection, owner_index, slot_element, element_cell):
    velocity = velocity.reshape(3, 128, LANES)
    face = shape(FACE, LANES, dtype=BF)
    state = shape(ROWS, LANES)
    send = shape(XV + FACE, LANES, dtype=BF)
    chosen = shape(LANES, LANES, dtype=BF)
    lines, faces = call(
        load_kernel,
        (shape(2, XV, LANES, dtype=BF), shape(LANES, LANES, dtype=BF)),
        velocity,
        acoustic,
        far_in=(0, 1),
        grant=START_GRANT,
        scratch=[
            pltpu.VMEM((2, 3, 16, LANES), F32),
            pltpu.VMEM((2, 32, 4, LANES), F32),
            pltpu.SemaphoreType.DMA((4,)),
        ],
    )
    chosen = shape(LANES, LANES, dtype=BF)
    xlow, xhigh, chosen = call(start_kernel, (send, send, chosen), lines, faces, element_cell)
    xlow, xhigh = both_ways(xlow, xhigh, "gx")
    first, base, targets = call(
        prepare_kernel,
        (state, state, shape(1, LANES)),
        acoustic,
        chosen,
        element_cell,
        slot_element,
    )
    send = shape(YV + FACE, LANES, dtype=BF)
    ylow, yhigh, base = call(
        y_kernel,
        (send, send, state),
        velocity,
        xlow,
        xhigh,
        first,
        base,
        targets,
        scratch=[pltpu.VMEM((3, 208, LANES), F32)],
    )
    ylow, yhigh = both_ways(ylow, yhigh, "gy")
    back, table, faces, place, spots, later_spots = call(
        table_kernel,
        (
            shape(LANES, LANES, dtype=BF),
            shape(ROWS, 256, dtype=BF),
            shape(6, FACE, 256, dtype=BF),
            shape(256, 256, dtype=BF),
            shape(2 * ZV, 9 * LANES, dtype=BF),
            shape(160, 9 * LANES, dtype=BF),
        ),
        base,
        chosen,
        projection,
        owner_index.reshape(1, 32),
        far_in=(0,),
        scratch=[pltpu.VMEM((2, ROWS, LANES), F32), pltpu.VMEM((160, 9 * LANES), F32)],
    )
    send = shape(ZV + FACE, LANES, dtype=BF)
    wide, own, zlow, zhigh, base, near = call(
        z_kernel,
        (shape(3, 20, 16, LANES), shape(3, 8, 384), send, send, state, shape(2 * FACE, LANES)),
        spots,
        velocity,
        xlow,
        xhigh,
        ylow,
        yhigh,
        first,
        base,
        targets,
        far_in=(0,),
        scratch=[pltpu.VMEM((2, YV // 2, LANES), F32)],
    )
    zlow, zhigh = both_ways(zlow, zhigh, "gz")
    middle, sums = call(
        inner_flow_kernel, (shape(3, 20, 16, LANES), shape(2, 96, LANES)), wide
    )
    side, gather = call(
        near_kernel,
        (shape(FACE, LANES), shape(2, 256, 512, dtype=BF)),
        first,
        near,
        targets,
        ylow,
        yhigh,
    )
    flow, volumes, base = call(
        flow_kernel,
        (shape(3, 128, LANES), shape(32, 24, LANES, dtype=BF), state),
        wide,
        own,
        zlow,
        zhigh,
        place,
        middle,
        sums,
        first,
        base,
        spots,
        later_spots,
        scratch=[
            pltpu.VMEM((3, 8, 384), F32),
            pltpu.VMEM((2, 3, 24, 16, LANES), F32),
            pltpu.VMEM((3, 20, 16, LANES), F32),
            pltpu.VMEM((2, 192, LANES), F32),
        ],
    )
    volumes, side, gather = lax.optimization_barrier((volumes, side, gather))
    arrived = lax.all_to_all(volumes, ("gy", "gz"), split_axis=0, concat_axis=0, tiled=True)
    low, high, cells = call(
        send_kernel, (face, face, shape(256, 256, dtype=BF)), arrived, gather, faces, base
    )
    low, high = both_ways(low, high, "gx")
    main, ends, flow = call(
        second_kernel,
        (shape(*acoustic.shape), shape(2, LANES, LANES), shape(3, 128, LANES)),
        arrived,
        gather,
        table,
        faces,
        cells,
        base,
        first,
        near,
        side,
        zlow,
        zhigh,
        back,
        flow,
        far_out=(0, 2),
        scratch=[pltpu.VMEM((2 * FACE, LANES), F32)]
        + [pltpu.VMEM((ROWS, LANES), F32)] * 3
        + [pltpu.VMEM((32, 4, 2 * LANES), F32), pltpu.SemaphoreType.DMA((2,))],
    )
    out = call(
        last_kernel,
        shape(*acoustic.shape),
        main,
        ends,
        back,
        low,
        high,
        far_in=(0,),
        far_out=(0,),
        alias={0: 0},
        scratch=[pltpu.VMEM((2, 32, 4, LANES), F32), pltpu.SemaphoreType.DMA((2 * PARTS,))],
    )
    return flow.reshape(3, 16, 8, LANES), out


def solution(mesh):
    whole = P(("gx", "gy", "gz"), None, None)
    rows = P(("gx", "gy", "gz"), None)
    flow = P(None, "gx", "gy", "gz")
    return jax.shard_map(
        on_device,
        mesh=mesh,
        in_specs=(flow, whole, P(), rows, rows, rows),
        out_specs=(flow, whole),
        check_vma=False,
    )
```
